32 devices in a mesh: dp: 8 (over z, y), tensor: 4 (over x, core).
Axes of the slice: x: 2, y: 2, z: 4, core: 2. Of those that a mesh axis runs over, the one named last changes fastest.
Arguments:
- inputs: bfloat16 [8192, 2048], P(('dp', 'tensor')), may hold values from -6 to 6
- cotangent: bfloat16 [8192, 2048], P(('dp', 'tensor')), may hold values from -6 to 6
- segment_ids: int32 [8, 1024], P('dp'), may hold values from 0 to 12, never falling along the last dimension, each value on 1 to 256 neighbouring positions
- parent_links: int32 [8, 13], P('dp'), may hold values from 0 to 11, as said below
- adapter_choice: int32 [8], P('dp'), may hold values from 0 to 7
- gain_one: float32 [2048], replicated, may hold values from 0.25 to 1.75
- shift_one: float32 [2048], replicated, may hold values from -1.75 to 1.75
- gain_two: float32 [2048], replicated, may hold values from 0.25 to 1.75
- shift_two: float32 [2048], replicated, may hold values from -1.75 to 1.75
- query_weight: bfloat16 [2048, 2048], P('dp', 'tensor'), may hold values from -0.125 to 0.125
- key_weight: bfloat16 [2048, 2048], P('dp', 'tensor'), may hold values from -0.125 to 0.125
- value_weight: bfloat16 [2048, 2048], P('dp', 'tensor'), may hold values from -0.125 to 0.125
- output_weight: bfloat16 [2048, 2048], P('tensor', 'dp'), may hold values from -0.5 to 0.5
- expand_weight: bfloat16 [2048, 8192], P('dp', 'tensor'), may hold values from -0.125 to 0.125
- shrink_weight: bfloat16 [8192, 2048], P('tensor', 'dp'), may hold values from -0.0625 to 0.0625
- query_bias: float32 [2048], P('tensor'), may hold values from -1.75 to 1.75
- value_bias: float32 [2048], P('tensor'), may hold values from -1.75 to 1.75
- output_bias: float32 [2048], replicated, may hold values from -1.75 to 1.75
- expand_bias: float32 [8192], P('tensor'), may hold values from -1.75 to 1.75
- shrink_bias: float32 [2048], replicated, may hold values from -1.75 to 1.75
- query_down: bfloat16 [8, 16, 2048], replicated, may hold values from -0.125 to 0.125
- query_up: bfloat16 [8, 16, 2048], P(None, None, 'tensor'), may hold values from -0.5 to 0.5
- key_down: bfloat16 [8, 16, 2048], replicated, may hold values from -0.125 to 0.125
- key_up: bfloat16 [8, 16, 2048], P(None, None, 'tensor'), may hold values from -0.5 to 0.5
- value_down: bfloat16 [8, 16, 2048], replicated, may hold values from -0.125 to 0.125
- value_up: bfloat16 [8, 16, 2048], P(None, None, 'tensor'), may hold values from -0.5 to 0.5
- output_down: bfloat16 [8, 16, 2048], P(None, None, 'tensor'), may hold values from -0.5 to 0.5
- output_up: bfloat16 [8, 16, 2048], replicated, may hold values from -0.5 to 0.5
- expand_down: bfloat16 [8, 16, 2048], replicated, may hold values from -0.125 to 0.125
- expand_up: bfloat16 [8, 16, 8192], P(None, None, 'tensor'), may hold values from -0.5 to 0.5
- shrink_down: bfloat16 [8, 16, 8192], P(None, None, 'tensor'), may hold values from -0.125 to 0.125
- shrink_up: bfloat16 [8, 16, 2048], replicated, may hold values from -0.5 to 0.5
Outputs:
- output: bfloat16 [8192, 2048], P(('dp', 'tensor'))
- input_delta: bfloat16 [8192, 2048], P(('dp', 'tensor'))
- query_down_delta: float32 [8, 16, 2048], replicated
- query_up_delta: float32 [8, 16, 2048], P(None, None, 'tensor')
- key_down_delta: float32 [8, 16, 2048], replicated
- key_up_delta: float32 [8, 16, 2048], P(None, None, 'tensor')
- value_down_delta: float32 [8, 16, 2048], replicated
- value_up_delta: float32 [8, 16, 2048], P(None, None, 'tensor')
- output_down_delta: float32 [8, 16, 2048], P(None, None, 'tensor')
- output_up_delta: float32 [8, 16, 2048], replicated
- expand_down_delta: float32 [8, 16, 2048], replicated
- expand_up_delta: float32 [8, 16, 8192], P(None, None, 'tensor')
- shrink_down_delta: float32 [8, 16, 8192], P(None, None, 'tensor')
- shrink_up_delta: float32 [8, 16, 2048], replicated
The draws below stay inside these ranges and needn't reach their ends.
Inputs may be any that keep to these rules, and one draw needn't show every extreme that they name: `segment_ids`: within a tree the ids never fall, all 13 segments occur, and each holds 1 to a quarter of 1024 tokens. `parent_links`: entry 0 is 0; entry s above 0 names an earlier segment, so that the segments of a tree form a tree rooted at segment 0; the last segment's parent is the segment before it.
All inputs are finite; a program needn't handle non-finite values.
Results may differ from the reference program's by a relative error of at most 0.015.
Values may be sent and summed in bfloat16 or wider, within the bound.
No kernel may reach another device: no remote copies, remote signals or barrier semaphores. Data moves between devices by JAX's collectives and lax.ppermute only.
A program may use at most 192 MiB of HBM per device.

```python
import math
import jax
import jax.numpy as jnp
import numpy as np
from jax import lax

D = 2048
HEAD_DIM = 128
FF = 8192
RANK = 16
ADAPTERS = 8
SEGS = 13
SEQ = 1024
TREES = 8
TOKENS = 8192


def draw_parent_links(key, part):
    seg_range = jnp.arange(SEGS, dtype=jnp.int32)
    upper_bound = jnp.maximum(seg_range, 1)
    picked = jax.random.randint(key, (TREES, SEGS), 0, upper_bound[None, :], dtype=jnp.int32)
    picked = jnp.where(seg_range[None, :] == SEGS - 1, SEGS - 2, picked)
    return jnp.where(seg_range[None, :] == 0, 0, picked).astype(jnp.int32)


def plant(entries, key, least, largest):
    extent = entries.shape
    place = [jax.random.randint(jax.random.fold_in(key, axis), (), 0, extent[axis]) for axis in range(len(extent))]
    entries = entries.at[tuple(place)].set(least)
    longest = extent.index(max(extent))
    place[longest] = (place[longest] + 1) % extent[longest]
    return entries.at[tuple(place)].set(largest)


def levels(stream_key, extent, shards, least, largest):
    gain, own = 1.0, jax.random.fold_in(stream_key, 6)
    for position, parts in shards:
        steps = jnp.exp(jax.random.uniform(jax.random.fold_in(own, position), (parts,), jnp.float32, least / len(shards), largest / len(shards)))
        gain = gain * jnp.repeat(steps, extent[position] // parts).reshape([-1 if axis == position else 1 for axis in range(len(extent))])
    return gain


def profile(count, total, bound, skew):
    loads = [(1 << 20) // math.isqrt(grade ** skew) + 1 for grade in range(2, count + 1)]
    surplus, holding = total - bound - (count - 1), [1] * (count - 1)
    while surplus > 0:
        candidates = [i for i in range(count - 1) if holding[i] < bound]
        whole, budget = sum([loads[i] for i in candidates]), surplus
        for i in candidates:
            more = min(bound - holding[i], max(1, budget * loads[i] // whole), surplus)
            holding[i] = holding[i] + more
            surplus = surplus - more
    return np.array([bound] + holding)


def uneven_parts(key, number_of, total, most, skew):
    if number_of == 2:
        one = jax.random.randint(key, (), max(1, total - most), min(most, total - 1) + 1)
        return jnp.stack([one, total - one])
    sizes = jnp.asarray(profile(number_of, total, most, skew), jnp.int32)
    couples = (number_of - 1) // 2
    giver, taker = sizes[1:1 + 2 * couples:2], sizes[2:2 + 2 * couples:2]
    slack = jnp.minimum(giver - 1, most - taker)
    passed = jax.random.randint(jax.random.fold_in(key, 1), (couples,), 0, 1 << 20) % (slack + 1)
    sizes = sizes.at[1:1 + 2 * couples:2].set(giver - passed).at[2:2 + 2 * couples:2].set(taker + passed)
    return sizes[jax.random.permutation(jax.random.fold_in(key, 2), number_of)]


def gaussian(own_key, dims, deviation, most, split=(), kind=jnp.bfloat16):
    level = levels(own_key, dims, split, -0.22, 0.18) if split else 1.0
    result = jax.random.normal(own_key, dims, jnp.float32) * deviation * level
    return jnp.minimum(jnp.maximum(result, -most), most).astype(kind)


def setup_inputs(seed: int = 0) -> dict:
    seeds = jax.random.split(jax.random.key(seed), 33)
    inputs = gaussian(seeds[0], (TOKENS, D), 1.0, 6.0, ((0, 32),))
    cotangent = gaussian(seeds[1], (TOKENS, D), 1.0, 6.0, ((0, 32),))
    segment_ids = jax.vmap(lambda own: jnp.searchsorted(jnp.cumsum(uneven_parts(own, SEGS, SEQ, SEQ // 4, 2)), jnp.arange(SEQ), side="right"))(jax.random.split(seeds[2], TREES)).reshape((TREES, SEQ)).astype(jnp.int32)
    parent_links = draw_parent_links(jax.random.fold_in(seeds[32], 71), 0)
    adapter_choice = plant(jax.random.randint(seeds[4], (TREES,), 0, ADAPTERS), jax.random.fold_in(seeds[4], 1), 0, ADAPTERS - 1).astype(jnp.int32)
    gain_one = jnp.clip(1.0 + 0.15 * jax.random.normal(seeds[5], (D,), jnp.float32), 0.25, 1.75)
    shift_one = gaussian(seeds[6], (D,), 0.3, 1.75, (), jnp.float32)
    gain_two = jnp.clip(1.0 + 0.15 * jax.random.normal(seeds[7], (D,), jnp.float32), 0.25, 1.75)
    shift_two = gaussian(seeds[8], (D,), 0.3, 1.75, (), jnp.float32)
    query_weight = gaussian(seeds[9], (D, D), D ** -0.5, 0.125, ((0, 8), (1, 4)))
    key_weight = gaussian(seeds[10], (D, D), D ** -0.5, 0.125, ((0, 8), (1, 4)))
    value_weight = gaussian(seeds[11], (D, D), D ** -0.5, 0.125, ((0, 8), (1, 4)))
    output_weight = gaussian(seeds[12], (D, D), (D // 16) ** -0.5, 0.5, ((0, 4), (1, 8)))
    expand_weight = gaussian(seeds[13], (D, FF), D ** -0.5, 0.125, ((0, 8), (1, 4)))
    shrink_weight = gaussian(seeds[14], (FF, D), FF ** -0.5, 0.0625, ((0, 4), (1, 8)))
    query_bias = gaussian(seeds[15], (D,), 0.3, 1.75, ((0, 4),), jnp.float32)
    value_bias = gaussian(seeds[16], (D,), 0.3, 1.75, ((0, 4),), jnp.float32)
    output_bias = gaussian(seeds[17], (D,), 0.3, 1.75, (), jnp.float32)
    expand_bias = gaussian(seeds[18], (FF,), 0.3, 1.75, ((0, 4),), jnp.float32)
    shrink_bias = gaussian(seeds[19], (D,), 0.3, 1.75, (), jnp.float32)
    query_down = gaussian(seeds[20], (ADAPTERS, RANK, D), D ** -0.5, 0.125)
    query_up = gaussian(seeds[21], (ADAPTERS, RANK, D), 0.08, 0.5, ((2, 4),))
    key_down = gaussian(seeds[22], (ADAPTERS, RANK, D), D ** -0.5, 0.125)
    key_up = gaussian(seeds[23], (ADAPTERS, RANK, D), 0.08, 0.5, ((2, 4),))
    value_down = gaussian(seeds[24], (ADAPTERS, RANK, D), D ** -0.5, 0.125)
    value_up = gaussian(seeds[25], (ADAPTERS, RANK, D), 0.08, 0.5, ((2, 4),))
    output_down = gaussian(seeds[26], (ADAPTERS, RANK, D), (D // 16) ** -0.5, 0.5, ((2, 4),))
    output_up = gaussian(seeds[27], (ADAPTERS, RANK, D), 0.08, 0.5)
    expand_down = gaussian(seeds[28], (ADAPTERS, RANK, D), D ** -0.5, 0.125)
    expand_up = gaussian(seeds[29], (ADAPTERS, RANK, FF), 0.08, 0.5, ((2, 4),))
    shrink_down = gaussian(seeds[30], (ADAPTERS, RANK, FF), (FF // 4) ** -0.5, 0.125, ((2, 4),))
    shrink_up = gaussian(seeds[31], (ADAPTERS, RANK, D), 0.08, 0.5)
    return {"inputs": inputs, "cotangent": cotangent, "segment_ids": segment_ids, "parent_links": parent_links, "adapter_choice": adapter_choice, "gain_one": gain_one, "shift_one": shift_one, "gain_two": gain_two, "shift_two": shift_two, "query_weight": query_weight, "key_weight": key_weight, "value_weight": value_weight, "output_weight": output_weight, "expand_weight": expand_weight, "shrink_weight": shrink_weight, "query_bias": query_bias, "value_bias": value_bias, "output_bias": output_bias, "expand_bias": expand_bias, "shrink_bias": shrink_bias, "query_down": query_down, "query_up": query_up, "key_down": key_down, "key_up": key_up, "value_down": value_down, "value_up": value_up, "output_down": output_down, "output_up": output_up, "expand_down": expand_down, "expand_up": expand_up, "shrink_down": shrink_down, "shrink_up": shrink_up}


HIGHEST = lax.Precision.HIGHEST

@jax.custom_vjp
def low(v):
    return lax.optimization_barrier(v.astype(jnp.bfloat16)).astype(jnp.float32)

@jax.custom_vjp
def low_back(v):
    return v

def low_keep(v):
    return (low(v), None)

def low_pass(kept, grad):
    return (grad,)

def back_keep(v):
    return (v, None)

def back_low(kept, grad):
    return (low(grad),)
low.defvjp(low_keep, low_pass)
low_back.defvjp(back_keep, back_low)

def exact_product(left, right):
    return jnp.dot(left, right, precision=HIGHEST, preferred_element_type=jnp.float32)

def layer_norm(values, gain_vec, shift_vec):
    row_mean = lax.optimization_barrier(jnp.mean(values, axis=-1, keepdims=True))
    centred = values - row_mean
    row_var = lax.optimization_barrier(jnp.mean(centred * centred, axis=-1, keepdims=True))
    return centred * lax.rsqrt(row_var + 1e-05) * gain_vec + shift_vec

def ancestry(parents):
    seg_range = jnp.arange(SEGS, dtype=jnp.int32)
    current = seg_range
    ancestors = current[:, None] == seg_range[None, :]
    for hop_index in range(SEGS - 1):
        current = lax.optimization_barrier(jnp.sum(jnp.where(current[:, None] == seg_range[None, :], parents[None, :], 0), axis=1)).astype(jnp.int32)
        ancestors = jnp.logical_or(ancestors, current[:, None] == seg_range[None, :])
    return ancestors

def tree_forward(inputs_tree, adapters, frozen, select, allowed):
    gain_one, shift_one, gain_two, shift_two, query_weight, key_weight, value_weight, output_weight, expand_weight, shrink_weight, query_bias, value_bias, output_bias, expand_bias, shrink_bias = frozen
    query_down, query_up, key_down, key_up, value_down, value_up, output_down, output_up, expand_down, expand_up, shrink_down, shrink_up = adapters

    def adapter_of(adapter_table):
        return jnp.einsum('a,ard->rd', select, adapter_table, precision=HIGHEST)

    def adapted(source, weight, down_table, lift_table, bias_vec):
        ranked = low_back(low(exact_product(source, adapter_of(down_table).T)))
        combined = exact_product(source, weight) + exact_product(ranked, adapter_of(lift_table))
        return combined + bias_vec
    seq_len = inputs_tree.shape[0]
    head_count = D // HEAD_DIM
    normed_one = low(layer_norm(inputs_tree, gain_one, shift_one))
    queries = low_back(low(adapted(normed_one, query_weight, query_down, query_up, query_bias)))
    keys_all = low_back(low(adapted(normed_one, key_weight, key_down, key_up, 0.0)))
    values_all = low_back(low(adapted(normed_one, value_weight, value_down, value_up, value_bias)))
    query_heads = queries.reshape(seq_len, head_count, HEAD_DIM)
    key_heads = keys_all.reshape(seq_len, head_count, HEAD_DIM)
    value_heads = values_all.reshape(seq_len, head_count, HEAD_DIM)
    block_rows = min(512, seq_len)
    block_count = seq_len // block_rows
    score_scale = HEAD_DIM ** (-0.5)

    def attend(block_index):
        row_start = block_index * block_rows
        query_rows = lax.dynamic_slice_in_dim(query_heads, row_start, block_rows, 0)
        mask_rows = lax.dynamic_slice_in_dim(allowed, row_start, block_rows, 0)
        scores = low_back(jnp.einsum('qhd,khd->hqk', query_rows, key_heads, precision=HIGHEST) * score_scale)
        scores = jnp.where(mask_rows[None], scores, -1e+30)
        row_top = lax.optimization_barrier(jnp.max(scores, axis=-1, keepdims=True))
        raised = jnp.exp(scores - row_top)
        probs = low(raised / lax.optimization_barrier(jnp.sum(raised, axis=-1, keepdims=True)))
        return jnp.einsum('hqk,khd->qhd', probs, value_heads, precision=HIGHEST)
    blocks_out = lax.map(jax.checkpoint(attend), jnp.arange(block_count, dtype=jnp.int32))
    attended = low_back(low(blocks_out.reshape(seq_len, D)))
    branch = low_back(adapted(attended, output_weight, output_down, output_up, output_bias))
    residual = inputs_tree + branch
    normed_two = low(layer_norm(residual, gain_two, shift_two))
    pre_act = low_back(adapted(normed_two, expand_weight, expand_down, expand_up, expand_bias))
    hidden = low(jax.nn.gelu(pre_act, approximate=False))
    mlp_out = low_back(adapted(hidden, shrink_weight, shrink_down, shrink_up, shrink_bias))
    return residual + mlp_out

def reference(inputs, cotangent, segment_ids, parent_links, adapter_choice, gain_one, shift_one, gain_two, shift_two, query_weight, key_weight, value_weight, output_weight, expand_weight, shrink_weight, query_bias, value_bias, output_bias, expand_bias, shrink_bias, query_down, query_up, key_down, key_up, value_down, value_up, output_down, output_up, expand_down, expand_up, shrink_down, shrink_up):
    frozen = tuple((member.astype(jnp.float32) for member in (gain_one, shift_one, gain_two, shift_two, query_weight, key_weight, value_weight, output_weight, expand_weight, shrink_weight, query_bias, value_bias, output_bias, expand_bias, shrink_bias)))
    adapters = tuple((member.astype(jnp.float32) for member in (query_down, query_up, key_down, key_up, value_down, value_up, output_down, output_up, expand_down, expand_up, shrink_down, shrink_up)))
    tree_inputs = inputs.astype(jnp.float32).reshape(TREES, SEQ, D)
    tree_cots = cotangent.astype(jnp.float32).reshape(TREES, SEQ, D)
    positions = jnp.arange(SEQ, dtype=jnp.int32)

    def one_tree(running, tree_parts):
        tree_x, tree_cot, seg_row, parents, chosen = tree_parts
        select = (jnp.arange(ADAPTERS, dtype=jnp.int32) == chosen).astype(jnp.float32)
        ancestors = ancestry(parents)
        allowed = jnp.logical_and(ancestors[seg_row][:, seg_row], positions[None, :] <= positions[:, None])
        primal, pullback = jax.vjp(lambda rows_in, adapt_in: tree_forward(rows_in, adapt_in, frozen, select, allowed), tree_x, adapters)
        input_grad, adapter_grads = pullback(tree_cot)
        running = tuple((total + extra for total, extra in zip(running, adapter_grads)))
        return (running, (primal.astype(jnp.bfloat16), input_grad.astype(jnp.bfloat16)))
    start_sums = tuple((jnp.zeros(member.shape, jnp.float32) for member in adapters))
    sums, (outs_tree, grads_tree) = lax.scan(one_tree, start_sums, (tree_inputs, tree_cots, segment_ids, parent_links, adapter_choice))
    return (outs_tree.reshape(TOKENS, D), grads_tree.reshape(TOKENS, D), sums[0], sums[1], sums[2], sums[3], sums[4], sums[5], sums[6], sums[7], sums[8], sums[9], sums[10], sums[11])
```

```python
import functools

import jax
import jax.numpy as jnp
from jax import lax
from jax.sharding import PartitionSpec as P

HEAD_DIM = 128
SEGS = 13
BF = jnp.bfloat16
F32 = jnp.float32


def ancestry(parents):
    seg_range = jnp.arange(SEGS, dtype=jnp.int32)
    current = seg_range
    ancestors = current[:, None] == seg_range[None, :]
    for hop_index in range(SEGS - 1):
        current = jnp.sum(
            jnp.where(current[:, None] == seg_range[None, :], parents[None, :], 0), axis=1
        )
        ancestors = jnp.logical_or(ancestors, current[:, None] == seg_range[None, :])
    return ancestors


def product(left, right):
    return jnp.dot(left, right, preferred_element_type=F32)


def product_cols(left, right):
    return lax.dot_general(
        left, right, (((1,), (1,)), ((), ())), preferred_element_type=F32
    )


def product_rows(left, right):
    return lax.dot_general(
        left, right, (((0,), (0,)), ((), ())), preferred_element_type=F32
    )


def shards(
    dp_size,
    inputs,
    cotangent,
    segment_ids,
    parent_links,
    adapter_choice,
    gain_one,
    shift_one,
    gain_two,
    shift_two,
    query_weight,
    key_weight,
    value_weight,
    output_weight,
    expand_weight,
    shrink_weight,
    query_bias,
    value_bias,
    output_bias,
    expand_bias,
    shrink_bias,
    query_down,
    query_up,
    key_down,
    key_up,
    value_down,
    value_up,
    output_down,
    output_up,
    expand_down,
    expand_up,
    shrink_down,
    shrink_up,
):
    slot_count = query_down.shape[0]
    rank_width = query_down.shape[1]
    feats = inputs.shape[1]
    row_count = inputs.shape[0]
    width_local = query_weight.shape[1]
    hidden_local = expand_weight.shape[1]
    pair_count = dp_size // 2
    block = feats // dp_size
    half = feats // 2

    tensor_index = lax.axis_index("tensor")
    core_odd = (tensor_index % 2) == 1
    chip_odd = (tensor_index // 2) == 1
    dp_odd = (lax.axis_index("dp") % 2) == 1

    core_pairs = [(0, 1), (1, 0), (2, 3), (3, 2)]
    chip_pairs = [(0, 2), (2, 0), (1, 3), (3, 1)]
    dp_pairs = [(i, i ^ 1) for i in range(dp_size)]
    line_groups = [list(range(0, dp_size, 2)), list(range(1, dp_size, 2))]

    def to_core(v):
        return lax.ppermute(v, "tensor", core_pairs)

    def to_chip(v):
        return lax.ppermute(v, "tensor", chip_pairs)

    def own_first(v):
        parts = [v[..., b * block : (b + 1) * block] for b in range(dp_size)]
        pairs = [(parts[2 * p], parts[2 * p + 1]) for p in range(pair_count)]
        return jnp.concatenate(
            [jnp.where(dp_odd, odd, even) for even, odd in pairs]
            + [jnp.where(dp_odd, even, odd) for even, odd in pairs],
            axis=-1,
        )

    def natural(v):
        parts = [v[..., b * block : (b + 1) * block] for b in range(dp_size)]
        pairs = [(parts[p], parts[pair_count + p]) for p in range(pair_count)]
        return jnp.concatenate(
            [
                jnp.where(dp_odd, a, b)
                for own, other in pairs
                for a, b in ((other, own), (own, other))
            ],
            axis=-1,
        )

    def after(value, *others):
        return lax.optimization_barrier((value,) + others)[0]

    def swap_blocks(v):
        parts = [v[k * row_count : (k + 1) * row_count] for k in range(4)]
        low = [jnp.where(core_odd, parts[1], parts[0]), jnp.where(core_odd, parts[0], parts[1])]
        high = [jnp.where(core_odd, parts[3], parts[2]), jnp.where(core_odd, parts[2], parts[3])]
        return jnp.concatenate(
            [
                jnp.where(chip_odd, high[0], low[0]),
                jnp.where(chip_odd, high[1], low[1]),
                jnp.where(chip_odd, low[0], high[0]),
                jnp.where(chip_odd, low[1], high[1]),
            ],
            axis=0,
        )

    def gather_rows(rows):
        near = to_core(rows)
        far = to_chip(rows)
        far_near = to_core(far)
        return jnp.concatenate([rows, near, far, far_near], axis=0)

    def reduce_rows(partial):
        parts = [partial[k * row_count : (k + 1) * row_count] for k in range(4)]
        far = parts[2] + to_core(parts[3].astype(BF)).astype(F32)
        far_sum = to_chip(far.astype(BF))
        near = parts[0] + to_core(parts[1].astype(BF)).astype(F32)
        return near + far_sum.astype(F32)

    def fetch(pieces, *held):
        shard = jnp.concatenate(pieces, axis=1)
        if held:
            shard = after(shard, *held)
        own = lax.all_gather(shard, "dp", axis=0, tiled=True, axis_index_groups=line_groups)
        return own, lax.ppermute(own, "dp", dp_pairs), 0

    def fetch_paired(pieces, *held):
        shard = jnp.concatenate(pieces, axis=1)
        shard = jnp.concatenate([shard, lax.ppermute(shard, "dp", dp_pairs)], axis=1)
        if held:
            shard = after(shard, *held)
        both = lax.all_gather(shard, "dp", axis=0, tiled=True, axis_index_groups=line_groups)
        return both, both, shard.shape[1] // 2

    def into(left, weight, first, last):
        own, other, skip = weight
        return product(left[:, :half], own[:, first:last]) + product(
            left[:, half:], other[:, skip + first : skip + last]
        )

    def out_of(left, weight, first, last, base=None):
        own, other, skip = weight
        near = product_cols(left, own[:, first:last])
        far = product_cols(left, other[:, skip + first : skip + last])
        if base is not None:
            near, far = base[0] + near, base[1] + far
        return near, far

    def beside(pair):
        return jnp.concatenate(pair, axis=1)

    chunk_count = 4
    chunk = hidden_local // chunk_count
    output_turned = output_weight.T
    shrink_turned = shrink_weight.T
    weight_qk = fetch([query_weight, key_weight])
    weight_vo = fetch([value_weight, output_turned])
    weight_ffn, held = [], [weight_qk, weight_vo]
    for h in range(chunk_count):
        pieces = [
            expand_weight[:, h * chunk : (h + 1) * chunk],
            shrink_turned[:, h * chunk : (h + 1) * chunk],
        ]
        got = (fetch_paired if h == chunk_count - 1 else fetch)(pieces, held[-2][0])
        held.append(got)
        weight_ffn.append(got)

    select = (jnp.arange(slot_count, dtype=jnp.int32) == adapter_choice[0]).astype(BF)

    def adapter_of(adapter_table):
        return jnp.einsum(
            "a,ard->rd", select, adapter_table, preferred_element_type=F32
        ).astype(BF)

    down_qkv = own_first(
        jnp.concatenate(
            [adapter_of(query_down), adapter_of(key_down), adapter_of(value_down)], axis=0
        )
    )
    lift_query = adapter_of(query_up)
    lift_key = adapter_of(key_up)
    lift_value = adapter_of(value_up)
    down_output = adapter_of(output_down)
    lift_output = own_first(adapter_of(output_up))
    down_expand = own_first(adapter_of(expand_down))
    lift_expand = adapter_of(expand_up)
    down_shrink = adapter_of(shrink_down)
    lift_shrink = own_first(adapter_of(shrink_up))

    gain_a, shift_a = own_first(gain_one), own_first(shift_one)
    gain_b, shift_b = own_first(gain_two), own_first(shift_two)
    out_bias = own_first(output_bias)
    last_bias = own_first(shrink_bias)

    def normalize(values):
        row_mean = jnp.mean(values, axis=-1, keepdims=True)
        centred = values - row_mean
        row_var = jnp.mean(centred * centred, axis=-1, keepdims=True)
        scale = lax.rsqrt(row_var + 1e-05)
        return centred * scale, scale

    def norm_back(grad, gain, unit, scale):
        scaled = grad * gain
        return (
            scaled
            - jnp.mean(scaled, axis=-1, keepdims=True)
            - unit * jnp.mean(scaled * unit, axis=-1, keepdims=True)
        ) * scale

    inputs_wide = own_first(inputs).astype(F32)
    cot = own_first(cotangent)
    unit_one, scale_one = normalize(inputs_wide)
    rows_one = (unit_one * gain_a + shift_a).astype(BF)
    full_one = gather_rows(rows_one)
    full_cot = gather_rows(cot)
    seq_len = full_one.shape[0]
    head_count = width_local // HEAD_DIM

    rank_one = product_cols(full_one, down_qkv).astype(BF)
    rank_query = rank_one[:, :rank_width]
    rank_key = rank_one[:, rank_width : 2 * rank_width]
    rank_value = rank_one[:, 2 * rank_width :]
    query_key = into(after(full_one, weight_vo[0]), weight_qk, 0, 2 * width_local)
    queries = swap_blocks(
        (query_key[:, :width_local] + product(rank_query, lift_query) + query_bias).astype(BF)
    )
    keys_low = swap_blocks((query_key[:, width_local:] + product(rank_key, lift_key)).astype(BF))
    values_low = swap_blocks(
        (
            into(after(full_one, weight_ffn[0][0]), weight_vo, 0, width_local)
            + product(rank_value, lift_value)
            + value_bias
        ).astype(BF)
    )
    seg_range = jnp.arange(SEGS, dtype=jnp.int32)
    seg_hot = (segment_ids[0][:, None] == seg_range[None, :]).astype(BF)
    path_hot = product(seg_hot, ancestry(parent_links[0]).astype(BF)).astype(BF)
    positions = jnp.arange(seq_len, dtype=jnp.int32)
    block_rows = min(512, seq_len)
    block_count = seq_len // block_rows
    score_scale = HEAD_DIM ** (-0.5)
    query_heads = queries.reshape(seq_len, head_count, HEAD_DIM)
    key_heads = keys_low.reshape(seq_len, head_count, HEAD_DIM)
    value_heads = values_low.reshape(seq_len, head_count, HEAD_DIM)

    def block_scores(row_start, key_end):
        same_path = (
            product_cols(path_hot[row_start : row_start + block_rows], seg_hot[:key_end]) > 0.5
        )
        causal = positions[row_start : row_start + block_rows, None] >= positions[None, :key_end]
        raw_scores = (
            jnp.einsum(
                "qhd,khd->hqk",
                query_heads[row_start : row_start + block_rows],
                key_heads[:key_end],
                preferred_element_type=F32,
            )
            * score_scale
        )
        return jnp.where(jnp.logical_and(same_path, causal)[None], raw_scores, -1e30)

    attended_parts = []
    lse_parts = []
    for block_index in range(block_count):
        row_start = block_index * block_rows
        key_end = row_start + block_rows
        scores = block_scores(row_start, key_end)
        row_top = jnp.max(scores, axis=-1, keepdims=True)
        raised = jnp.exp(scores - row_top)
        row_total = jnp.sum(raised, axis=-1, keepdims=True)
        lse_parts.append(row_top + jnp.log(row_total))
        probs_low = (raised / row_total).astype(BF)
        attended_parts.append(
            jnp.einsum(
                "hqk,khd->qhd", probs_low, value_heads[:key_end], preferred_element_type=F32
            )
        )
    attended = swap_blocks(
        jnp.concatenate(attended_parts, axis=0).reshape(seq_len, width_local).astype(BF)
    )
    rank_out = product_cols(attended, down_output).astype(BF)
    main_rows = reduce_rows(
        beside(out_of(attended, weight_vo, width_local, 2 * width_local))
        + product(rank_out, lift_output)
    )
    main_rows = after(main_rows, weight_ffn[1][0])
    residual = inputs_wide + main_rows + out_bias
    unit_two, scale_two = normalize(residual)
    rows_two = (unit_two * gain_b + shift_b).astype(BF)
    full_two = after(gather_rows(rows_two), weight_ffn[2][0])
    rank_two = product_cols(full_two, down_expand).astype(BF)
    rank_grad = product_cols(full_cot, lift_shrink).astype(BF)

    hidden_parts = []
    grad_pre_parts = []
    grad_two, main_two = None, None
    for h in range(chunk_count):
        cols = slice(h * chunk, (h + 1) * chunk)
        weight = weight_ffn[h]
        here_two, here_cot = full_two, full_cot
        if h:
            here_two, here_cot, _ = lax.optimization_barrier(
                (full_two, full_cot, grad_pre_parts[-1])
            )
        pre_act = (
            into(here_two, weight, 0, chunk)
            + product(rank_two, lift_expand[:, cols])
            + expand_bias[cols]
        )
        grad_hidden = into(here_cot, weight, chunk, 2 * chunk) + product(
            rank_grad, down_shrink[:, cols]
        )
        bell = 0.5 * (1.0 + lax.erf(pre_act * (0.5**0.5)))
        slope = bell + pre_act * jnp.exp(-0.5 * pre_act * pre_act) * (0.5 / jnp.pi) ** 0.5
        hidden_parts.append((pre_act * bell).astype(BF))
        grad_pre_parts.append((grad_hidden * slope).astype(BF))
        grad_two = out_of(grad_pre_parts[h], weight, 0, chunk, grad_two)
        main_two = out_of(hidden_parts[h], weight, chunk, 2 * chunk, main_two)

    grad_rank_two = sum(
        product_cols(grad_pre_parts[h], lift_expand[:, h * chunk : (h + 1) * chunk])
        for h in range(chunk_count)
    ).astype(BF)
    grad_norm_two = reduce_rows(beside(grad_two) + product(grad_rank_two, down_expand))
    grad_residual = cot.astype(F32) + norm_back(grad_norm_two, gain_b, unit_two, scale_two)
    grad_branch = grad_residual.astype(BF)
    full_branch = gather_rows(grad_branch)
    rank_grad_out = product_cols(full_branch, lift_output).astype(BF)
    grad_attended = swap_blocks(
        (
            into(full_branch, weight_vo, width_local, 2 * width_local)
            + product(rank_grad_out, down_output)
        ).astype(BF)
    )

    rank_shrink = sum(
        product_cols(hidden_parts[h], down_shrink[:, h * chunk : (h + 1) * chunk])
        for h in range(chunk_count)
    ).astype(BF)
    main_rows_two = reduce_rows(beside(main_two) + product(rank_shrink, lift_shrink))
    output = natural((residual + main_rows_two + last_bias).astype(BF))

    delta_shrink_up = product_rows(rank_shrink, full_cot)
    delta_expand_down = product_rows(grad_rank_two, full_two)
    delta_output_up = product_rows(rank_out, full_branch)
    delta_shrink_down = jnp.concatenate(
        [product_rows(rank_grad, part) for part in hidden_parts], axis=1
    )
    delta_expand_up = jnp.concatenate(
        [product_rows(rank_two, part) for part in grad_pre_parts], axis=1
    )
    delta_output_down = product_rows(rank_grad_out, attended)

    hot_lanes = (
        jnp.arange(128, dtype=jnp.int32)[None, :] == adapter_choice[0]
    ).astype(BF) * jnp.ones((rank_width, 1), BF)

    def by_tensor(parts):
        low = [jnp.where(core_odd, parts[1], parts[0]), jnp.where(core_odd, parts[0], parts[1])]
        high = [jnp.where(core_odd, parts[3], parts[2]), jnp.where(core_odd, parts[2], parts[3])]
        return [jnp.where(chip_odd, b, a) for a, b in zip(low + high, high + low)]

    def settle(wide, slim):
        count = len(wide)
        quarter = feats // 4
        stacked = natural(jnp.concatenate(wide, axis=0).astype(BF))
        parts = by_tensor([stacked[:, t * quarter : (t + 1) * quarter] for t in range(4)])
        got = to_core(jnp.concatenate([parts[1], parts[3]], axis=0)).astype(F32)
        rows = stacked.shape[0]
        far = to_chip((parts[2] + got[rows:]).astype(BF)).astype(F32)
        mine = (parts[0] + got[:rows] + far).astype(BF)
        flat = jnp.concatenate(
            [mine[k * rank_width : (k + 1) * rank_width] for k in range(count)]
            + [d.astype(BF) for d in slim]
            + [hot_lanes],
            axis=1,
        )
        pair = jnp.stack([flat, lax.ppermute(flat, "dp", dp_pairs)])
        trees = [pair] + [
            lax.ppermute(pair, "dp", [(i, (i + 2 * s) % dp_size) for i in range(dp_size)])
            for s in range(1, pair_count)
        ]
        trees = jnp.concatenate(trees, axis=0)
        hot = trees[:, 0, flat.shape[1] - 128 : flat.shape[1] - 128 + slot_count]
        summed = lax.dot_general(
            hot,
            trees[:, :, : flat.shape[1] - 128],
            (((0,), (0,)), ((), ())),
            preferred_element_type=F32,
        )
        own = summed[:, :, : count * quarter].astype(BF)
        near = to_core(own)
        away = to_chip(own)
        across = by_tensor([own, near, away, to_core(away)])
        wide_out = [
            jnp.concatenate(
                [piece[:, :, k * quarter : (k + 1) * quarter] for piece in across], axis=-1
            ).astype(F32)
            for k in range(count)
        ]
        slim_out, at = [], count * quarter
        for d in slim:
            slim_out.append(summed[:, :, at : at + d.shape[1]])
            at += d.shape[1]
        return wide_out, slim_out

    (shrink_up_out, expand_down_out, output_up_out), (
        shrink_down_out,
        expand_up_out,
        output_down_out,
    ) = settle(
        [delta_shrink_up, delta_expand_down, delta_output_up],
        [delta_shrink_down, delta_expand_up, delta_output_down],
    )

    grad_heads = grad_attended.reshape(seq_len, head_count, HEAD_DIM)
    grad_query_parts = []
    grad_keys = jnp.zeros((seq_len, head_count, HEAD_DIM), F32)
    grad_values = jnp.zeros((seq_len, head_count, HEAD_DIM), F32)
    for block_index in range(block_count):
        row_start = block_index * block_rows
        key_end = row_start + block_rows
        scores = block_scores(row_start, key_end)
        probs = jnp.exp(scores - lse_parts[block_index])
        probs_low = probs.astype(BF)
        grad_block = grad_heads[row_start:key_end]
        grad_values = grad_values.at[:key_end].add(
            jnp.einsum("hqk,qhd->khd", probs_low, grad_block, preferred_element_type=F32)
        )
        grad_probs = jnp.einsum(
            "qhd,khd->hqk", grad_block, value_heads[:key_end], preferred_element_type=F32
        )
        grad_scores = (
            probs * (grad_probs - jnp.sum(grad_probs * probs, axis=-1, keepdims=True))
        ).astype(BF)
        grad_query_parts.append(
            jnp.einsum(
                "hqk,khd->qhd", grad_scores, key_heads[:key_end], preferred_element_type=F32
            )
            * score_scale
        )
        grad_keys = grad_keys.at[:key_end].add(
            jnp.einsum(
                "hqk,qhd->khd",
                grad_scores,
                query_heads[row_start:key_end],
                preferred_element_type=F32,
            )
            * score_scale
        )
    grad_query_low = swap_blocks(
        jnp.concatenate(grad_query_parts, axis=0).reshape(seq_len, width_local).astype(BF)
    )
    grad_key_low = swap_blocks(grad_keys.reshape(seq_len, width_local).astype(BF))
    grad_value_low = swap_blocks(grad_values.reshape(seq_len, width_local).astype(BF))
    delta_query_up = product_rows(rank_query, grad_query_low)
    delta_key_up = product_rows(rank_key, grad_key_low)
    delta_value_up = product_rows(rank_value, grad_value_low)
    grad_rank_one = jnp.concatenate(
        [
            product_cols(grad_query_low, lift_query),
            product_cols(grad_key_low, lift_key),
            product_cols(grad_value_low, lift_value),
        ],
        axis=1,
    ).astype(BF)
    grad_rows_one = (
        beside(
            out_of(
                grad_value_low,
                weight_vo,
                0,
                width_local,
                out_of(
                    jnp.concatenate([grad_query_low, grad_key_low], axis=1),
                    weight_qk,
                    0,
                    2 * width_local,
                ),
            )
        )
        + product(grad_rank_one, down_qkv)
    )
    delta_qkv_down = product_rows(grad_rank_one, full_one)
    grad_norm_one = reduce_rows(grad_rows_one)
    input_delta = natural(
        (grad_residual + norm_back(grad_norm_one, gain_a, unit_one, scale_one)).astype(BF)
    )
    (query_down_out, key_down_out, value_down_out), (
        query_up_out,
        key_up_out,
        value_up_out,
    ) = settle(
        [
            delta_qkv_down[:rank_width],
            delta_qkv_down[rank_width : 2 * rank_width],
            delta_qkv_down[2 * rank_width :],
        ],
        [delta_query_up, delta_key_up, delta_value_up],
    )
    return (
        output,
        input_delta,
        query_down_out,
        query_up_out,
        key_down_out,
        key_up_out,
        value_down_out,
        value_up_out,
        output_down_out,
        output_up_out,
        expand_down_out,
        expand_up_out,
        shrink_down_out,
        shrink_up_out,
    )


def solution(mesh):
    rows = P(("dp", "tensor"), None)
    tree = P("dp", None)
    whole = P()
    slim = P(None, None, "tensor")
    inward = P("dp", "tensor")
    outward = P("tensor", "dp")
    return jax.shard_map(
        functools.partial(shards, mesh.shape["dp"]),
        mesh=mesh,
        in_specs=(
            rows,
            rows,
            tree,
            tree,
            P("dp"),
            whole,
            whole,
            whole,
            whole,
            inward,
            inward,
            inward,
            outward,
            inward,
            outward,
            P("tensor"),
            P("tensor"),
            whole,
            P("tensor"),
            whole,
            whole,
            slim,
            whole,
            slim,
            whole,
            slim,
            slim,
            whole,
            whole,
            slim,
            slim,
            whole,
        ),
        out_specs=(
            rows,
            rows,
            whole,
            slim,
            whole,
            slim,
            whole,
            slim,
            slim,
            whole,
            whole,
            slim,
            slim,
            whole,
        ),
        check_vma=False,
    )
```

```python
import functools

import jax
import jax.numpy as jnp
from jax import lax
from jax.experimental import pallas as pl
from jax.experimental.pallas import tpu as pltpu
from jax.sharding import PartitionSpec as P

HEAD_DIM = 128
SEGS = 13
BF = jnp.bfloat16
F32 = jnp.float32


def ancestry(parents):
    seg_range = jnp.arange(SEGS, dtype=jnp.int32)
    current = seg_range
    ancestors = current[:, None] == seg_range[None, :]
    for hop_index in range(SEGS - 1):
        current = jnp.sum(
            jnp.where(current[:, None] == seg_range[None, :], parents[None, :], 0), axis=1
        )
        ancestors = jnp.logical_or(ancestors, current[:, None] == seg_range[None, :])
    return ancestors


def product(left, right):
    return jnp.dot(left, right, preferred_element_type=F32)


def product_cols(left, right):
    return lax.dot_general(
        left, right, (((1,), (1,)), ((), ())), preferred_element_type=F32
    )


def product_rows(left, right):
    return lax.dot_general(
        left, right, (((0,), (0,)), ((), ())), preferred_element_type=F32
    )


def feed_kernel(first, last, pieces, *refs):
    rows, cots, rank_in, rank_grad, lift, bias, down = refs[:7]
    weights, refs = refs[7 : 7 + pieces], refs[7 + pieces :]
    if not first:
        main_in, grad_in, rank_main_in, rank_back_in = refs[:4]
        refs = refs[4:]
    if last:
        lift_after, down_before = refs[:2]
        refs = refs[2:]
    mains, grads = refs[: len(refs) // 2 - 2], refs[len(refs) // 2 - 2 : -4]
    rank_main, rank_back, down_delta, up_delta = refs[-4:]
    chunk = lift.shape[1]
    parts, at = [], 0
    for weight in weights:
        parts.append((slice(at, at + weight.shape[0]), weight))
        at += weight.shape[0]

    pre_act = (
        sum(product(rows[:, here], weight[:, :chunk]) for here, weight in parts)
        + product(rank_in[...], lift[...])
        + bias[...]
    )
    grad_hidden = sum(
        product(cots[:, here], weight[:, chunk:]) for here, weight in parts
    ) + product(rank_grad[...], down[...])
    bell = 0.5 * (1.0 + lax.erf(pre_act * (0.5**0.5)))
    slope = bell + pre_act * jnp.exp(-0.5 * pre_act * pre_act) * (0.5 / jnp.pi) ** 0.5
    hidden = (pre_act * bell).astype(BF)
    grad_pre = (grad_hidden * slope).astype(BF)

    main_rank = product_cols(hidden, down[...])
    back_rank = product_cols(grad_pre, lift[...])
    if not first:
        main_rank = main_rank + rank_main_in[...]
        back_rank = back_rank + rank_back_in[...]
    rank_main[...] = main_rank
    rank_back[...] = back_rank
    for here, weight in parts:
        ahead = product_cols(hidden, weight[:, chunk:])
        back = product_cols(grad_pre, weight[:, :chunk])
        if not first:
            ahead = ahead + main_in[:, here]
            back = back + grad_in[:, here]
        if last:
            ahead = ahead + product(main_rank.astype(BF), lift_after[:, here])
            back = back + product(back_rank.astype(BF), down_before[:, here])
        for k, (main, grad) in enumerate(zip(mains, grads)):

            @pl.when((pl.program_id(0) == k) | (len(mains) == 1))
            def _(main=main, grad=grad, here=here, ahead=ahead, back=back):
                main[:, here] = ahead.astype(main.dtype)
                grad[:, here] = back.astype(grad.dtype)

    down_part = product_rows(rank_grad[...], hidden)
    up_part = product_rows(rank_in[...], grad_pre)

    @pl.when(pl.program_id(0) == 0)
    def _():
        down_delta[...] = down_part
        up_delta[...] = up_part

    @pl.when(pl.program_id(0) > 0)
    def _():
        down_delta[...] += down_part
        up_delta[...] += up_part


def feed_forward(rows, cots, rank_in, rank_grad, weight, lift, bias, down, at, before, final, span):
    tile = 256
    feats = rows.shape[1]
    chunk = bias.shape[0]
    rank = lift.shape[0]
    begin, count = span[0] // tile, (span[1] - span[0]) // tile
    first, last = before is None, final is not None

    def row_block(width):
        return pl.BlockSpec((tile, width), lambda i: (begin + i, 0))

    def out_block(width):
        return pl.BlockSpec((tile, width), lambda i: (i, 0))

    def fixed(shape, column=0):
        return pl.BlockSpec(shape, lambda i: (0, column), pipeline_mode=pl.Buffered(1))

    args = [rows, cots, rank_in, rank_grad, lift, bias[None], down]
    specs = [
        row_block(feats),
        row_block(feats),
        row_block(rank),
        row_block(rank),
        fixed((rank, chunk), at),
        fixed((1, chunk), 0),
        fixed((rank, chunk), at),
    ]
    for piece, column in weight:
        args.append(piece)
        specs.append(fixed((piece.shape[0], 2 * chunk), column))
    if not first:
        args += [before[0][0], before[1][0], before[2], before[3]]
        specs += [row_block(feats), row_block(feats), row_block(rank), row_block(rank)]
    if last:
        args += list(final)
        specs += [fixed((rank, feats)), fixed((rank, feats))]
    size = span[1] - span[0]
    flops = size * feats * chunk
    if last:
        wide_specs = [fixed((tile, feats))] * (2 * count)
        wide_shapes = [jax.ShapeDtypeStruct((tile, feats), BF)] * (2 * count)
    else:
        wide_specs = [out_block(feats)] * 2
        wide_shapes = [jax.ShapeDtypeStruct((size, feats), F32)] * 2
    results = pl.pallas_call(
        functools.partial(feed_kernel, first, last, len(weight)),
        grid=(count,),
        in_specs=specs,
        out_specs=wide_specs
        + [
            out_block(rank),
            out_block(rank),
            pl.BlockSpec((rank, chunk), lambda i: (0, 0)),
            pl.BlockSpec((rank, chunk), lambda i: (0, 0)),
        ],
        out_shape=wide_shapes
        + [
            jax.ShapeDtypeStruct((size, rank), F32),
            jax.ShapeDtypeStruct((size, rank), F32),
            jax.ShapeDtypeStruct((rank, chunk), F32),
            jax.ShapeDtypeStruct((rank, chunk), F32),
        ],
        cost_estimate=pl.CostEstimate(
            flops=flops, bytes_accessed=size * feats * 20, transcendentals=size * chunk * 2
        ),
        name="feed_forward",
    )(*args)
    wide = len(wide_specs) // 2
    return results[:wide], results[wide : 2 * wide], *results[2 * wide :]


def attend_kernel(scale, turn, *refs):
    count = (len(refs) - 3) // 3
    query, key, value = refs[:count], refs[count : 2 * count], refs[2 * count : 3 * count]
    bias, attended, level = refs[3 * count :]
    rows = query[0].shape[0]
    for i in range(count):
        here = slice(i * rows, (i + 1) * rows)
        scores = [
            product_cols(query[i][...], key[j][...]) * scale
            + bias[here, j * rows : (j + 1) * rows]
            for j in range(i + 1)
        ]
        top = functools.reduce(
            jnp.maximum, [jnp.max(v, axis=-1, keepdims=True) for v in scores]
        )
        raised = [jnp.exp(v - top) for v in scores]
        total = sum(jnp.sum(v, axis=-1, keepdims=True) for v in raised)
        share = 1.0 / total
        mixed = sum(
            product((v * share).astype(BF), value[j][...]) for j, v in enumerate(raised)
        )
        to = pl.multiple_of((i ^ turn[0]) * rows, rows)
        attended[pl.ds(to, rows), :] = mixed.astype(BF)
        level[here, :] = jnp.broadcast_to(top + jnp.log(total), (rows, level.shape[1]))


def attend_back_kernel(scale, turn, *refs):
    count = (len(refs) - 7) // 4 if len(refs) % 4 == 3 else (len(refs) - 10) // 4
    query, key, value, grad = (refs[n * count : (n + 1) * count] for n in range(4))
    bias, level = refs[4 * count : 4 * count + 2]
    grad_query, grad_key, grad_value, key_sum, value_sum = refs[-5:]
    rows = query[0].shape[0]
    for i in range(count):
        here = slice(i * rows, (i + 1) * rows)
        row_level = level[here, :1]
        probs = [
            jnp.exp(
                product_cols(query[i][...], key[j][...]) * scale
                + bias[here, j * rows : (j + 1) * rows]
                - row_level
            )
            for j in range(i + 1)
        ]
        grad_probs = [product_cols(grad[i][...], value[j][...]) for j in range(i + 1)]
        mean = sum(
            jnp.sum(p * g, axis=-1, keepdims=True) for p, g in zip(probs, grad_probs)
        )
        query_sum = 0.0
        for j in range(i + 1):
            there = slice(j * rows, (j + 1) * rows)
            grad_score = (probs[j] * (grad_probs[j] - mean)).astype(BF)
            query_sum = query_sum + product(grad_score, key[j][...])
            key_part = product_rows(grad_score, query[i][...])
            value_part = product_rows(probs[j].astype(BF), grad[i][...])
            if i > j:
                key_part = key_part + key_sum[there, :]
                value_part = value_part + value_sum[there, :]
            key_sum[there, :] = key_part
            value_sum[there, :] = value_part
        to = pl.multiple_of((i ^ turn[0]) * rows, rows)
        grad_query[pl.ds(to, rows), :] = (query_sum * scale).astype(BF)
    for j in range(count):
        there = slice(j * rows, (j + 1) * rows)
        to = pl.multiple_of((j ^ turn[0]) * rows, rows)
        grad_key[pl.ds(to, rows), :] = (key_sum[there, :] * scale).astype(BF)
        grad_value[pl.ds(to, rows), :] = value_sum[there, :].astype(BF)


def by_head(kernel, turn, blocked, whole, outs, scratch, heads, name, before=()):
    first, count = heads
    seq_len, width = blocked[0].shape
    blocks = 4
    rows = seq_len // blocks
    specs, args = [], []
    for v in blocked:
        for k in range(blocks):
            specs.append(
                pl.BlockSpec((rows, HEAD_DIM), lambda h, turn, k=k: (k ^ turn[0], first + h))
            )
            args.append(v)
    for v in whole:
        if v.shape[1] == seq_len:
            specs.append(
                pl.BlockSpec(v.shape, lambda h, turn: (0, 0), pipeline_mode=pl.Buffered(1))
            )
        else:
            specs.append(pl.BlockSpec((seq_len, HEAD_DIM), lambda h, turn: (0, first + h)))
        args.append(v)
    aliases = {1 + len(args) + n: n for n in range(len(before))}
    specs += [pl.BlockSpec(memory_space=pl.ANY)] * len(before)
    args += before
    return pl.pallas_call(
        functools.partial(kernel, HEAD_DIM ** (-0.5)),
        grid_spec=pltpu.PrefetchScalarGridSpec(
            num_scalar_prefetch=1,
            grid=(count,),
            in_specs=specs,
            out_specs=[pl.BlockSpec((seq_len, HEAD_DIM), lambda h, turn: (0, first + h))] * len(outs),
            scratch_shapes=scratch,
        ),
        out_shape=[jax.ShapeDtypeStruct((seq_len, width), t) for t in outs],
        input_output_aliases=aliases,
        cost_estimate=pl.CostEstimate(flops=10**8, bytes_accessed=10**6, transcendentals=0),
        name=name,
    )(turn, *args)


def back_kernel(query, key, value, rank, qk_own, qk_other, vo_own, vo_other, down, *outs):
    width = query.shape[1]
    half = qk_own.shape[0]
    for at, qk, vo in ((0, qk_own, vo_own), (half, qk_other, vo_other)):
        rows = (
            product_cols(query[...], qk[:, :width])
            + product_cols(key[...], qk[:, width:])
            + product_cols(value[...], vo[...])
            + product(rank[...], down[:, at : at + half])
        ).astype(BF)
        for k, out in enumerate(outs):

            @pl.when(pl.program_id(0) == k)
            def _(out=out, rows=rows, at=at):
                out[:, at : at + half] = rows


def back_rows(grads, weight_qk, weight_vo, down, tile, first):
    half, width = weight_vo[0].shape[0], grads[0].shape[1]

    def fixed(shape):
        return pl.BlockSpec(shape, lambda i: (0, 0), pipeline_mode=pl.Buffered(1))

    return pl.pallas_call(
        back_kernel,
        grid=(2,),
        in_specs=[pl.BlockSpec((tile, v.shape[1]), lambda i: (first - i, 0)) for v in grads]
        + [fixed((half, 2 * width))] * 2
        + [fixed((half, width))] * 2
        + [fixed(down.shape)],
        out_specs=[fixed((tile, down.shape[1]))] * 2,
        out_shape=[jax.ShapeDtypeStruct((tile, down.shape[1]), BF)] * 2,
        cost_estimate=pl.CostEstimate(flops=10**8, bytes_accessed=10**6, transcendentals=0),
        name="back_rows",
    )(*grads, *weight_qk[:2], *weight_vo[:2], down)


def flat_kernel(rank, *refs):
    base, near, far, *slim, marks, out = refs
    mine = (
        base[...].astype(F32) + near[...].astype(F32) + far[...].astype(F32)
    ).astype(BF)
    width = mine.shape[1]
    at = 0
    for k in range(mine.shape[0] // rank):
        out[:, at : at + width] = mine[k * rank : (k + 1) * rank]
        at += width
    for part in slim:
        out[:, at : at + part.shape[1]] = part[...].astype(BF)
        at += part.shape[1]
    out[:, at:] = marks[...]


def slots_kernel(slot_count, rank, *refs):
    tree_count = len(refs) - 4
    trees = jnp.concatenate([ref[...] for ref in refs[:tree_count]], axis=0)
    lanes = slot_count * rank
    width = trees.shape[1] - lanes
    source = lax.broadcasted_iota(jnp.int32, (lanes, lanes), 0)
    target = lax.broadcasted_iota(jnp.int32, (lanes, lanes), 1)
    spread = jnp.where(source == target // rank, 1.0, 0.0).astype(BF)
    marks = product(trees[:, width:], spread)
    row = lax.broadcasted_iota(jnp.int32, marks.shape, 0)
    lane = lax.broadcasted_iota(jnp.int32, marks.shape, 1)
    marks = jnp.where(row % rank == lane % rank, marks, 0.0).astype(BF)
    at = 0
    for out in refs[tree_count:]:
        size = out.shape[1]
        out[...] = product_rows(marks, trees[:, at : at + size]).astype(out.dtype)
        at += size


def sum_slots(trees, slot_count, rank, wide, slim):
    rows = slot_count * rank
    wide_sum, *slim_sums = pl.pallas_call(
        functools.partial(slots_kernel, slot_count, rank),
        out_shape=[jax.ShapeDtypeStruct((rows, wide), BF)]
        + [jax.ShapeDtypeStruct((rows, n), F32) for n in slim],
        cost_estimate=pl.CostEstimate(
            flops=2 * rows * rows * (wide + sum(slim)),
            bytes_accessed=rows * (4 * wide + 6 * sum(slim)),
            transcendentals=0,
        ),
        name="sum_slots",
    )(*trees)
    return [v.reshape(slot_count, rank, -1) for v in (wide_sum, *slim_sums)]


def shards(
    dp_size,
    inputs,
    cotangent,
    segment_ids,
    parent_links,
    adapter_choice,
    gain_one,
    shift_one,
    gain_two,
    shift_two,
    query_weight,
    key_weight,
    value_weight,
    output_weight,
    expand_weight,
    shrink_weight,
    query_bias,
    value_bias,
    output_bias,
    expand_bias,
    shrink_bias,
    query_down,
    query_up,
    key_down,
    key_up,
    value_down,
    value_up,
    output_down,
    output_up,
    expand_down,
    expand_up,
    shrink_down,
    shrink_up,
):
    slot_count = query_down.shape[0]
    rank_width = query_down.shape[1]
    feats = inputs.shape[1]
    row_count = inputs.shape[0]
    width_local = query_weight.shape[1]
    hidden_local = expand_weight.shape[1]
    pair_count = dp_size // 2
    block = feats // dp_size
    half = feats // 2

    tensor_index = lax.axis_index("tensor")
    core_odd = (tensor_index % 2) == 1
    chip_odd = (tensor_index // 2) == 1
    dp_odd = (lax.axis_index("dp") % 2) == 1

    core_pairs = [(0, 1), (1, 0), (2, 3), (3, 2)]
    chip_pairs = [(0, 2), (2, 0), (1, 3), (3, 1)]
    dp_pairs = [(i, i ^ 1) for i in range(dp_size)]
    line_groups = [list(range(0, dp_size, 2)), list(range(1, dp_size, 2))]

    def to_core(v):
        return lax.ppermute(v, "tensor", core_pairs)

    def to_chip(v):
        return lax.ppermute(v, "tensor", chip_pairs)

    def own_first(v):
        parts = [v[..., b * block : (b + 1) * block] for b in range(dp_size)]
        pairs = [(parts[2 * p], parts[2 * p + 1]) for p in range(pair_count)]
        return jnp.concatenate(
            [jnp.where(dp_odd, odd, even) for even, odd in pairs]
            + [jnp.where(dp_odd, even, odd) for even, odd in pairs],
            axis=-1,
        )

    def natural(v):
        parts = [v[..., b * block : (b + 1) * block] for b in range(dp_size)]
        pairs = [(parts[p], parts[pair_count + p]) for p in range(pair_count)]
        return jnp.concatenate(
            [
                jnp.where(dp_odd, a, b)
                for own, other in pairs
                for a, b in ((other, own), (own, other))
            ],
            axis=-1,
        )

    def after(value, *others):
        return lax.optimization_barrier((value,) + others)[0]

    def gather_rows(rows, *held):
        near = to_core(rows)
        far = to_chip(rows)
        if held:
            far = after(far, *held)
        far_near = to_core(far)
        return jnp.concatenate([rows, near, far, far_near], axis=0)

    def reduce_rows(partial):
        parts = [partial[k * row_count : (k + 1) * row_count] for k in range(4)]
        far = parts[2] + to_core(parts[3].astype(BF)).astype(F32)
        far_sum = to_chip(far.astype(BF))
        near = parts[0] + to_core(parts[1].astype(BF)).astype(F32)
        return near + far_sum.astype(F32)

    def line_gather(shard, held):
        if held:
            shard = after(shard, *held)
        return lax.all_gather(shard, "dp", axis=0, tiled=True, axis_index_groups=line_groups)

    def fetch(shard, *held):
        own = line_gather(shard, held)
        return own, lax.ppermute(own, "dp", dp_pairs), 0

    def fetch_pieces(shard, *held):
        own = line_gather(shard, held)
        middle = own.shape[0] // 2
        swapped = [
            lax.ppermute(v, "dp", dp_pairs) for v in (own[:middle], own[middle:])
        ]
        return [(v, 0) for v in (own, *swapped)]

    def fetch_paired(pair, *held):
        both = line_gather(pair, held)
        return [(both, 0), (both, 1)]

    def into(left, weight, first, last):
        own, other, skip = weight
        return product(left[:, :half], own[:, first:last]) + product(
            left[:, half:], other[:, skip + first : skip + last]
        )

    def out_of(left, weight, first, last, base=None):
        own, other, skip = weight
        near = product_cols(left, own[:, first:last])
        far = product_cols(left, other[:, skip + first : skip + last])
        if base is not None:
            near, far = base[0] + near, base[1] + far
        return near, far

    def beside(pair):
        return jnp.concatenate(pair, axis=1)

    chunk_count = 4
    chunk = hidden_local // chunk_count
    output_turned = output_weight.T
    shrink_turned = shrink_weight.T
    def feed_shard(h):
        return jnp.concatenate(
            [
                expand_weight[:, h * chunk : (h + 1) * chunk],
                shrink_turned[:, h * chunk : (h + 1) * chunk],
            ],
            axis=1,
        )

    last_shard = feed_shard(chunk_count - 1)
    last_pair = jnp.concatenate([last_shard, lax.ppermute(last_shard, "dp", dp_pairs)], axis=1)
    weight_qk = fetch(jnp.concatenate([query_weight, key_weight], axis=1))
    weight_vo = fetch(jnp.concatenate([value_weight, output_turned], axis=1))
    weight_ffn, held = [], [weight_qk[0], weight_vo[0]]
    for h in range(chunk_count - 1):
        more = (last_pair,) if h == 0 else ()
        weight_ffn.append(fetch_pieces(feed_shard(h), held[h], *more))
        held.append(weight_ffn[-1][0][0])
    weight_ffn.append(fetch_paired(last_pair, held[-2]))

    select = (jnp.arange(slot_count, dtype=jnp.int32) == adapter_choice[0]).astype(BF)

    def adapter_of(adapter_table):
        return jnp.einsum(
            "a,ard->rd", select, adapter_table, preferred_element_type=F32
        ).astype(BF)

    down_qkv = own_first(
        jnp.concatenate(
            [adapter_of(query_down), adapter_of(key_down), adapter_of(value_down)], axis=0
        )
    )
    lift_query = adapter_of(query_up)
    lift_key = adapter_of(key_up)
    lift_value = adapter_of(value_up)
    down_output = adapter_of(output_down)
    lift_output = own_first(adapter_of(output_up))
    down_expand = own_first(adapter_of(expand_down))
    lift_expand = adapter_of(expand_up)
    down_shrink = adapter_of(shrink_down)
    lift_shrink = own_first(adapter_of(shrink_up))

    gain_a, shift_a = own_first(gain_one), own_first(shift_one)
    gain_b, shift_b = own_first(gain_two), own_first(shift_two)
    out_bias = own_first(output_bias)
    last_bias = own_first(shrink_bias)

    def normalize(values):
        row_mean = jnp.mean(values, axis=-1, keepdims=True)
        centred = values - row_mean
        row_var = jnp.mean(centred * centred, axis=-1, keepdims=True)
        scale = lax.rsqrt(row_var + 1e-05)
        return centred * scale, scale

    def norm_back(grad, gain, unit, scale):
        scaled = grad * gain
        return (
            scaled
            - jnp.mean(scaled, axis=-1, keepdims=True)
            - unit * jnp.mean(scaled * unit, axis=-1, keepdims=True)
        ) * scale

    inputs_wide = own_first(inputs).astype(F32)
    cot = own_first(cotangent)
    unit_one, scale_one = normalize(inputs_wide)
    rows_one = (unit_one * gain_a + shift_a).astype(BF)
    full_one = gather_rows(rows_one)
    full_cot = gather_rows(cot)
    seq_len = full_one.shape[0]
    head_count = width_local // HEAD_DIM

    rank_one = product_cols(full_one, down_qkv).astype(BF)
    rank_query = rank_one[:, :rank_width]
    rank_key = rank_one[:, rank_width : 2 * rank_width]
    rank_value = rank_one[:, 2 * rank_width :]
    query_key = into(after(full_one, weight_vo[0]), weight_qk, 0, 2 * width_local)
    queries = (query_key[:, :width_local] + product(rank_query, lift_query) + query_bias).astype(BF)
    keys_low = (query_key[:, width_local:] + product(rank_key, lift_key)).astype(BF)
    values_low = (
        into(after(full_one, held[2]), weight_vo, 0, width_local)
        + product(rank_value, lift_value)
        + value_bias
    ).astype(BF)
    seg_range = jnp.arange(SEGS, dtype=jnp.int32)
    seg_hot = (segment_ids[0][:, None] == seg_range[None, :]).astype(BF)
    path_hot = product(seg_hot, ancestry(parent_links[0]).astype(BF)).astype(BF)
    positions = jnp.arange(seq_len, dtype=jnp.int32)
    allowed = jnp.logical_and(
        product_cols(path_hot, seg_hot) > 0.5, positions[:, None] >= positions[None, :]
    )
    bias = jnp.where(allowed, 0.0, -1e30)
    turn = tensor_index.astype(jnp.int32).reshape(1)
    attended, level = by_head(
        attend_kernel,
        turn,
        [queries, keys_low, values_low],
        [bias],
        [BF, F32],
        [],
        (0, head_count),
        "attend",
    )
    attended = after(attended, weight_ffn[0][1][0])
    rank_out = product_cols(attended, down_output).astype(BF)
    main_rows = reduce_rows(
        beside(out_of(attended, weight_vo, width_local, 2 * width_local))
        + product(rank_out, lift_output)
    )
    main_rows = after(main_rows, weight_ffn[0][2][0], held[3])
    residual = inputs_wide + main_rows + out_bias
    unit_two, scale_two = normalize(residual)
    rows_two = (unit_two * gain_b + shift_b).astype(BF)
    full_two = after(gather_rows(rows_two, weight_ffn[1][1][0]), held[4])
    rank_two = product_cols(full_two, down_expand).astype(BF)
    rank_grad = product_cols(full_cot, lift_shrink).astype(BF)

    state = None
    down_parts, up_parts = [], []

    def feed(h, rows, span):
        last = h == chunk_count - 1
        results = feed_forward(
            rows,
            full_cot,
            rank_two,
            rank_grad,
            weight_ffn[h],
            lift_expand,
            expand_bias[h * chunk : (h + 1) * chunk],
            down_shrink,
            h,
            state,
            (lift_shrink, down_expand) if last else None,
            span,
        )
        return results[:4], results[4], results[5]

    for h in range(chunk_count - 1):
        state, down_part, up_part = feed(h, full_two, (0, seq_len))
        down_parts.append(down_part)
        up_parts.append(up_part)

    def far_part(two, three):
        return (two.astype(F32) + to_core(three).astype(F32)).astype(BF)

    def near_part(zero, one):
        return zero.astype(F32) + to_core(one).astype(F32)

    last = chunk_count - 1
    third, *third_deltas = feed(last, full_two, (3 * row_count, seq_len))
    second, *second_deltas = feed(
        last, after(full_two, third[1][0]), (2 * row_count, 3 * row_count)
    )
    grad_far = far_part(second[1][0], third[1][0])
    near, *near_deltas = feed(last, after(full_two, grad_far), (0, 2 * row_count))
    down_parts.append(third_deltas[0] + second_deltas[0] + near_deltas[0])
    up_parts.append(third_deltas[1] + second_deltas[1] + near_deltas[1])
    grad_rank_two = jnp.concatenate([near[3], second[3], third[3]], axis=0).astype(BF)
    rank_shrink = jnp.concatenate([near[2], second[2], third[2]], axis=0).astype(BF)
    far_arrived = to_chip(grad_far)
    grad_norm_two = near_part(near[1][0], after(near[1][1], far_arrived)) + far_arrived.astype(F32)
    grad_residual = cot.astype(F32) + norm_back(grad_norm_two, gain_b, unit_two, scale_two)
    grad_branch = grad_residual.astype(BF)

    branch_near = to_core(grad_branch)
    branch_far = to_chip(grad_branch)
    delta_shrink_up = product_rows(after(rank_shrink, grad_branch), full_cot)
    delta_expand_down = product_rows(after(grad_rank_two, grad_branch), full_two)
    main_far = far_part(after(second[0][0], grad_branch), after(third[0][0], grad_branch))
    main_near = near_part(*near[0])
    branch_held = after(branch_far, delta_shrink_up, delta_expand_down, main_far)
    full_branch = jnp.concatenate(
        [grad_branch, branch_near, branch_held, to_core(branch_held)], axis=0
    )
    rank_grad_out = product_cols(full_branch, lift_output).astype(BF)
    delta_output_up = product_rows(rank_out, full_branch)

    hot_lanes = (
        jnp.arange(128, dtype=jnp.int32)[None, :] == adapter_choice[0]
    ).astype(BF) * jnp.ones((rank_width, 1), BF)

    def by_tensor(parts):
        low = [jnp.where(core_odd, parts[1], parts[0]), jnp.where(core_odd, parts[0], parts[1])]
        high = [jnp.where(core_odd, parts[3], parts[2]), jnp.where(core_odd, parts[2], parts[3])]
        return [jnp.where(chip_odd, b, a) for a, b in zip(low + high, high + low)]

    quarter = feats // 4

    def settle_core(wide):
        stacked = natural(jnp.concatenate(wide, axis=0).astype(BF))
        parts = by_tensor([stacked[:, t * quarter : (t + 1) * quarter] for t in range(4)])
        near = to_core(jnp.concatenate([parts[1], parts[3]], axis=0))
        rows = stacked.shape[0]
        far = (parts[2].astype(F32) + near[rows:].astype(F32)).astype(BF)
        return parts[0], near[:rows], far

    def settle_flat(base, near, far, slim):
        parts = [base, near, to_chip(far), *slim, hot_lanes]
        rows = base.shape[0] // rank_width
        width = rows * quarter + sum(v.shape[1] for v in slim) + hot_lanes.shape[1]
        return pl.pallas_call(
            functools.partial(flat_kernel, rank_width),
            out_shape=jax.ShapeDtypeStruct((rank_width, width), BF),
            name="flatten",
        )(*parts)

    def settle_pair(flat):
        return jnp.concatenate([flat, lax.ppermute(flat, "dp", dp_pairs)], axis=0)

    def settle_line(pair):
        return [pair] + [
            lax.ppermute(pair, "dp", [(i, (i + 2 * s) % dp_size) for i in range(dp_size)])
            for s in range(1, pair_count)
        ]

    def settle_across(own, count):
        away = to_chip(own)
        across = by_tensor([own, to_core(own), away, to_core(away)])
        return [
            jnp.concatenate(
                [piece[:, :, k * quarter : (k + 1) * quarter] for piece in across], axis=-1
            ).astype(F32)
            for k in range(count)
        ]

    early_parts = settle_core([delta_shrink_up, delta_expand_down, delta_output_up])
    grad_attended = (
        into(after(full_branch, early_parts[0]), weight_vo, width_local, 2 * width_local)
        + product(rank_grad_out, down_output)
    ).astype(BF)
    delta_output_down = product_rows(rank_grad_out, attended)
    main_arrived = to_chip(after(main_far, early_parts[2], branch_far))

    def attend_back(grad, heads, before=()):
        return by_head(
            attend_back_kernel,
            turn,
            [queries, keys_low, values_low, grad],
            [bias, level],
            [BF, BF, BF],
            [pltpu.VMEM((seq_len, HEAD_DIM), F32)] * 2,
            heads,
            "attend_back",
            before,
        )

    grads = attend_back(after(grad_attended, early_parts[2]), (0, 1))
    early_flat = settle_flat(
        after(early_parts[0], grads[0]),
        *early_parts[1:],
        [*down_parts, *up_parts, delta_output_down],
    )
    early_pair = settle_pair(early_flat)
    grads = attend_back(after(grad_attended, early_flat), (1, 1), grads)
    early_trees = settle_line(after(early_pair, grads[0]))
    grads = attend_back(after(grad_attended, early_pair), (2, head_count - 2), grads)
    *grads, main_arrived = lax.optimization_barrier((*grads, main_arrived))
    grad_query_low, grad_key_low, grad_value_low = grads
    grad_rank_one = jnp.concatenate(
        [
            product_cols(grad_query_low, lift_query),
            product_cols(grad_key_low, lift_key),
            product_cols(grad_value_low, lift_value),
        ],
        axis=1,
    ).astype(BF)
    delta_qkv_down = product_rows(grad_rank_one, full_one)
    delta_query_up = product_rows(rank_query, grad_query_low)
    delta_key_up = product_rows(rank_key, grad_key_low)
    delta_value_up = product_rows(rank_value, grad_value_low)
    late_parts = settle_core(
        [
            delta_qkv_down[:rank_width],
            delta_qkv_down[rank_width : 2 * rank_width],
            delta_qkv_down[2 * rank_width :],
        ]
    )
    late_flat = settle_flat(*late_parts, [delta_query_up, delta_key_up, delta_value_up])
    def rows_back(first, *held):
        rank = after(grad_rank_one, *held) if held else grad_rank_one
        return back_rows(
            [grad_query_low, grad_key_low, grad_value_low, rank],
            weight_qk,
            weight_vo,
            down_qkv,
            row_count,
            first,
        )

    back_third, back_second = rows_back(3, late_parts[2])
    back_far = far_part(back_second, back_third)
    late_pair = settle_pair(late_flat)
    early_own, shrink_down_out, expand_up_out, output_down_out = sum_slots(
        [after(early_trees[0], late_flat), *early_trees[1:]],
        slot_count,
        rank_width,
        3 * quarter,
        [hidden_local, hidden_local, width_local],
    )
    late_trees = settle_line(after(late_pair, early_own))
    back_first, back_zero = rows_back(1, back_far, late_pair, early_own)
    back_arrived = to_chip(back_far)
    early_own = after(early_own, back_zero)
    shrink_up_out, expand_down_out, output_up_out = settle_across(early_own, 3)
    main_rows_two = main_near + main_arrived.astype(F32)
    output = natural((residual + main_rows_two + last_bias).astype(BF))
    grad_norm_one = near_part(back_zero, after(back_first, back_arrived)) + back_arrived.astype(F32)
    input_delta = natural(
        (grad_residual + norm_back(grad_norm_one, gain_a, unit_one, scale_one)).astype(BF)
    )
    late_own, query_up_out, key_up_out, value_up_out = sum_slots(
        [after(late_trees[0], back_arrived, shrink_up_out), *late_trees[1:]],
        slot_count,
        rank_width,
        3 * quarter,
        [width_local] * 3,
    )
    query_down_out, key_down_out, value_down_out = settle_across(late_own, 3)
    return (
        output,
        input_delta,
        query_down_out,
        query_up_out,
        key_down_out,
        key_up_out,
        value_down_out,
        value_up_out,
        output_down_out,
        output_up_out,
        expand_down_out,
        expand_up_out,
        shrink_down_out,
        shrink_up_out,
    )


def solution(mesh):
    rows = P(("dp", "tensor"), None)
    tree = P("dp", None)
    whole = P()
    slim = P(None, None, "tensor")
    inward = P("dp", "tensor")
    outward = P("tensor", "dp")
    return jax.shard_map(
        functools.partial(shards, mesh.shape["dp"]),
        mesh=mesh,
        in_specs=(
            rows,
            rows,
            tree,
            tree,
            P("dp"),
            whole,
            whole,
            whole,
            whole,
            inward,
            inward,
            inward,
            outward,
            inward,
            outward,
            P("tensor"),
            P("tensor"),
            whole,
            P("tensor"),
            whole,
            whole,
            slim,
            whole,
            slim,
            whole,
            slim,
            slim,
            whole,
            whole,
            slim,
            slim,
            whole,
        ),
        out_specs=(
            rows,
            rows,
            whole,
            slim,
            whole,
            slim,
            whole,
            slim,
            slim,
            whole,
            whole,
            slim,
            slim,
            whole,
        ),
        check_vma=False,
    )
```

```python
import functools

import jax
import jax.numpy as jnp
from jax import lax
from jax.experimental import pallas as pl
from jax.experimental.pallas import tpu as pltpu
from jax.sharding import PartitionSpec as P

HEAD_DIM = 128
SEGS = 13
BF = jnp.bfloat16
F32 = jnp.float32


def ancestry(parents):
    seg_range = jnp.arange(SEGS, dtype=jnp.int32)
    current = seg_range
    ancestors = current[:, None] == seg_range[None, :]
    for hop_index in range(SEGS - 1):
        current = jnp.sum(
            jnp.where(current[:, None] == seg_range[None, :], parents[None, :], 0), axis=1
        )
        ancestors = jnp.logical_or(ancestors, current[:, None] == seg_range[None, :])
    return ancestors


def product(left, right):
    return jnp.dot(left, right, preferred_element_type=F32)


def product_cols(left, right):
    return lax.dot_general(
        left, right, (((1,), (1,)), ((), ())), preferred_element_type=F32
    )


def product_rows(left, right):
    return lax.dot_general(
        left, right, (((0,), (0,)), ((), ())), preferred_element_type=F32
    )


def feed_kernel(first, last, pieces, *refs):
    rows, cots, rank_in, rank_grad, lift, bias, down = refs[:7]
    weights, refs = refs[7 : 7 + pieces], refs[7 + pieces :]
    if not first:
        main_in, grad_in, rank_main_in, rank_back_in = refs[:4]
        refs = refs[4:]
    if last:
        lift_after, down_before = refs[:2]
        refs = refs[2:]
    mains, grads = refs[: len(refs) // 2 - 2], refs[len(refs) // 2 - 2 : -4]
    rank_main, rank_back, down_delta, up_delta = refs[-4:]
    chunk = lift.shape[1]
    parts, at = [], 0
    for weight in weights:
        parts.append((slice(at, at + weight.shape[0]), weight))
        at += weight.shape[0]

    pre_act = (
        sum(product(rows[:, here], weight[:, :chunk]) for here, weight in parts)
        + product(rank_in[...], lift[...])
        + bias[...]
    )
    grad_hidden = sum(
        product(cots[:, here], weight[:, chunk:]) for here, weight in parts
    ) + product(rank_grad[...], down[...])
    bell = 0.5 * (1.0 + lax.erf(pre_act * (0.5**0.5)))
    slope = bell + pre_act * jnp.exp(-0.5 * pre_act * pre_act) * (0.5 / jnp.pi) ** 0.5
    hidden = (pre_act * bell).astype(BF)
    grad_pre = (grad_hidden * slope).astype(BF)

    main_rank = product_cols(hidden, down[...])
    back_rank = product_cols(grad_pre, lift[...])
    if not first:
        main_rank = main_rank + rank_main_in[...]
        back_rank = back_rank + rank_back_in[...]
    rank_main[...] = main_rank
    rank_back[...] = back_rank
    for here, weight in parts:
        ahead = product_cols(hidden, weight[:, chunk:])
        back = product_cols(grad_pre, weight[:, :chunk])
        if not first:
            ahead = ahead + main_in[:, here]
            back = back + grad_in[:, here]
        if last:
            ahead = ahead + product(main_rank.astype(BF), lift_after[:, here])
            back = back + product(back_rank.astype(BF), down_before[:, here])
        for k, (main, grad) in enumerate(zip(mains, grads)):

            @pl.when((pl.program_id(0) == k) | (len(mains) == 1))
            def _(main=main, grad=grad, here=here, ahead=ahead, back=back):
                main[:, here] = ahead.astype(main.dtype)
                grad[:, here] = back.astype(grad.dtype)

    down_part = product_rows(rank_grad[...], hidden)
    up_part = product_rows(rank_in[...], grad_pre)

    @pl.when(pl.program_id(0) == 0)
    def _():
        down_delta[...] = down_part
        up_delta[...] = up_part

    @pl.when(pl.program_id(0) > 0)
    def _():
        down_delta[...] += down_part
        up_delta[...] += up_part


def feed_forward(rows, cots, rank_in, rank_grad, weight, lift, bias, down, at, before, final, span):
    tile = 256
    feats = rows.shape[1]
    chunk = bias.shape[0]
    rank = lift.shape[0]
    begin, count = span[0] // tile, (span[1] - span[0]) // tile
    first, last = before is None, final is not None

    def row_block(width):
        return pl.BlockSpec((tile, width), lambda i: (begin + i, 0))

    def out_block(width):
        return pl.BlockSpec((tile, width), lambda i: (i, 0))

    def fixed(shape, column=0):
        return pl.BlockSpec(shape, lambda i: (0, column), pipeline_mode=pl.Buffered(1))

    args = [rows, cots, rank_in, rank_grad, lift, bias[None], down]
    specs = [
        row_block(feats),
        row_block(feats),
        row_block(rank),
        row_block(rank),
        fixed((rank, chunk), at),
        fixed((1, chunk), 0),
        fixed((rank, chunk), at),
    ]
    for piece, column in weight:
        args.append(piece)
        specs.append(fixed((piece.shape[0], 2 * chunk), column))
    if not first:
        args += [before[0][0], before[1][0], before[2], before[3]]
        specs += [row_block(feats), row_block(feats), row_block(rank), row_block(rank)]
    if last:
        args += list(final)
        specs += [fixed((rank, feats)), fixed((rank, feats))]
    size = span[1] - span[0]
    flops = size * feats * chunk
    if last:
        wide_specs = [fixed((tile, feats))] * (2 * count)
        wide_shapes = [jax.ShapeDtypeStruct((tile, feats), BF)] * (2 * count)
    else:
        wide_specs = [out_block(feats)] * 2
        wide_shapes = [jax.ShapeDtypeStruct((size, feats), F32)] * 2
    results = pl.pallas_call(
        functools.partial(feed_kernel, first, last, len(weight)),
        grid=(count,),
        in_specs=specs,
        out_specs=wide_specs
        + [
            out_block(rank),
            out_block(rank),
            pl.BlockSpec((rank, chunk), lambda i: (0, 0)),
            pl.BlockSpec((rank, chunk), lambda i: (0, 0)),
        ],
        out_shape=wide_shapes
        + [
            jax.ShapeDtypeStruct((size, rank), F32),
            jax.ShapeDtypeStruct((size, rank), F32),
            jax.ShapeDtypeStruct((rank, chunk), F32),
            jax.ShapeDtypeStruct((rank, chunk), F32),
        ],
        cost_estimate=pl.CostEstimate(
            flops=flops, bytes_accessed=size * feats * 20, transcendentals=size * chunk * 2
        ),
        name="feed_forward",
    )(*args)
    wide = len(wide_specs) // 2
    return results[:wide], results[wide : 2 * wide], *results[2 * wide :]


def attend_kernel(scale, turn, *refs):
    count = (len(refs) - 3) // 3
    query, key, value = refs[:count], refs[count : 2 * count], refs[2 * count : 3 * count]
    bias, attended, level = refs[3 * count :]
    rows = query[0].shape[0]
    for i in range(count):
        here = slice(i * rows, (i + 1) * rows)
        scores = [
            product_cols(query[i][...], key[j][...]) * scale
            + bias[here, j * rows : (j + 1) * rows]
            for j in range(i + 1)
        ]
        top = functools.reduce(
            jnp.maximum, [jnp.max(v, axis=-1, keepdims=True) for v in scores]
        )
        raised = [jnp.exp(v - top) for v in scores]
        total = sum(jnp.sum(v, axis=-1, keepdims=True) for v in raised)
        share = 1.0 / total
        mixed = sum(
            product((v * share).astype(BF), value[j][...]) for j, v in enumerate(raised)
        )
        to = pl.multiple_of((i ^ turn[0]) * rows, rows)
        attended[pl.ds(to, rows), :] = mixed.astype(BF)
        level[here, :] = jnp.broadcast_to(top + jnp.log(total), (rows, level.shape[1]))


def attend_back_kernel(scale, turn, *refs):
    count = (len(refs) - 7) // 4
    query, key, value, grad = (refs[n * count : (n + 1) * count] for n in range(4))
    bias, level = refs[4 * count : 4 * count + 2]
    grad_query, grad_key, grad_value, key_sum, value_sum = refs[-5:]
    rows = query[0].shape[0]
    for i in range(count):
        here = slice(i * rows, (i + 1) * rows)
        row_level = level[here, :1]
        probs = [
            jnp.exp(
                product_cols(query[i][...], key[j][...]) * scale
                + bias[here, j * rows : (j + 1) * rows]
                - row_level
            )
            for j in range(i + 1)
        ]
        grad_probs = [product_cols(grad[i][...], value[j][...]) for j in range(i + 1)]
        mean = sum(
            jnp.sum(p * g, axis=-1, keepdims=True) for p, g in zip(probs, grad_probs)
        )
        query_sum = 0.0
        for j in range(i + 1):
            there = slice(j * rows, (j + 1) * rows)
            grad_score = (probs[j] * (grad_probs[j] - mean)).astype(BF)
            query_sum = query_sum + product(grad_score, key[j][...])
            key_part = product_rows(grad_score, query[i][...])
            value_part = product_rows(probs[j].astype(BF), grad[i][...])
            if i > j:
                key_part = key_part + key_sum[there, :]
                value_part = value_part + value_sum[there, :]
            key_sum[there, :] = key_part
            value_sum[there, :] = value_part
        to = pl.multiple_of((i ^ turn[0]) * rows, rows)
        grad_query[pl.ds(to, rows), :] = (query_sum * scale).astype(BF)
    for j in range(count):
        there = slice(j * rows, (j + 1) * rows)
        to = pl.multiple_of((j ^ turn[0]) * rows, rows)
        grad_key[pl.ds(to, rows), :] = (key_sum[there, :] * scale).astype(BF)
        grad_value[pl.ds(to, rows), :] = value_sum[there, :].astype(BF)


def by_head(kernel, turn, blocked, whole, outs, scratch, heads, name, before=()):
    first, count = heads
    seq_len, width = blocked[0].shape
    blocks = 4
    rows = seq_len // blocks
    specs, args = [], []
    for v in blocked:
        for k in range(blocks):
            specs.append(
                pl.BlockSpec((rows, HEAD_DIM), lambda h, turn, k=k: (k ^ turn[0], first + h))
            )
            args.append(v)
    for v in whole:
        if v.shape[1] == seq_len:
            specs.append(
                pl.BlockSpec(v.shape, lambda h, turn: (0, 0), pipeline_mode=pl.Buffered(1))
            )
        else:
            specs.append(pl.BlockSpec((seq_len, HEAD_DIM), lambda h, turn: (0, first + h)))
        args.append(v)
    aliases = {1 + len(args) + n: n for n in range(len(before))}
    specs += [pl.BlockSpec(memory_space=pl.ANY)] * len(before)
    args += before
    return pl.pallas_call(
        functools.partial(kernel, HEAD_DIM ** (-0.5)),
        grid_spec=pltpu.PrefetchScalarGridSpec(
            num_scalar_prefetch=1,
            grid=(count,),
            in_specs=specs,
            out_specs=[pl.BlockSpec((seq_len, HEAD_DIM), lambda h, turn: (0, first + h))] * len(outs),
            scratch_shapes=scratch,
        ),
        out_shape=[jax.ShapeDtypeStruct((seq_len, width), t) for t in outs],
        input_output_aliases=aliases,
        cost_estimate=pl.CostEstimate(flops=10**8, bytes_accessed=10**6, transcendentals=0),
        name=name,
    )(turn, *args)


def branch_kernel(zero, one, far, base, unit, scale, gain, wide, low):
    unit_rows = unit[...]
    scaled = (
        zero[...].astype(F32) + one[...].astype(F32) + far[...].astype(F32)
    ) * gain[...]
    total = base[...].astype(F32) + scale[...] * (
        scaled
        - jnp.mean(scaled, axis=-1, keepdims=True)
        - unit_rows * jnp.mean(scaled * unit_rows, axis=-1, keepdims=True)
    )
    wide[...] = total
    low[...] = total.astype(BF)


def branch_rows(zero, one, far, base, unit, scale, gain):
    rows, feats = unit.shape
    tile = rows // 4
    wide = pl.BlockSpec((tile, feats), lambda i: (i, 0))
    return pl.pallas_call(
        branch_kernel,
        grid=(rows // tile,),
        in_specs=[wide] * 5
        + [pl.BlockSpec((tile, 1), lambda i: (i, 0)), pl.BlockSpec((1, feats), lambda i: (0, 0))],
        out_specs=[wide, wide],
        out_shape=[
            jax.ShapeDtypeStruct((rows, feats), F32),
            jax.ShapeDtypeStruct((rows, feats), BF),
        ],
        cost_estimate=pl.CostEstimate(flops=10**7, bytes_accessed=10**6, transcendentals=0),
        name="branch_rows",
    )(zero, one, far, base, unit, scale, gain[None])


def back_kernel(query, key, value, rank, qk_own, qk_other, vo_own, vo_other, down, *outs):
    width = query.shape[1]
    half = qk_own.shape[0]
    for at, qk, vo in ((0, qk_own, vo_own), (half, qk_other, vo_other)):
        rows = (
            product_cols(query[...], qk[:, :width])
            + product_cols(key[...], qk[:, width:])
            + product_cols(value[...], vo[...])
            + product(rank[...], down[:, at : at + half])
        ).astype(BF)
        for k, out in enumerate(outs):

            @pl.when(pl.program_id(0) == k)
            def _(out=out, rows=rows, at=at):
                out[:, at : at + half] = rows


def out_kernel(rows, down, lift, own, other, *outs):
    half = own.shape[0]
    rank = product_cols(rows[...], down[...]).astype(BF)
    for at, weight in ((0, own), (half, other)):
        here = slice(at, at + half)
        mixed = product_cols(rows[...], weight[...]) + product(rank, lift[:, here])
        for k, out in enumerate(outs):

            @pl.when(pl.program_id(0) == k)
            def _(out=out, mixed=mixed, here=here):
                out[:, here] = mixed.astype(BF)


def out_rows(rows, down, lift, weight, tile, first, count):
    half, width = weight[0].shape[0], rows.shape[1]

    def fixed(shape, column=0):
        return pl.BlockSpec(shape, lambda i: (0, column), pipeline_mode=pl.Buffered(1))

    return pl.pallas_call(
        out_kernel,
        grid=(count,),
        in_specs=[pl.BlockSpec((tile, width), lambda i: (first - i, 0))]
        + [fixed(down.shape), fixed(lift.shape)]
        + [fixed((half, width), 1)] * 2,
        out_specs=[fixed((tile, lift.shape[1]))] * count,
        out_shape=[jax.ShapeDtypeStruct((tile, lift.shape[1]), BF)] * count,
        cost_estimate=pl.CostEstimate(flops=10**7, bytes_accessed=10**5, transcendentals=0),
        name="out_rows",
    )(rows, down, lift, *weight[:2])


def back_rows(grads, weight_qk, weight_vo, down, tile, first, count):
    half, width = weight_vo[0].shape[0], grads[0].shape[1]

    def fixed(shape):
        return pl.BlockSpec(shape, lambda i: (0, 0), pipeline_mode=pl.Buffered(1))

    return pl.pallas_call(
        back_kernel,
        grid=(count,),
        in_specs=[pl.BlockSpec((tile, v.shape[1]), lambda i: (first - i, 0)) for v in grads]
        + [fixed((half, 2 * width))] * 2
        + [fixed((half, width))] * 2
        + [fixed(down.shape)],
        out_specs=[fixed((tile, down.shape[1]))] * count,
        out_shape=[jax.ShapeDtypeStruct((tile, down.shape[1]), BF)] * count,
        cost_estimate=pl.CostEstimate(flops=10**8, bytes_accessed=10**6, transcendentals=0),
        name="back_rows",
    )(*grads, *weight_qk[:2], *weight_vo[:2], down)


def by_place(place, parts):
    core_odd, chip_odd = place[1] % 2 == 1, place[1] // 2 == 1
    low = [jnp.where(core_odd, parts[1], parts[0]), jnp.where(core_odd, parts[0], parts[1])]
    high = [jnp.where(core_odd, parts[3], parts[2]), jnp.where(core_odd, parts[2], parts[3])]
    return [jnp.where(chip_odd, b, a) for a, b in zip(low + high, high + low)]


def in_order(place, blocks, values):
    size = values.shape[1] // blocks
    parts = [values[:, k * size : (k + 1) * size] for k in range(blocks)]
    ordered = []
    for own, other in zip(parts[: blocks // 2], parts[blocks // 2 :]):
        ordered.append(jnp.where(place[0] == 1, other, own))
        ordered.append(jnp.where(place[0] == 1, own, other))
    return jnp.concatenate(ordered, axis=1)


def pack(place, blocks, wide, base, send, far):
    total = base.shape[0]
    for k, values in enumerate(wide):
        ordered = in_order(place, blocks, values)
        size = ordered.shape[1] // 4
        parts = by_place(place, [ordered[:, t * size : (t + 1) * size] for t in range(4)])
        at, rows = k * values.shape[0], values.shape[0]
        base[at : at + rows] = parts[0].astype(BF)
        send[at : at + rows] = parts[1].astype(BF)
        send[total + at : total + at + rows] = parts[3].astype(BF)
        far[at : at + rows] = parts[2].astype(BF)


def pack_kernel(blocks, place, *refs):
    *wide, rank, first, second, base, send, far = refs
    tile = first.shape[0]
    wide = [ref[...] for ref in wide]
    wide[-1] = (
        wide[-1] + product_rows(rank[:tile], first[...]) + product_rows(rank[tile:], second[...])
    )
    pack(place, blocks, wide, base, send, far)


def in_kernel(first, second, lift, down, own, other, grad, rank):
    half, tile = own.shape[0], first.shape[0]
    for k, rows in enumerate((first, second)):
        here = slice(k * tile, (k + 1) * tile)
        ranks = product_cols(rows[...], lift[...]).astype(BF)
        rank[here, :] = ranks
        grad[here, :] = (
            product(rows[:, :half], own[...])
            + product(rows[:, half:], other[...])
            + product(ranks, down[...])
        ).astype(BF)


def in_rows(first, second, lift, down, weight):
    half, width = weight[0].shape[0], down.shape[1]
    rows = 2 * first.shape[0]
    whole = [pl.BlockSpec(v.shape, lambda i: (0, 0)) for v in (first, second, lift, down)]
    return pl.pallas_call(
        in_kernel,
        grid=(1,),
        in_specs=whole + [pl.BlockSpec((half, width), lambda i: (0, 1))] * 2,
        out_specs=[
            pl.BlockSpec((rows, width), lambda i: (0, 0)),
            pl.BlockSpec((rows, lift.shape[0]), lambda i: (0, 0)),
        ],
        out_shape=[
            jax.ShapeDtypeStruct((rows, width), BF),
            jax.ShapeDtypeStruct((rows, lift.shape[0]), BF),
        ],
        cost_estimate=pl.CostEstimate(flops=10**7, bytes_accessed=10**5, transcendentals=0),
        name="in_rows",
    )(first, second, lift, down, *weight[:2])


def late_kernel(blocks, place, *refs):
    grads, lifts, rows, ranks = refs[:3], refs[3:6], refs[6], refs[7]
    rank_grad, base, send, far, *ups = refs[8:]
    width = lifts[0].shape[0]
    wide = []
    for k, (grad, lift, up) in enumerate(zip(grads, lifts, ups)):
        here = slice(k * width, (k + 1) * width)
        rank = product_cols(grad[...], lift[...]).astype(BF)
        rank_grad[:, here] = rank
        wide.append(product_rows(rank, rows[...]))
        up[...] = product_rows(ranks[:, here], grad[...])
    pack(place, blocks, wide, base, send, far)


def across_kernel(place, *refs):
    parts, outs = refs[:4], refs[4:]
    size = parts[0].shape[1] // len(outs)
    for k, out in enumerate(outs):
        here = slice(k * size, (k + 1) * size)
        for t, part in enumerate(by_place(place, [v[:, here].astype(F32) for v in parts])):
            out[:, t * size : (t + 1) * size] = part


def output_kernel(blocks, place, zero, one, far, base, bias, out):
    total = base[...] + bias[...] + zero[...].astype(F32)
    total = total + one[...].astype(F32) + far[...].astype(F32)
    out[...] = in_order(place, blocks, total).astype(BF)


def local_call(kernel, name, place, args, shapes, tile=None):
    specs = [pl.BlockSpec(memory_space=pltpu.SMEM)]
    options = {}
    if tile is None:
        specs += [pl.BlockSpec(memory_space=pltpu.VMEM) for _ in args]
        out_specs = [pl.BlockSpec(memory_space=pltpu.VMEM) for _ in shapes]
    else:
        rows = shapes[0][0][0]

        def spec(shape):
            if shape[0] == rows:
                return pl.BlockSpec((tile, shape[1]), lambda i: (i, 0))
            return pl.BlockSpec(shape, lambda i: (0, 0))

        options = {"grid": (rows // tile,)}
        specs += [spec(v.shape) for v in args]
        out_specs = [spec(shape) for shape, _ in shapes]
    return pl.pallas_call(
        kernel,
        in_specs=specs,
        out_specs=out_specs,
        out_shape=[jax.ShapeDtypeStruct(shape, kind) for shape, kind in shapes],
        cost_estimate=pl.CostEstimate(flops=10**6, bytes_accessed=10**5, transcendentals=0),
        name=name,
        **options,
    )(place, *args)


def flat_kernel(rank, *refs):
    base, near, far, *slim, marks, out = refs
    mine = (
        base[...].astype(F32) + near[...].astype(F32) + far[...].astype(F32)
    ).astype(BF)
    width = mine.shape[1]
    at = 0
    for k in range(mine.shape[0] // rank):
        out[:, at : at + width] = mine[k * rank : (k + 1) * rank]
        at += width
    for part in slim:
        out[:, at : at + part.shape[1]] = part[...].astype(BF)
        at += part.shape[1]
    out[:, at:] = marks[...]


def slots_kernel(slot_count, rank, *refs):
    tree_count = len(refs) - 4
    trees = jnp.concatenate([ref[...] for ref in refs[:tree_count]], axis=0)
    lanes = slot_count * rank
    width = trees.shape[1] - lanes
    source = lax.broadcasted_iota(jnp.int32, (lanes, lanes), 0)
    target = lax.broadcasted_iota(jnp.int32, (lanes, lanes), 1)
    spread = jnp.where(source == target // rank, 1.0, 0.0).astype(BF)
    marks = product(trees[:, width:], spread)
    row = lax.broadcasted_iota(jnp.int32, marks.shape, 0)
    lane = lax.broadcasted_iota(jnp.int32, marks.shape, 1)
    marks = jnp.where(row % rank == lane % rank, marks, 0.0).astype(BF)
    at = 0
    for out in refs[tree_count:]:
        size = out.shape[1]
        out[...] = product_rows(marks, trees[:, at : at + size]).astype(out.dtype)
        at += size


def sum_slots(trees, slot_count, rank, wide, slim):
    rows = slot_count * rank
    wide_sum, *slim_sums = pl.pallas_call(
        functools.partial(slots_kernel, slot_count, rank),
        out_shape=[jax.ShapeDtypeStruct((rows, wide), BF)]
        + [jax.ShapeDtypeStruct((rows, n), F32) for n in slim],
        cost_estimate=pl.CostEstimate(flops=10**6, bytes_accessed=10**5, transcendentals=0),
        name="sum_slots",
    )(*trees)
    return [v.reshape(slot_count, rank, -1) for v in (wide_sum, *slim_sums)]


def shards(
    dp_size,
    inputs,
    cotangent,
    segment_ids,
    parent_links,
    adapter_choice,
    gain_one,
    shift_one,
    gain_two,
    shift_two,
    query_weight,
    key_weight,
    value_weight,
    output_weight,
    expand_weight,
    shrink_weight,
    query_bias,
    value_bias,
    output_bias,
    expand_bias,
    shrink_bias,
    query_down,
    query_up,
    key_down,
    key_up,
    value_down,
    value_up,
    output_down,
    output_up,
    expand_down,
    expand_up,
    shrink_down,
    shrink_up,
):
    slot_count = query_down.shape[0]
    rank_width = query_down.shape[1]
    feats = inputs.shape[1]
    row_count = inputs.shape[0]
    width_local = query_weight.shape[1]
    hidden_local = expand_weight.shape[1]
    pair_count = dp_size // 2
    block = feats // dp_size
    half = feats // 2

    tensor_index = lax.axis_index("tensor")
    core_odd = (tensor_index % 2) == 1
    chip_odd = (tensor_index // 2) == 1
    dp_odd = (lax.axis_index("dp") % 2) == 1

    core_pairs = [(0, 1), (1, 0), (2, 3), (3, 2)]
    chip_pairs = [(0, 2), (2, 0), (1, 3), (3, 1)]
    dp_pairs = [(i, i ^ 1) for i in range(dp_size)]
    line_groups = [list(range(0, dp_size, 2)), list(range(1, dp_size, 2))]

    def to_core(v):
        return lax.ppermute(v, "tensor", core_pairs)

    def to_chip(v):
        return lax.ppermute(v, "tensor", chip_pairs)

    def own_first(v):
        parts = [v[..., b * block : (b + 1) * block] for b in range(dp_size)]
        pairs = [(parts[2 * p], parts[2 * p + 1]) for p in range(pair_count)]
        return jnp.concatenate(
            [jnp.where(dp_odd, odd, even) for even, odd in pairs]
            + [jnp.where(dp_odd, even, odd) for even, odd in pairs],
            axis=-1,
        )

    def natural(v):
        parts = [v[..., b * block : (b + 1) * block] for b in range(dp_size)]
        pairs = [(parts[p], parts[pair_count + p]) for p in range(pair_count)]
        return jnp.concatenate(
            [
                jnp.where(dp_odd, a, b)
                for own, other in pairs
                for a, b in ((other, own), (own, other))
            ],
            axis=-1,
        )

    def after(value, *others):
        return lax.optimization_barrier((value,) + others)[0]

    def gather_rows(rows, *held):
        near = to_core(rows)
        far = to_chip(rows)
        if held:
            far = after(far, *held)
        far_near = to_core(far)
        return jnp.concatenate([rows, near, far, far_near], axis=0)

    def line_gather(shard, held):
        if held:
            shard = after(shard, *held)
        return lax.all_gather(shard, "dp", axis=0, tiled=True, axis_index_groups=line_groups)

    def fetch(shard, *held):
        own = line_gather(shard, held)
        return own, lax.ppermute(own, "dp", dp_pairs), 0

    def fetch_pieces(shard, parts, *held):
        own = line_gather(shard, held)
        size = own.shape[0] // parts
        swapped = [
            lax.ppermute(own[k * size : (k + 1) * size], "dp", dp_pairs) for k in range(parts)
        ]
        return [(v, 0) for v in (own, *swapped)]

    def fetch_paired(pair, *held):
        both = line_gather(pair, held)
        return [(both, 0), (both, 1)]

    def into(left, weight, first, last):
        own, other, skip = weight
        return product(left[:, :half], own[:, first:last]) + product(
            left[:, half:], other[:, skip + first : skip + last]
        )

    def out_of(left, weight, first, last, base=None):
        own, other, skip = weight
        near = product_cols(left, own[:, first:last])
        far = product_cols(left, other[:, skip + first : skip + last])
        if base is not None:
            near, far = base[0] + near, base[1] + far
        return near, far

    def beside(pair):
        return jnp.concatenate(pair, axis=1)

    chunk_count = 4
    chunk = hidden_local // chunk_count
    output_turned = output_weight.T
    shrink_turned = shrink_weight.T
    def feed_shard(h):
        return jnp.concatenate(
            [
                expand_weight[:, h * chunk : (h + 1) * chunk],
                shrink_turned[:, h * chunk : (h + 1) * chunk],
            ],
            axis=1,
        )

    last_shard = feed_shard(chunk_count - 1)
    last_pair = jnp.concatenate([last_shard, lax.ppermute(last_shard, "dp", dp_pairs)], axis=1)
    weight_qk = fetch(jnp.concatenate([query_weight, key_weight], axis=1))
    weight_vo = fetch(jnp.concatenate([value_weight, output_turned], axis=1))
    weight_ffn, held = [], [weight_qk[0], weight_vo[0]]
    for h in range(chunk_count - 1):
        more = (last_pair,) if h == 0 else ()
        weight_ffn.append(fetch_pieces(feed_shard(h), 2 if h == 1 else 1, held[h], *more))
        held.append(weight_ffn[-1][0][0])
    weight_ffn.append(fetch_paired(last_pair, held[-2]))

    select = (jnp.arange(slot_count, dtype=jnp.int32) == adapter_choice[0]).astype(BF)

    def adapter_of(adapter_table):
        return jnp.einsum(
            "a,ard->rd", select, adapter_table, preferred_element_type=F32
        ).astype(BF)

    down_qkv = own_first(
        jnp.concatenate(
            [adapter_of(query_down), adapter_of(key_down), adapter_of(value_down)], axis=0
        )
    )
    lift_query = adapter_of(query_up)
    lift_key = adapter_of(key_up)
    lift_value = adapter_of(value_up)
    down_output = adapter_of(output_down)
    lift_output = own_first(adapter_of(output_up))
    down_expand = own_first(adapter_of(expand_down))
    lift_expand = adapter_of(expand_up)
    down_shrink = adapter_of(shrink_down)
    lift_shrink = own_first(adapter_of(shrink_up))

    gain_a, shift_a = own_first(gain_one), own_first(shift_one)
    gain_b, shift_b = own_first(gain_two), own_first(shift_two)
    out_bias = own_first(output_bias)
    last_bias = own_first(shrink_bias)

    def normalize(values):
        row_mean = jnp.mean(values, axis=-1, keepdims=True)
        centred = values - row_mean
        row_var = jnp.mean(centred * centred, axis=-1, keepdims=True)
        scale = lax.rsqrt(row_var + 1e-05)
        return centred * scale, scale

    def norm_back(grad, gain, unit, scale):
        scaled = grad * gain
        return (
            scaled
            - jnp.mean(scaled, axis=-1, keepdims=True)
            - unit * jnp.mean(scaled * unit, axis=-1, keepdims=True)
        ) * scale

    inputs_wide = own_first(inputs).astype(F32)
    cot = own_first(cotangent)
    unit_one, scale_one = normalize(inputs_wide)
    rows_one = (unit_one * gain_a + shift_a).astype(BF)
    full_one = gather_rows(rows_one, gain_b, shift_b, out_bias, last_bias)
    full_cot = gather_rows(cot)
    seq_len = full_one.shape[0]
    head_count = width_local // HEAD_DIM

    rank_one = product_cols(full_one, down_qkv).astype(BF)
    rank_query = rank_one[:, :rank_width]
    rank_key = rank_one[:, rank_width : 2 * rank_width]
    rank_value = rank_one[:, 2 * rank_width :]
    query_key = into(after(full_one, weight_vo[0]), weight_qk, 0, 2 * width_local)
    queries = (query_key[:, :width_local] + product(rank_query, lift_query) + query_bias).astype(BF)
    keys_low = (query_key[:, width_local:] + product(rank_key, lift_key)).astype(BF)
    values_low = (
        into(after(full_one, held[2]), weight_vo, 0, width_local)
        + product(rank_value, lift_value)
        + value_bias
    ).astype(BF)
    seg_range = jnp.arange(SEGS, dtype=jnp.int32)
    seg_hot = (segment_ids[0][:, None] == seg_range[None, :]).astype(BF)
    path_hot = product(seg_hot, ancestry(parent_links[0]).astype(BF)).astype(BF)
    positions = jnp.arange(seq_len, dtype=jnp.int32)
    allowed = jnp.logical_and(
        product_cols(path_hot, seg_hot) > 0.5, positions[:, None] >= positions[None, :]
    )
    bias = jnp.where(allowed, 0.0, -1e30)
    turn = tensor_index.astype(jnp.int32).reshape(1)
    attended, level = by_head(
        attend_kernel,
        turn,
        [queries, keys_low, values_low],
        [bias],
        [BF, F32],
        [],
        (0, head_count),
        "attend",
    )
    rank_out = product_cols(attended, down_output).astype(BF)

    def far_part(two, three):
        return (two.astype(F32) + to_core(three).astype(F32)).astype(BF)

    def near_part(zero, one):
        return zero.astype(F32) + to_core(one).astype(F32)

    def out_blocks(rows, first):
        return out_rows(rows, down_output, lift_output, weight_vo, row_count, first, 2)

    out_third, out_second = out_blocks(attended, 3)
    out_far = far_part(out_second, out_third)
    out_first, out_zero = out_blocks(after(attended, out_far, weight_ffn[0][1][0]), 1)
    main_rows = near_part(out_zero, out_first) + to_chip(out_far).astype(F32)
    main_rows = after(main_rows, held[3])
    rank_grad = product_cols(full_cot, lift_shrink).astype(BF)
    residual = inputs_wide + main_rows + out_bias
    unit_two, scale_two = normalize(residual)
    rows_two = (unit_two * gain_b + shift_b).astype(BF)
    full_two = after(gather_rows(rows_two, weight_ffn[1][1][0], weight_ffn[1][2][0], rank_grad), held[4])
    rank_two = product_cols(full_two, down_expand).astype(BF)

    state = None
    down_parts, up_parts = [], []

    def feed(h, rows, span):
        last = h == chunk_count - 1
        results = feed_forward(
            rows,
            full_cot,
            rank_two,
            rank_grad,
            weight_ffn[h],
            lift_expand,
            expand_bias[h * chunk : (h + 1) * chunk],
            down_shrink,
            h,
            state,
            (lift_shrink, down_expand) if last else None,
            span,
        )
        return results[:4], results[4], results[5]

    for h in range(chunk_count - 1):
        state, down_part, up_part = feed(h, full_two, (0, seq_len))
        down_parts.append(down_part)
        up_parts.append(up_part)

    last = chunk_count - 1
    third, *third_deltas = feed(last, full_two, (3 * row_count, seq_len))
    second, *second_deltas = feed(
        last, after(full_two, third[1][0]), (2 * row_count, 3 * row_count)
    )
    grad_far = far_part(second[1][0], third[1][0])
    near, *near_deltas = feed(last, after(full_two, grad_far), (0, 2 * row_count))
    down_parts.append(third_deltas[0] + second_deltas[0] + near_deltas[0])
    up_parts.append(third_deltas[1] + second_deltas[1] + near_deltas[1])
    grad_rank_two = jnp.concatenate([near[3], second[3], third[3]], axis=0).astype(BF)
    rank_shrink = jnp.concatenate([near[2], second[2], third[2]], axis=0).astype(BF)
    far_arrived = to_chip(grad_far)
    grad_residual, grad_branch = branch_rows(
        near[1][0],
        to_core(after(near[1][1], far_arrived)),
        far_arrived,
        cot,
        unit_two,
        scale_two,
        gain_b,
    )

    branch_near = to_core(grad_branch)
    branch_far = to_chip(grad_branch)
    delta_shrink_up = product_rows(after(rank_shrink, grad_branch), full_cot)
    delta_expand_down = product_rows(after(grad_rank_two, grad_branch), full_two)
    main_far = far_part(after(second[0][0], grad_branch), after(third[0][0], grad_branch))
    main_one = to_core(near[0][1])
    near_grad, near_rank = in_rows(
        grad_branch, branch_near, lift_output, down_output, weight_vo
    )
    middle = 2 * row_count
    delta_near = product_rows(rank_out[:row_count], grad_branch) + product_rows(
        rank_out[row_count:middle], branch_near
    )
    branch_held = after(
        branch_far, delta_shrink_up, delta_expand_down, main_far, near_grad, delta_near
    )
    branch_last = to_core(branch_held)

    hot_lanes = (
        jnp.arange(128, dtype=jnp.int32)[None, :] == adapter_choice[0]
    ).astype(BF) * jnp.ones((rank_width, 1), BF)

    quarter = feats // 4

    place = jnp.stack([dp_odd.astype(jnp.int32), tensor_index.astype(jnp.int32)])

    def packed(count):
        rows = count * rank_width
        return [((rows, quarter), BF), ((2 * rows, quarter), BF), ((rows, quarter), BF)]

    def settle_near(base, send, far):
        near = to_core(send)
        far = (far.astype(F32) + near[base.shape[0] :].astype(F32)).astype(BF)
        return base, near, far

    def settle_flat(base, near, far, slim):
        parts = [base, near, far, *slim, hot_lanes]
        rows = base.shape[0] // rank_width
        width = rows * quarter + sum(v.shape[1] for v in slim) + hot_lanes.shape[1]
        shapes = [v.shape for v in parts]
        shapes[1] = base.shape
        return pl.pallas_call(
            functools.partial(flat_kernel, rank_width),
            grid=(1,),
            in_specs=[pl.BlockSpec(shape, lambda i: (0, 0)) for shape in shapes],
            out_specs=pl.BlockSpec((rank_width, width), lambda i: (0, 0)),
            out_shape=jax.ShapeDtypeStruct((rank_width, width), BF),
            cost_estimate=pl.CostEstimate(flops=10**6, bytes_accessed=10**5, transcendentals=0),
            name="flatten",
        )(*parts)

    def settle_outs(own, near, away, away_near):
        flat = [v.reshape(slot_count * rank_width, -1) for v in (own, near, away, away_near)]
        shapes = [((slot_count * rank_width, feats), F32)] * 3
        outs = local_call(across_kernel, "across", place, flat, shapes)
        return [v.reshape(slot_count, rank_width, feats) for v in outs]

    def settle_pair(flat):
        return jnp.concatenate([flat, lax.ppermute(flat, "dp", dp_pairs)], axis=0)

    def settle_line(pair):
        return [pair] + [
            lax.ppermute(pair, "dp", [(i, (i + 2 * s) % dp_size) for i in range(dp_size)])
            for s in range(1, pair_count)
        ]

    early_parts = settle_near(
        *local_call(
            functools.partial(pack_kernel, dp_size),
            "pack",
            place,
            [
                delta_shrink_up,
                delta_expand_down,
                delta_near,
                rank_out[middle:],
                branch_held,
                branch_last,
            ],
            packed(3),
        )
    )
    far_grad, far_rank = in_rows(
        after(branch_held, early_parts[2]), branch_last, lift_output, down_output, weight_vo
    )
    rank_grad_out = jnp.concatenate([near_rank, far_rank], axis=0)
    grad_attended = jnp.concatenate([near_grad, far_grad], axis=0)
    delta_output_down = product_rows(rank_grad_out, attended)
    main_arrived = to_chip(after(main_far, early_parts[2], branch_far))

    def attend_back(grad, heads, before=()):
        return by_head(
            attend_back_kernel,
            turn,
            [queries, keys_low, values_low, grad],
            [bias, level],
            [BF, BF, BF],
            [pltpu.VMEM((seq_len, HEAD_DIM), F32)] * 2,
            heads,
            "attend_back",
            before,
        )

    grads = attend_back(after(grad_attended, early_parts[2]), (0, 1))
    early_flat = settle_flat(
        after(early_parts[0], grads[0]),
        early_parts[1],
        to_chip(early_parts[2]),
        [*down_parts, *up_parts, delta_output_down],
    )
    early_pair = settle_pair(early_flat)
    grads = attend_back(after(grad_attended, early_flat), (1, 1), grads)
    early_trees = lax.all_gather(
        after(early_pair, grads[0]), "dp", axis=0, tiled=True, axis_index_groups=line_groups
    )
    grads = attend_back(after(grad_attended, early_pair), (2, head_count - 2), grads)
    grad_query_low, grad_key_low, grad_value_low = grads
    grad_rank_one, *late_parts, delta_query_up, delta_key_up, delta_value_up = local_call(
        functools.partial(late_kernel, dp_size),
        "late_deltas",
        place,
        [*grads, lift_query, lift_key, lift_value, full_one, rank_one],
        [((seq_len, 3 * rank_width), BF)]
        + packed(3)
        + [((rank_width, width_local), F32)] * 3,
    )
    late_parts[1] = after(late_parts[1], main_arrived)
    late_base, late_near, late_far = settle_near(*late_parts)
    late_chip = to_chip(late_far)

    def rows_back(first, count, *held):
        rank = after(grad_rank_one, *held) if held else grad_rank_one
        return back_rows(
            [grad_query_low, grad_key_low, grad_value_low, rank],
            weight_qk,
            weight_vo,
            down_qkv,
            row_count,
            first,
            count,
        )

    late_flat = settle_flat(
        late_base, late_near, late_chip, [delta_query_up, delta_key_up, delta_value_up]
    )
    late_other = lax.ppermute(late_flat, "dp", dp_pairs)
    early_own, shrink_down_out, expand_up_out, output_down_out = sum_slots(
        [after(early_trees, late_flat)],
        slot_count,
        rank_width,
        3 * quarter,
        [hidden_local, hidden_local, width_local],
    )
    late_pair = jnp.concatenate([late_flat, after(late_other, early_own)], axis=0)
    late_trees = settle_line(late_pair)
    (back_third,) = rows_back(3, 1, late_pair)
    back_core = to_core(back_third)
    (back_second,) = rows_back(2, 1, back_third)
    early_away = to_chip(early_own)
    back_far = (back_second.astype(F32) + back_core.astype(F32)).astype(BF)
    back_far = after(back_far, early_away)
    back_arrived = to_chip(back_far)
    (output,) = local_call(
        functools.partial(output_kernel, dp_size),
        "output",
        place,
        [near[0][0], main_one, after(main_arrived, back_far), residual, last_bias[None]],
        [((row_count, feats), BF)],
        row_count // 4,
    )
    (back_first,) = rows_back(1, 1, output, late_trees[1])
    (back_zero,) = rows_back(0, 1, back_first, *late_trees[1:])
    late_own, query_up_out, key_up_out, value_up_out = sum_slots(
        [after(late_trees[0], back_zero), *late_trees[1:]],
        slot_count,
        rank_width,
        3 * quarter,
        [width_local] * 3,
    )
    late_away = to_chip(after(late_own, back_far))
    early_outs = settle_outs(
        early_own, to_core(early_own), early_away, to_core(after(early_away, late_own))
    )
    shrink_up_out, expand_down_out, output_up_out = early_outs
    back_one = to_core(after(back_first, back_arrived, late_own))
    grad_norm_one = (
        back_zero.astype(F32) + back_one.astype(F32) + back_arrived.astype(F32)
    )
    input_delta = natural(
        (grad_residual + norm_back(grad_norm_one, gain_a, unit_one, scale_one)).astype(BF)
    )
    query_down_out, key_down_out, value_down_out = settle_outs(
        late_own, to_core(late_own), late_away, to_core(after(late_away, input_delta, early_outs[0]))
    )
    return (
        output,
        input_delta,
        query_down_out,
        query_up_out,
        key_down_out,
        key_up_out,
        value_down_out,
        value_up_out,
        output_down_out,
        output_up_out,
        expand_down_out,
        expand_up_out,
        shrink_down_out,
        shrink_up_out,
    )


def solution(mesh):
    rows = P(("dp", "tensor"), None)
    tree = P("dp", None)
    whole = P()
    slim = P(None, None, "tensor")
    inward = P("dp", "tensor")
    outward = P("tensor", "dp")
    return jax.shard_map(
        functools.partial(shards, mesh.shape["dp"]),
        mesh=mesh,
        in_specs=(
            rows,
            rows,
            tree,
            tree,
            P("dp"),
            whole,
            whole,
            whole,
            whole,
            inward,
            inward,
            inward,
            outward,
            inward,
            outward,
            P("tensor"),
            P("tensor"),
            whole,
            P("tensor"),
            whole,
            whole,
            slim,
            whole,
            slim,
            whole,
            slim,
            slim,
            whole,
            whole,
            slim,
            slim,
            whole,
        ),
        out_specs=(
            rows,
            rows,
            whole,
            slim,
            whole,
            slim,
            whole,
            slim,
            slim,
            whole,
            whole,
            slim,
            slim,
            whole,
        ),
        check_vma=False,
    )
```

```python
import functools

import jax
import jax.numpy as jnp
from jax import lax
from jax.experimental import pallas as pl
from jax.experimental.pallas import tpu as pltpu
from jax.sharding import PartitionSpec as P

HEAD_DIM = 128
SEGS = 13
BF = jnp.bfloat16
F32 = jnp.float32


def ancestry(parents):
    seg_range = jnp.arange(SEGS, dtype=jnp.int32)
    current = seg_range
    ancestors = current[:, None] == seg_range[None, :]
    for hop_index in range(SEGS - 1):
        current = jnp.sum(
            jnp.where(current[:, None] == seg_range[None, :], parents[None, :], 0), axis=1
        )
        ancestors = jnp.logical_or(ancestors, current[:, None] == seg_range[None, :])
    return ancestors


def product(left, right):
    return jnp.dot(left, right, preferred_element_type=F32)


def product_cols(left, right):
    return lax.dot_general(
        left, right, (((1,), (1,)), ((), ())), preferred_element_type=F32
    )


def product_rows(left, right):
    return lax.dot_general(
        left, right, (((0,), (0,)), ((), ())), preferred_element_type=F32
    )


def join_kernel(*refs):
    *blocks, down, out, rank = refs
    for k, block in enumerate(blocks):

        @pl.when(pl.program_id(0) == k)
        def _(block=block):
            out[...] = block[...]
            rank[...] = product_cols(block[...], down[...]).astype(BF)


def join_rows(blocks, down):
    tile, feats = blocks[0].shape
    rank = down.shape[0]
    return pl.pallas_call(
        join_kernel,
        grid=(len(blocks),),
        in_specs=[
            pl.BlockSpec(v.shape, lambda i: (0, 0), pipeline_mode=pl.Buffered(1))
            for v in (*blocks, down)
        ],
        out_specs=[
            pl.BlockSpec((tile, feats), lambda i: (i, 0)),
            pl.BlockSpec((tile, rank), lambda i: (i, 0)),
        ],
        out_shape=[
            jax.ShapeDtypeStruct((len(blocks) * tile, feats), BF),
            jax.ShapeDtypeStruct((len(blocks) * tile, rank), BF),
        ],
        cost_estimate=pl.CostEstimate(flops=10**6, bytes_accessed=10**5, transcendentals=0),
        name="join_rows",
    )(*blocks, down)


def feed_kernel(first, last, pieces, *refs):
    rows, cots, rank_in, rank_grad, lift, bias, down = refs[:7]
    weights, refs = refs[7 : 7 + pieces], refs[7 + pieces :]
    if not first:
        main_in, grad_in, rank_main_in, rank_back_in = refs[:4]
        refs = refs[4:]
    if last:
        lift_after, down_before = refs[:2]
        refs = refs[2:]
    mains, grads = refs[: len(refs) // 2 - 2], refs[len(refs) // 2 - 2 : -4]
    rank_main, rank_back, down_delta, up_delta = refs[-4:]
    chunk = lift.shape[1]
    parts, at = [], 0
    for weight in weights:
        parts.append((slice(at, at + weight.shape[0]), weight))
        at += weight.shape[0]

    pre_act = (
        sum(product(rows[:, here], weight[:, :chunk]) for here, weight in parts)
        + product(rank_in[...], lift[...])
        + bias[...]
    )
    grad_hidden = sum(
        product(cots[:, here], weight[:, chunk:]) for here, weight in parts
    ) + product(rank_grad[...], down[...])
    bell = 0.5 * (1.0 + lax.erf(pre_act * (0.5**0.5)))
    slope = bell + pre_act * jnp.exp(-0.5 * pre_act * pre_act) * (0.5 / jnp.pi) ** 0.5
    hidden = (pre_act * bell).astype(BF)
    grad_pre = (grad_hidden * slope).astype(BF)

    main_rank = product_cols(hidden, down[...])
    back_rank = product_cols(grad_pre, lift[...])
    if not first:
        main_rank = main_rank + rank_main_in[...]
        back_rank = back_rank + rank_back_in[...]
    rank_main[...] = main_rank
    rank_back[...] = back_rank
    for here, weight in parts:
        ahead = product_cols(hidden, weight[:, chunk:])
        back = product_cols(grad_pre, weight[:, :chunk])
        if not first:
            ahead = ahead + main_in[:, here]
            back = back + grad_in[:, here]
        if last:
            ahead = ahead + product(main_rank.astype(BF), lift_after[:, here])
            back = back + product(back_rank.astype(BF), down_before[:, here])
        for k, (main, grad) in enumerate(zip(mains, grads)):

            @pl.when((pl.program_id(0) == k) | (len(mains) == 1))
            def _(main=main, grad=grad, here=here, ahead=ahead, back=back):
                main[:, here] = ahead.astype(main.dtype)
                grad[:, here] = back.astype(grad.dtype)

    down_part = product_rows(rank_grad[...], hidden)
    up_part = product_rows(rank_in[...], grad_pre)

    @pl.when(pl.program_id(0) == 0)
    def _():
        down_delta[...] = down_part
        up_delta[...] = up_part

    @pl.when(pl.program_id(0) > 0)
    def _():
        down_delta[...] += down_part
        up_delta[...] += up_part


def feed_forward(rows, cots, rank_in, rank_grad, weight, lift, bias, down, at, before, final, span):
    tile = 256
    feats = rows.shape[1]
    chunk = bias.shape[0]
    rank = lift.shape[0]
    begin, count = span[0] // tile, (span[1] - span[0]) // tile
    first, last = before is None, final is not None

    def row_block(width):
        return pl.BlockSpec((tile, width), lambda i: (begin + i, 0))

    def out_block(width):
        return pl.BlockSpec((tile, width), lambda i: (i, 0))

    def fixed(shape, column=0):
        return pl.BlockSpec(shape, lambda i: (0, column), pipeline_mode=pl.Buffered(1))

    args = [rows, cots, rank_in, rank_grad, lift, bias[None], down]
    specs = [
        row_block(feats),
        row_block(feats),
        row_block(rank),
        row_block(rank),
        fixed((rank, chunk), at),
        fixed((1, chunk), 0),
        fixed((rank, chunk), at),
    ]
    for piece, column in weight:
        args.append(piece)
        specs.append(fixed((piece.shape[0], 2 * chunk), column))
    if not first:
        args += [before[0][0], before[1][0], before[2], before[3]]
        specs += [row_block(feats), row_block(feats), row_block(rank), row_block(rank)]
    if last:
        args += list(final)
        specs += [fixed((rank, feats)), fixed((rank, feats))]
    size = span[1] - span[0]
    flops = size * feats * chunk
    if last:
        wide_specs = [fixed((tile, feats))] * (2 * count)
        wide_shapes = [jax.ShapeDtypeStruct((tile, feats), BF)] * (2 * count)
    else:
        wide_specs = [out_block(feats)] * 2
        wide_shapes = [jax.ShapeDtypeStruct((size, feats), BF)] * 2
    results = pl.pallas_call(
        functools.partial(feed_kernel, first, last, len(weight)),
        grid=(count,),
        in_specs=specs,
        out_specs=wide_specs
        + [
            out_block(rank),
            out_block(rank),
            pl.BlockSpec((rank, chunk), lambda i: (0, 0)),
            pl.BlockSpec((rank, chunk), lambda i: (0, 0)),
        ],
        out_shape=wide_shapes
        + [
            jax.ShapeDtypeStruct((size, rank), F32),
            jax.ShapeDtypeStruct((size, rank), F32),
            jax.ShapeDtypeStruct((rank, chunk), F32),
            jax.ShapeDtypeStruct((rank, chunk), F32),
        ],
        cost_estimate=pl.CostEstimate(
            flops=flops, bytes_accessed=size * feats * 20, transcendentals=size * chunk * 2
        ),
        name="feed_forward",
    )(*args)
    wide = len(wide_specs) // 2
    return results[:wide], results[wide : 2 * wide], *results[2 * wide :]


def attend_kernel(scale, turn, *refs):
    count = (len(refs) - 3) // 3
    query, key, value = refs[:count], refs[count : 2 * count], refs[2 * count : 3 * count]
    bias, attended, level = refs[3 * count :]
    rows = query[0].shape[0]
    for i in range(count):
        here = slice(i * rows, (i + 1) * rows)
        scores = [
            product_cols(query[i][...], key[j][...]) * scale
            + bias[here, j * rows : (j + 1) * rows]
            for j in range(i + 1)
        ]
        top = functools.reduce(
            jnp.maximum, [jnp.max(v, axis=-1, keepdims=True) for v in scores]
        )
        raised = [jnp.exp(v - top) for v in scores]
        total = sum(jnp.sum(v, axis=-1, keepdims=True) for v in raised)
        share = 1.0 / total
        mixed = sum(
            product((v * share).astype(BF), value[j][...]) for j, v in enumerate(raised)
        )
        to = pl.multiple_of((i ^ turn[0]) * rows, rows)
        attended[pl.ds(to, rows), :] = mixed.astype(BF)
        level[here, :] = jnp.broadcast_to(top + jnp.log(total), (rows, level.shape[1]))


def attend_back_kernel(scale, turn, *refs):
    count = (len(refs) - 7) // 4
    query, key, value, grad = (refs[n * count : (n + 1) * count] for n in range(4))
    bias, level = refs[4 * count : 4 * count + 2]
    grad_query, grad_key, grad_value, key_sum, value_sum = refs[-5:]
    rows = query[0].shape[0]
    for i in range(count):
        here = slice(i * rows, (i + 1) * rows)
        row_level = level[here, :1]
        probs = [
            jnp.exp(
                product_cols(query[i][...], key[j][...]) * scale
                + bias[here, j * rows : (j + 1) * rows]
                - row_level
            )
            for j in range(i + 1)
        ]
        grad_probs = [product_cols(grad[i][...], value[j][...]) for j in range(i + 1)]
        mean = sum(
            jnp.sum(p * g, axis=-1, keepdims=True) for p, g in zip(probs, grad_probs)
        )
        query_sum = 0.0
        for j in range(i + 1):
            there = slice(j * rows, (j + 1) * rows)
            grad_score = (probs[j] * (grad_probs[j] - mean)).astype(BF)
            query_sum = query_sum + product(grad_score, key[j][...])
            key_part = product_rows(grad_score, query[i][...])
            value_part = product_rows(probs[j].astype(BF), grad[i][...])
            if i > j:
                key_part = key_part + key_sum[there, :]
                value_part = value_part + value_sum[there, :]
            key_sum[there, :] = key_part
            value_sum[there, :] = value_part
        to = pl.multiple_of((i ^ turn[0]) * rows, rows)
        grad_query[pl.ds(to, rows), :] = (query_sum * scale).astype(BF)
    for j in range(count):
        there = slice(j * rows, (j + 1) * rows)
        to = pl.multiple_of((j ^ turn[0]) * rows, rows)
        grad_key[pl.ds(to, rows), :] = (key_sum[there, :] * scale).astype(BF)
        grad_value[pl.ds(to, rows), :] = value_sum[there, :].astype(BF)


def by_head(kernel, turn, blocked, whole, outs, scratch, heads, name, before=()):
    first, count = heads
    seq_len, width = blocked[0].shape
    blocks = 4
    rows = seq_len // blocks
    specs, args = [], []
    for v in blocked:
        for k in range(blocks):
            specs.append(
                pl.BlockSpec((rows, HEAD_DIM), lambda h, turn, k=k: (k ^ turn[0], first + h))
            )
            args.append(v)
    for v in whole:
        if v.shape[1] == seq_len:
            specs.append(
                pl.BlockSpec(v.shape, lambda h, turn: (0, 0), pipeline_mode=pl.Buffered(1))
            )
        else:
            specs.append(pl.BlockSpec((seq_len, HEAD_DIM), lambda h, turn: (0, first + h)))
        args.append(v)
    aliases = {1 + len(args) + n: n for n in range(len(before))}
    specs += [pl.BlockSpec(memory_space=pl.ANY)] * len(before)
    args += before
    return pl.pallas_call(
        functools.partial(kernel, HEAD_DIM ** (-0.5)),
        grid_spec=pltpu.PrefetchScalarGridSpec(
            num_scalar_prefetch=1,
            grid=(count,),
            in_specs=specs,
            out_specs=[pl.BlockSpec((seq_len, HEAD_DIM), lambda h, turn: (0, first + h))] * len(outs),
            scratch_shapes=scratch,
        ),
        out_shape=[jax.ShapeDtypeStruct((seq_len, width), t) for t in outs],
        input_output_aliases=aliases,
        cost_estimate=pl.CostEstimate(flops=10**8, bytes_accessed=10**6, transcendentals=0),
        name=name,
    )(turn, *args)


def branch_kernel(zero, one, far, base, unit, scale, gain, wide, low):
    unit_rows = unit[...]
    scaled = (
        zero[...].astype(F32) + one[...].astype(F32) + far[...].astype(F32)
    ) * gain[...]
    total = base[...].astype(F32) + scale[...] * (
        scaled
        - jnp.mean(scaled, axis=-1, keepdims=True)
        - unit_rows * jnp.mean(scaled * unit_rows, axis=-1, keepdims=True)
    )
    wide[...] = total
    low[...] = total.astype(BF)


def branch_rows(zero, one, far, base, unit, scale, gain):
    rows, feats = unit.shape
    tile = rows // 4
    wide = pl.BlockSpec((tile, feats), lambda i: (i, 0))
    return pl.pallas_call(
        branch_kernel,
        grid=(rows // tile,),
        in_specs=[wide] * 5
        + [pl.BlockSpec((tile, 1), lambda i: (i, 0)), pl.BlockSpec((1, feats), lambda i: (0, 0))],
        out_specs=[wide, wide],
        out_shape=[
            jax.ShapeDtypeStruct((rows, feats), F32),
            jax.ShapeDtypeStruct((rows, feats), BF),
        ],
        cost_estimate=pl.CostEstimate(flops=10**7, bytes_accessed=10**6, transcendentals=0),
        name="branch_rows",
    )(zero, one, far, base, unit, scale, gain[None])


def back_kernel(query, key, value, rank, qk_own, qk_other, vo_own, vo_other, down, *outs):
    width = query.shape[1]
    half = qk_own.shape[0]
    for at, qk, vo in ((0, qk_own, vo_own), (half, qk_other, vo_other)):
        rows = (
            product_cols(query[...], qk[:, :width])
            + product_cols(key[...], qk[:, width:])
            + product_cols(value[...], vo[...])
            + product(rank[...], down[:, at : at + half])
        ).astype(BF)
        for k, out in enumerate(outs):

            @pl.when(pl.program_id(0) == k)
            def _(out=out, rows=rows, at=at):
                out[:, at : at + half] = rows


def out_kernel(rows, down, lift, own, other, *outs):
    half = own.shape[0]
    rank = product_cols(rows[...], down[...]).astype(BF)
    for at, weight in ((0, own), (half, other)):
        here = slice(at, at + half)
        mixed = product_cols(rows[...], weight[...]) + product(rank, lift[:, here])
        for k, out in enumerate(outs):

            @pl.when(pl.program_id(0) == k)
            def _(out=out, mixed=mixed, here=here):
                out[:, here] = mixed.astype(BF)


def out_rows(rows, down, lift, weight, tile, first, count):
    half, width = weight[0].shape[0], rows.shape[1]

    def fixed(shape, column=0):
        return pl.BlockSpec(shape, lambda i: (0, column), pipeline_mode=pl.Buffered(1))

    return pl.pallas_call(
        out_kernel,
        grid=(count,),
        in_specs=[pl.BlockSpec((tile, width), lambda i: (first - i, 0))]
        + [fixed(down.shape), fixed(lift.shape)]
        + [fixed((half, width), 1)] * 2,
        out_specs=[fixed((tile, lift.shape[1]))] * count,
        out_shape=[jax.ShapeDtypeStruct((tile, lift.shape[1]), BF)] * count,
        cost_estimate=pl.CostEstimate(flops=10**7, bytes_accessed=10**5, transcendentals=0),
        name="out_rows",
    )(rows, down, lift, *weight[:2])


def back_rows(grads, weight_qk, weight_vo, down, tile, first, count):
    half, width = weight_vo[0].shape[0], grads[0].shape[1]

    def fixed(shape):
        return pl.BlockSpec(shape, lambda i: (0, 0), pipeline_mode=pl.Buffered(1))

    return pl.pallas_call(
        back_kernel,
        grid=(count,),
        in_specs=[pl.BlockSpec((tile, v.shape[1]), lambda i: (first - i, 0)) for v in grads]
        + [fixed((half, 2 * width))] * 2
        + [fixed((half, width))] * 2
        + [fixed(down.shape)],
        out_specs=[fixed((tile, down.shape[1]))] * count,
        out_shape=[jax.ShapeDtypeStruct((tile, down.shape[1]), BF)] * count,
        cost_estimate=pl.CostEstimate(flops=10**8, bytes_accessed=10**6, transcendentals=0),
        name="back_rows",
    )(*grads, *weight_qk[:2], *weight_vo[:2], down)


def by_place(place, parts):
    core_odd, chip_odd = place[1] % 2 == 1, place[1] // 2 == 1
    low = [jnp.where(core_odd, parts[1], parts[0]), jnp.where(core_odd, parts[0], parts[1])]
    high = [jnp.where(core_odd, parts[3], parts[2]), jnp.where(core_odd, parts[2], parts[3])]
    return [jnp.where(chip_odd, b, a) for a, b in zip(low + high, high + low)]


def in_order(place, blocks, values):
    size = values.shape[1] // blocks
    parts = [values[:, k * size : (k + 1) * size] for k in range(blocks)]
    ordered = []
    for own, other in zip(parts[: blocks // 2], parts[blocks // 2 :]):
        ordered.append(jnp.where(place[0] == 1, other, own))
        ordered.append(jnp.where(place[0] == 1, own, other))
    return jnp.concatenate(ordered, axis=1)


def pack(place, blocks, wide, base, send, far):
    total = base.shape[0]
    for k, values in enumerate(wide):
        ordered = in_order(place, blocks, values)
        size = ordered.shape[1] // 4
        parts = by_place(place, [ordered[:, t * size : (t + 1) * size] for t in range(4)])
        at, rows = k * values.shape[0], values.shape[0]
        base[at : at + rows] = parts[0].astype(BF)
        send[at : at + rows] = parts[1].astype(BF)
        send[total + at : total + at + rows] = parts[3].astype(BF)
        far[at : at + rows] = parts[2].astype(BF)


def pack_kernel(blocks, place, *refs):
    *wide, rank, first, second, base, send, far = refs
    tile = first.shape[0]
    wide = [ref[...] for ref in wide]
    wide[-1] = (
        wide[-1] + product_rows(rank[:tile], first[...]) + product_rows(rank[tile:], second[...])
    )
    pack(place, blocks, wide, base, send, far)


def in_kernel(first, second, lift, down, own, other, grad, rank):
    half, tile = own.shape[0], first.shape[0]
    for k, rows in enumerate((first, second)):
        here = slice(k * tile, (k + 1) * tile)
        ranks = product_cols(rows[...], lift[...]).astype(BF)
        rank[here, :] = ranks
        grad[here, :] = (
            product(rows[:, :half], own[...])
            + product(rows[:, half:], other[...])
            + product(ranks, down[...])
        ).astype(BF)


def in_rows(first, second, lift, down, weight):
    half, width = weight[0].shape[0], down.shape[1]
    rows = 2 * first.shape[0]
    whole = [pl.BlockSpec(v.shape, lambda i: (0, 0)) for v in (first, second, lift, down)]
    return pl.pallas_call(
        in_kernel,
        grid=(1,),
        in_specs=whole + [pl.BlockSpec((half, width), lambda i: (0, 1))] * 2,
        out_specs=[
            pl.BlockSpec((rows, width), lambda i: (0, 0)),
            pl.BlockSpec((rows, lift.shape[0]), lambda i: (0, 0)),
        ],
        out_shape=[
            jax.ShapeDtypeStruct((rows, width), BF),
            jax.ShapeDtypeStruct((rows, lift.shape[0]), BF),
        ],
        cost_estimate=pl.CostEstimate(flops=10**7, bytes_accessed=10**5, transcendentals=0),
        name="in_rows",
    )(first, second, lift, down, *weight[:2])


def late_kernel(blocks, place, *refs):
    grads, lifts, rows, ranks = refs[:3], refs[3:6], refs[6], refs[7]
    rank_grad, base, send, far, *ups = refs[8:]
    width = lifts[0].shape[0]
    wide = []
    for k, (grad, lift, up) in enumerate(zip(grads, lifts, ups)):
        here = slice(k * width, (k + 1) * width)
        rank = product_cols(grad[...], lift[...]).astype(BF)
        rank_grad[:, here] = rank
        wide.append(product_rows(rank, rows[...]))
        up[...] = product_rows(ranks[:, here], grad[...])
    pack(place, blocks, wide, base, send, far)


def across_kernel(place, *refs):
    parts, outs = refs[:4], refs[4:]
    size = parts[0].shape[1] // len(outs)
    for k, out in enumerate(outs):
        here = slice(k * size, (k + 1) * size)
        for t, part in enumerate(by_place(place, [v[:, here].astype(F32) for v in parts])):
            out[:, t * size : (t + 1) * size] = part


def output_kernel(blocks, place, zero, one, far, base, bias, out):
    total = base[...] + bias[...] + zero[...].astype(F32)
    total = total + one[...].astype(F32) + far[...].astype(F32)
    out[...] = in_order(place, blocks, total).astype(BF)


def local_call(kernel, name, place, args, shapes, tile=None):
    specs = [pl.BlockSpec(memory_space=pltpu.SMEM)]
    options = {}
    if tile is None:
        specs += [pl.BlockSpec(memory_space=pltpu.VMEM) for _ in args]
        out_specs = [pl.BlockSpec(memory_space=pltpu.VMEM) for _ in shapes]
    else:
        rows = shapes[0][0][0]

        def spec(shape):
            if shape[0] == rows:
                return pl.BlockSpec((tile, shape[1]), lambda i: (i, 0))
            return pl.BlockSpec(shape, lambda i: (0, 0))

        options = {"grid": (rows // tile,)}
        specs += [spec(v.shape) for v in args]
        out_specs = [spec(shape) for shape, _ in shapes]
    return pl.pallas_call(
        kernel,
        in_specs=specs,
        out_specs=out_specs,
        out_shape=[jax.ShapeDtypeStruct(shape, kind) for shape, kind in shapes],
        cost_estimate=pl.CostEstimate(flops=10**6, bytes_accessed=10**5, transcendentals=0),
        name=name,
        **options,
    )(place, *args)


def flat_kernel(rank, *refs):
    base, near, far, *slim, marks, out = refs
    mine = (
        base[...].astype(F32) + near[...].astype(F32) + far[...].astype(F32)
    ).astype(BF)
    width = mine.shape[1]
    at = 0
    for k in range(mine.shape[0] // rank):
        out[:, at : at + width] = mine[k * rank : (k + 1) * rank]
        at += width
    for part in slim:
        out[:, at : at + part.shape[1]] = part[...].astype(BF)
        at += part.shape[1]
    out[:, at:] = marks[...]


def slots_kernel(slot_count, rank, *refs):
    tree_count = len(refs) - 4
    trees = jnp.concatenate([ref[...] for ref in refs[:tree_count]], axis=0)
    lanes = slot_count * rank
    width = trees.shape[1] - lanes
    source = lax.broadcasted_iota(jnp.int32, (lanes, lanes), 0)
    target = lax.broadcasted_iota(jnp.int32, (lanes, lanes), 1)
    spread = jnp.where(source == target // rank, 1.0, 0.0).astype(BF)
    marks = product(trees[:, width:], spread)
    row = lax.broadcasted_iota(jnp.int32, marks.shape, 0)
    lane = lax.broadcasted_iota(jnp.int32, marks.shape, 1)
    marks = jnp.where(row % rank == lane % rank, marks, 0.0).astype(BF)
    at = 0
    for out in refs[tree_count:]:
        size = out.shape[1]
        out[...] = product_rows(marks, trees[:, at : at + size]).astype(out.dtype)
        at += size


def sum_slots(trees, slot_count, rank, wide, slim):
    rows = slot_count * rank
    wide_sum, *slim_sums = pl.pallas_call(
        functools.partial(slots_kernel, slot_count, rank),
        out_shape=[jax.ShapeDtypeStruct((rows, wide), BF)]
        + [jax.ShapeDtypeStruct((rows, n), F32) for n in slim],
        cost_estimate=pl.CostEstimate(flops=10**6, bytes_accessed=10**5, transcendentals=0),
        name="sum_slots",
    )(*trees)
    return [v.reshape(slot_count, rank, -1) for v in (wide_sum, *slim_sums)]


def shards(
    dp_size,
    inputs,
    cotangent,
    segment_ids,
    parent_links,
    adapter_choice,
    gain_one,
    shift_one,
    gain_two,
    shift_two,
    query_weight,
    key_weight,
    value_weight,
    output_weight,
    expand_weight,
    shrink_weight,
    query_bias,
    value_bias,
    output_bias,
    expand_bias,
    shrink_bias,
    query_down,
    query_up,
    key_down,
    key_up,
    value_down,
    value_up,
    output_down,
    output_up,
    expand_down,
    expand_up,
    shrink_down,
    shrink_up,
):
    slot_count = query_down.shape[0]
    rank_width = query_down.shape[1]
    feats = inputs.shape[1]
    row_count = inputs.shape[0]
    width_local = query_weight.shape[1]
    hidden_local = expand_weight.shape[1]
    pair_count = dp_size // 2
    block = feats // dp_size
    half = feats // 2

    tensor_index = lax.axis_index("tensor")
    core_odd = (tensor_index % 2) == 1
    chip_odd = (tensor_index // 2) == 1
    dp_odd = (lax.axis_index("dp") % 2) == 1

    core_pairs = [(0, 1), (1, 0), (2, 3), (3, 2)]
    chip_pairs = [(0, 2), (2, 0), (1, 3), (3, 1)]
    dp_pairs = [(i, i ^ 1) for i in range(dp_size)]
    line_groups = [list(range(0, dp_size, 2)), list(range(1, dp_size, 2))]

    def to_core(v):
        return lax.ppermute(v, "tensor", core_pairs)

    def to_chip(v):
        return lax.ppermute(v, "tensor", chip_pairs)

    def own_first(v):
        parts = [v[..., b * block : (b + 1) * block] for b in range(dp_size)]
        pairs = [(parts[2 * p], parts[2 * p + 1]) for p in range(pair_count)]
        return jnp.concatenate(
            [jnp.where(dp_odd, odd, even) for even, odd in pairs]
            + [jnp.where(dp_odd, even, odd) for even, odd in pairs],
            axis=-1,
        )

    def natural(v):
        parts = [v[..., b * block : (b + 1) * block] for b in range(dp_size)]
        pairs = [(parts[p], parts[pair_count + p]) for p in range(pair_count)]
        return jnp.concatenate(
            [
                jnp.where(dp_odd, a, b)
                for own, other in pairs
                for a, b in ((other, own), (own, other))
            ],
            axis=-1,
        )

    def after(value, *others):
        return lax.optimization_barrier((value,) + others)[0]

    def gather_rows(rows, *held):
        near = to_core(rows)
        far = to_chip(rows)
        if held:
            far = after(far, *held)
        far_near = to_core(far)
        return jnp.concatenate([rows, near, far, far_near], axis=0)

    def line_gather(shard, held):
        if held:
            shard = after(shard, *held)
        return lax.all_gather(shard, "dp", axis=0, tiled=True, axis_index_groups=line_groups)

    def fetch(shard, *held):
        own = line_gather(shard, held)
        return own, lax.ppermute(own, "dp", dp_pairs), 0

    def fetch_pieces(shard, parts, *held):
        own = line_gather(shard, held)
        size = own.shape[0] // parts
        swapped = [
            lax.ppermute(own[k * size : (k + 1) * size], "dp", dp_pairs) for k in range(parts)
        ]
        return [(v, 0) for v in (own, *swapped)]

    def swap_after(pieces, *held):
        own = pieces[0][0]
        return [(own, 0), (lax.ppermute(after(own, *held), "dp", dp_pairs), 0)]

    def fetch_paired(pair, *held):
        both = line_gather(pair, held)
        return [(both, 0), (both, 1)]

    def into(left, weight, first, last):
        own, other, skip = weight
        return product(left[:, :half], own[:, first:last]) + product(
            left[:, half:], other[:, skip + first : skip + last]
        )

    def out_of(left, weight, first, last, base=None):
        own, other, skip = weight
        near = product_cols(left, own[:, first:last])
        far = product_cols(left, other[:, skip + first : skip + last])
        if base is not None:
            near, far = base[0] + near, base[1] + far
        return near, far

    def beside(pair):
        return jnp.concatenate(pair, axis=1)

    chunk_count = 4
    chunk = hidden_local // chunk_count
    output_turned = output_weight.T
    shrink_turned = shrink_weight.T
    def feed_shard(h):
        return jnp.concatenate(
            [
                expand_weight[:, h * chunk : (h + 1) * chunk],
                shrink_turned[:, h * chunk : (h + 1) * chunk],
            ],
            axis=1,
        )

    last_shard = feed_shard(chunk_count - 1)
    last_pair = jnp.concatenate([last_shard, lax.ppermute(last_shard, "dp", dp_pairs)], axis=1)
    weight_qk = fetch(jnp.concatenate([query_weight, key_weight], axis=1))
    weight_vo = fetch(jnp.concatenate([value_weight, output_turned], axis=1))
    select = (jnp.arange(slot_count, dtype=jnp.int32) == adapter_choice[0]).astype(BF)

    def adapter_of(adapter_table):
        return jnp.einsum(
            "a,ard->rd", select, adapter_table, preferred_element_type=F32
        ).astype(BF)

    down_qkv = own_first(
        jnp.concatenate(
            [adapter_of(query_down), adapter_of(key_down), adapter_of(value_down)], axis=0
        )
    )
    lift_query = adapter_of(query_up)
    lift_key = adapter_of(key_up)
    lift_value = adapter_of(value_up)
    down_output = adapter_of(output_down)
    lift_output = own_first(adapter_of(output_up))
    down_expand = own_first(adapter_of(expand_down))
    lift_expand = adapter_of(expand_up)
    down_shrink = adapter_of(shrink_down)
    lift_shrink = own_first(adapter_of(shrink_up))

    gain_a, shift_a = own_first(gain_one), own_first(shift_one)
    gain_b, shift_b = own_first(gain_two), own_first(shift_two)
    out_bias = own_first(output_bias)
    last_bias = own_first(shrink_bias)

    def normalize(values):
        row_mean = jnp.mean(values, axis=-1, keepdims=True)
        centred = values - row_mean
        row_var = jnp.mean(centred * centred, axis=-1, keepdims=True)
        scale = lax.rsqrt(row_var + 1e-05)
        return centred * scale, scale

    def norm_back(grad, gain, unit, scale):
        scaled = grad * gain
        return (
            scaled
            - jnp.mean(scaled, axis=-1, keepdims=True)
            - unit * jnp.mean(scaled * unit, axis=-1, keepdims=True)
        ) * scale

    inputs_wide = own_first(inputs).astype(F32)
    cot = own_first(cotangent)
    unit_one, scale_one = normalize(inputs_wide)
    rows_one = (unit_one * gain_a + shift_a).astype(BF)
    full_one = gather_rows(rows_one, gain_b, shift_b, out_bias, last_bias)
    full_cot = gather_rows(cot)
    seq_len = full_one.shape[0]
    head_count = width_local // HEAD_DIM

    rank_one = product_cols(full_one, down_qkv).astype(BF)
    weight_ffn, held = [], [weight_qk[0], weight_vo[0]]
    for h in range(chunk_count - 1):
        more = (last_pair, rank_one) if h == 0 else ()
        weight_ffn.append(fetch_pieces(feed_shard(h), 2 if h == 1 else 1, held[h], *more))
        held.append(weight_ffn[-1][0][0])
    weight_ffn.append(fetch_paired(last_pair, held[-2]))

    rank_query = rank_one[:, :rank_width]
    rank_key = rank_one[:, rank_width : 2 * rank_width]
    rank_value = rank_one[:, 2 * rank_width :]
    query_key = into(after(full_one, weight_vo[0]), weight_qk, 0, 2 * width_local)
    queries = (query_key[:, :width_local] + product(rank_query, lift_query) + query_bias).astype(BF)
    keys_low = (query_key[:, width_local:] + product(rank_key, lift_key)).astype(BF)
    values_low = (
        into(after(full_one, held[2]), weight_vo, 0, width_local)
        + product(rank_value, lift_value)
        + value_bias
    ).astype(BF)
    seg_range = jnp.arange(SEGS, dtype=jnp.int32)
    seg_hot = (segment_ids[0][:, None] == seg_range[None, :]).astype(BF)
    path_hot = product(seg_hot, ancestry(parent_links[0]).astype(BF)).astype(BF)
    positions = jnp.arange(seq_len, dtype=jnp.int32)
    allowed = jnp.logical_and(
        product_cols(path_hot, seg_hot) > 0.5, positions[:, None] >= positions[None, :]
    )
    bias = jnp.where(allowed, 0.0, -1e30)
    turn = tensor_index.astype(jnp.int32).reshape(1)
    attended, level = by_head(
        attend_kernel,
        turn,
        [queries, keys_low, values_low],
        [bias],
        [BF, F32],
        [],
        (0, head_count),
        "attend",
    )
    rank_out = product_cols(attended, down_output).astype(BF)

    def far_part(two, three):
        return (two.astype(F32) + to_core(three).astype(F32)).astype(BF)

    def near_part(zero, one):
        return zero.astype(F32) + to_core(one).astype(F32)

    def out_blocks(rows, first):
        return out_rows(rows, down_output, lift_output, weight_vo, row_count, first, 2)

    out_third, out_second = out_blocks(attended, 3)
    out_far = far_part(out_second, out_third)
    out_first, out_zero = out_blocks(after(attended, out_far, weight_ffn[0][1][0]), 1)
    main_rows = near_part(out_zero, out_first) + to_chip(out_far).astype(F32)
    main_rows = after(main_rows, held[3])
    rank_grad = product_cols(full_cot, lift_shrink).astype(BF)
    residual = inputs_wide + main_rows + out_bias
    unit_two, scale_two = normalize(residual)
    rows_two = (unit_two * gain_b + shift_b).astype(BF)
    near_two = to_core(rows_two)
    far_two = after(to_chip(rows_two), weight_ffn[1][1][0], weight_ffn[1][2][0], rank_grad)
    weight_ffn[2] = swap_after(weight_ffn[2], far_two)
    last_two = to_core(far_two)
    full_two, rank_two = join_rows([rows_two, near_two, far_two, last_two], down_expand)

    state = None
    down_parts, up_parts = [], []

    def feed(h, rows, span):
        last = h == chunk_count - 1
        results = feed_forward(
            rows,
            full_cot,
            rank_two,
            rank_grad,
            weight_ffn[h],
            lift_expand,
            expand_bias[h * chunk : (h + 1) * chunk],
            down_shrink,
            h,
            state,
            (lift_shrink, down_expand) if last else None,
            span,
        )
        return results[:4], results[4], results[5]

    for h in range(chunk_count - 1):
        state, down_part, up_part = feed(h, full_two, (0, seq_len))
        down_parts.append(down_part)
        up_parts.append(up_part)

    last = chunk_count - 1
    third, *third_deltas = feed(last, full_two, (3 * row_count, seq_len))
    second, *second_deltas = feed(
        last, after(full_two, third[1][0]), (2 * row_count, 3 * row_count)
    )
    grad_far = far_part(second[1][0], third[1][0])
    near, *near_deltas = feed(last, after(full_two, grad_far), (0, 2 * row_count))
    down_parts.append(third_deltas[0] + second_deltas[0] + near_deltas[0])
    up_parts.append(third_deltas[1] + second_deltas[1] + near_deltas[1])
    grad_rank_two = jnp.concatenate([near[3], second[3], third[3]], axis=0).astype(BF)
    rank_shrink = jnp.concatenate([near[2], second[2], third[2]], axis=0).astype(BF)
    far_arrived = to_chip(grad_far)
    grad_residual, grad_branch = branch_rows(
        near[1][0],
        to_core(after(near[1][1], far_arrived)),
        far_arrived,
        cot,
        unit_two,
        scale_two,
        gain_b,
    )

    branch_near = to_core(grad_branch)
    branch_far = to_chip(grad_branch)
    delta_shrink_up = product_rows(after(rank_shrink, grad_branch), full_cot)
    delta_expand_down = product_rows(after(grad_rank_two, grad_branch), full_two)
    main_far = far_part(after(second[0][0], grad_branch), after(third[0][0], grad_branch))
    main_one = to_core(near[0][1])
    near_grad, near_rank = in_rows(
        grad_branch, branch_near, lift_output, down_output, weight_vo
    )
    middle = 2 * row_count
    delta_near = product_rows(rank_out[:row_count], grad_branch) + product_rows(
        rank_out[row_count:middle], branch_near
    )
    branch_held = after(
        branch_far, delta_shrink_up, delta_expand_down, main_far, near_grad, delta_near
    )
    branch_last = to_core(branch_held)

    hot_lanes = (
        jnp.arange(128, dtype=jnp.int32)[None, :] == adapter_choice[0]
    ).astype(BF) * jnp.ones((rank_width, 1), BF)

    quarter = feats // 4

    place = jnp.stack([dp_odd.astype(jnp.int32), tensor_index.astype(jnp.int32)])

    def packed(count):
        rows = count * rank_width
        return [((rows, quarter), BF), ((2 * rows, quarter), BF), ((rows, quarter), BF)]

    def settle_near(base, send, far):
        near = to_core(send)
        far = (far.astype(F32) + near[base.shape[0] :].astype(F32)).astype(BF)
        return base, near, far

    def settle_flat(base, near, far, slim):
        parts = [base, near, far, *slim, hot_lanes]
        rows = base.shape[0] // rank_width
        width = rows * quarter + sum(v.shape[1] for v in slim) + hot_lanes.shape[1]
        shapes = [v.shape for v in parts]
        shapes[1] = base.shape
        return pl.pallas_call(
            functools.partial(flat_kernel, rank_width),
            grid=(1,),
            in_specs=[pl.BlockSpec(shape, lambda i: (0, 0)) for shape in shapes],
            out_specs=pl.BlockSpec((rank_width, width), lambda i: (0, 0)),
            out_shape=jax.ShapeDtypeStruct((rank_width, width), BF),
            cost_estimate=pl.CostEstimate(flops=10**6, bytes_accessed=10**5, transcendentals=0),
            name="flatten",
        )(*parts)

    def settle_outs(own, near, away, away_near):
        flat = [v.reshape(slot_count * rank_width, -1) for v in (own, near, away, away_near)]
        shapes = [((slot_count * rank_width, feats), F32)] * 3
        outs = local_call(across_kernel, "across", place, flat, shapes)
        return [v.reshape(slot_count, rank_width, feats) for v in outs]

    def settle_pair(flat):
        return jnp.concatenate([flat, lax.ppermute(flat, "dp", dp_pairs)], axis=0)

    def settle_line(pair):
        return [pair] + [
            lax.ppermute(pair, "dp", [(i, (i + 2 * s) % dp_size) for i in range(dp_size)])
            for s in range(1, pair_count)
        ]

    early_parts = settle_near(
        *local_call(
            functools.partial(pack_kernel, dp_size),
            "pack",
            place,
            [
                delta_shrink_up,
                delta_expand_down,
                delta_near,
                rank_out[middle:],
                branch_held,
                branch_last,
            ],
            packed(3),
        )
    )
    far_grad, far_rank = in_rows(
        after(branch_held, early_parts[2]), branch_last, lift_output, down_output, weight_vo
    )
    rank_grad_out = jnp.concatenate([near_rank, far_rank], axis=0)
    grad_attended = jnp.concatenate([near_grad, far_grad], axis=0)
    delta_output_down = product_rows(rank_grad_out, attended)
    main_arrived = to_chip(after(main_far, early_parts[2], branch_far))

    def attend_back(grad, heads, before=()):
        return by_head(
            attend_back_kernel,
            turn,
            [queries, keys_low, values_low, grad],
            [bias, level],
            [BF, BF, BF],
            [pltpu.VMEM((seq_len, HEAD_DIM), F32)] * 2,
            heads,
            "attend_back",
            before,
        )

    grads = attend_back(after(grad_attended, early_parts[2]), (0, 1))
    early_flat = settle_flat(
        after(early_parts[0], grads[0]),
        early_parts[1],
        to_chip(early_parts[2]),
        [*down_parts, *up_parts, delta_output_down],
    )
    early_pair = settle_pair(early_flat)
    grads = attend_back(after(grad_attended, early_flat), (1, 1), grads)
    early_trees = lax.all_gather(
        after(early_pair, grads[0]), "dp", axis=0, tiled=True, axis_index_groups=line_groups
    )
    grads = attend_back(after(grad_attended, early_pair), (2, head_count - 2), grads)
    grad_query_low, grad_key_low, grad_value_low = grads
    grad_rank_one, *late_parts, delta_query_up, delta_key_up, delta_value_up = local_call(
        functools.partial(late_kernel, dp_size),
        "late_deltas",
        place,
        [*grads, lift_query, lift_key, lift_value, full_one, rank_one],
        [((seq_len, 3 * rank_width), BF)]
        + packed(3)
        + [((rank_width, width_local), F32)] * 3,
    )
    late_parts[1] = after(late_parts[1], main_arrived)
    late_base, late_near, late_far = settle_near(*late_parts)
    late_chip = to_chip(late_far)

    def rows_back(first, count, *held):
        rank = after(grad_rank_one, *held) if held else grad_rank_one
        return back_rows(
            [grad_query_low, grad_key_low, grad_value_low, rank],
            weight_qk,
            weight_vo,
            down_qkv,
            row_count,
            first,
            count,
        )

    late_flat = settle_flat(
        late_base, late_near, late_chip, [delta_query_up, delta_key_up, delta_value_up]
    )
    late_other = lax.ppermute(late_flat, "dp", dp_pairs)
    early_own, shrink_down_out, expand_up_out, output_down_out = sum_slots(
        [after(early_trees, late_flat)],
        slot_count,
        rank_width,
        3 * quarter,
        [hidden_local, hidden_local, width_local],
    )
    late_pair = jnp.concatenate([late_flat, after(late_other, early_own)], axis=0)
    late_trees = settle_line(late_pair)
    (back_third,) = rows_back(3, 1, late_pair)
    back_core = to_core(back_third)
    (back_second,) = rows_back(2, 1, back_third)
    early_away = to_chip(early_own)
    back_far = (back_second.astype(F32) + back_core.astype(F32)).astype(BF)
    back_far = after(back_far, early_away)
    back_arrived = to_chip(back_far)
    (output,) = local_call(
        functools.partial(output_kernel, dp_size),
        "output",
        place,
        [near[0][0], main_one, after(main_arrived, back_far), residual, last_bias[None]],
        [((row_count, feats), BF)],
        row_count // 4,
    )
    (back_first,) = rows_back(1, 1, output, late_trees[1])
    (back_zero,) = rows_back(0, 1, back_first, *late_trees[1:])
    late_own, query_up_out, key_up_out, value_up_out = sum_slots(
        [after(late_trees[0], back_zero), *late_trees[1:]],
        slot_count,
        rank_width,
        3 * quarter,
        [width_local] * 3,
    )
    late_away = to_chip(after(late_own, back_far))
    early_outs = settle_outs(
        early_own, to_core(early_own), early_away, to_core(after(early_away, late_own))
    )
    shrink_up_out, expand_down_out, output_up_out = early_outs
    back_one = to_core(after(back_first, back_arrived, late_own))
    grad_norm_one = (
        back_zero.astype(F32) + back_one.astype(F32) + back_arrived.astype(F32)
    )
    input_delta = natural(
        (grad_residual + norm_back(grad_norm_one, gain_a, unit_one, scale_one)).astype(BF)
    )
    query_down_out, key_down_out, value_down_out = settle_outs(
        late_own, to_core(late_own), late_away, to_core(after(late_away, input_delta, early_outs[0]))
    )
    return (
        output,
        input_delta,
        query_down_out,
        query_up_out,
        key_down_out,
        key_up_out,
        value_down_out,
        value_up_out,
        output_down_out,
        output_up_out,
        expand_down_out,
        expand_up_out,
        shrink_down_out,
        shrink_up_out,
    )


def solution(mesh):
    rows = P(("dp", "tensor"), None)
    tree = P("dp", None)
    whole = P()
    slim = P(None, None, "tensor")
    inward = P("dp", "tensor")
    outward = P("tensor", "dp")
    return jax.shard_map(
        functools.partial(shards, mesh.shape["dp"]),
        mesh=mesh,
        in_specs=(
            rows,
            rows,
            tree,
            tree,
            P("dp"),
            whole,
            whole,
            whole,
            whole,
            inward,
            inward,
            inward,
            outward,
            inward,
            outward,
            P("tensor"),
            P("tensor"),
            whole,
            P("tensor"),
            whole,
            whole,
            slim,
            whole,
            slim,
            whole,
            slim,
            slim,
            whole,
            whole,
            slim,
            slim,
            whole,
        ),
        out_specs=(
            rows,
            rows,
            whole,
            slim,
            whole,
            slim,
            whole,
            slim,
            slim,
            whole,
            whole,
            slim,
            slim,
            whole,
        ),
        check_vma=False,
    )
```

```python
import functools

import jax
import jax.numpy as jnp
from jax import lax
from jax.experimental import pallas as pl
from jax.experimental.pallas import tpu as pltpu
from jax.sharding import PartitionSpec as P

HEAD_DIM = 128
SEGS = 13
BF = jnp.bfloat16
F32 = jnp.float32


def ancestry(parents):
    seg_range = jnp.arange(SEGS, dtype=jnp.int32)
    current = seg_range
    ancestors = current[:, None] == seg_range[None, :]
    for hop_index in range(SEGS - 1):
        current = jnp.sum(
            jnp.where(current[:, None] == seg_range[None, :], parents[None, :], 0), axis=1
        )
        ancestors = jnp.logical_or(ancestors, current[:, None] == seg_range[None, :])
    return ancestors


def product(left, right):
    return jnp.dot(left, right, preferred_element_type=F32)


def product_cols(left, right):
    return lax.dot_general(
        left, right, (((1,), (1,)), ((), ())), preferred_element_type=F32
    )


def product_rows(left, right):
    return lax.dot_general(
        left, right, (((0,), (0,)), ((), ())), preferred_element_type=F32
    )


def join_kernel(*refs):
    *blocks, down, out, rank = refs
    for k, block in enumerate(blocks):

        @pl.when(pl.program_id(0) == k)
        def _(block=block):
            out[...] = block[...]
            rank[...] = product_cols(block[...], down[...]).astype(BF)


def join_rows(blocks, down):
    tile, feats = blocks[0].shape
    rank = down.shape[0]
    return pl.pallas_call(
        join_kernel,
        grid=(len(blocks),),
        in_specs=[
            pl.BlockSpec(v.shape, lambda i: (0, 0), pipeline_mode=pl.Buffered(1))
            for v in (*blocks, down)
        ],
        out_specs=[
            pl.BlockSpec((tile, feats), lambda i: (i, 0)),
            pl.BlockSpec((tile, rank), lambda i: (i, 0)),
        ],
        out_shape=[
            jax.ShapeDtypeStruct((len(blocks) * tile, feats), BF),
            jax.ShapeDtypeStruct((len(blocks) * tile, rank), BF),
        ],
        cost_estimate=pl.CostEstimate(flops=10**6, bytes_accessed=10**5, transcendentals=0),
        name="join_rows",
    )(*blocks, down)


def feed_kernel(first, last, pieces, *refs):
    rows, cots, rank_in, rank_grad, lift, bias, down = refs[:7]
    weights, refs = refs[7 : 7 + pieces], refs[7 + pieces :]
    if not first:
        main_in, grad_in, rank_main_in, rank_back_in = refs[:4]
        refs = refs[4:]
    if last:
        lift_after, down_before = refs[:2]
        refs = refs[2:]
    mains, grads = refs[: len(refs) // 2 - 2], refs[len(refs) // 2 - 2 : -4]
    rank_main, rank_back, down_delta, up_delta = refs[-4:]
    chunk = lift.shape[1]
    parts, at = [], 0
    for weight in weights:
        parts.append((slice(at, at + weight.shape[0]), weight))
        at += weight.shape[0]

    pre_act = (
        sum(product(rows[:, here], weight[:, :chunk]) for here, weight in parts)
        + product(rank_in[...], lift[...])
        + bias[...]
    )
    grad_hidden = sum(
        product(cots[:, here], weight[:, chunk:]) for here, weight in parts
    ) + product(rank_grad[...], down[...])
    bell = 0.5 * (1.0 + lax.erf(pre_act * (0.5**0.5)))
    slope = bell + pre_act * jnp.exp(-0.5 * pre_act * pre_act) * (0.5 / jnp.pi) ** 0.5
    hidden = (pre_act * bell).astype(BF)
    grad_pre = (grad_hidden * slope).astype(BF)

    main_rank = product_cols(hidden, down[...])
    back_rank = product_cols(grad_pre, lift[...])
    if not first:
        main_rank = main_rank + rank_main_in[...]
        back_rank = back_rank + rank_back_in[...]
    rank_main[...] = main_rank
    rank_back[...] = back_rank
    for here, weight in parts:
        ahead = product_cols(hidden, weight[:, chunk:])
        back = product_cols(grad_pre, weight[:, :chunk])
        if not first:
            ahead = ahead + main_in[:, here]
            back = back + grad_in[:, here]
        if last:
            ahead = ahead + product(main_rank.astype(BF), lift_after[:, here])
            back = back + product(back_rank.astype(BF), down_before[:, here])
        for k, (main, grad) in enumerate(zip(mains, grads)):

            @pl.when((pl.program_id(0) == k) | (len(mains) == 1))
            def _(main=main, grad=grad, here=here, ahead=ahead, back=back):
                main[:, here] = ahead.astype(main.dtype)
                grad[:, here] = back.astype(grad.dtype)

    down_part = product_rows(rank_grad[...], hidden)
    up_part = product_rows(rank_in[...], grad_pre)

    @pl.when(pl.program_id(0) == 0)
    def _():
        down_delta[...] = down_part
        up_delta[...] = up_part

    @pl.when(pl.program_id(0) > 0)
    def _():
        down_delta[...] += down_part
        up_delta[...] += up_part


def feed_forward(rows, cots, rank_in, rank_grad, weight, lift, bias, down, at, before, final, span):
    tile = 256
    feats = rows.shape[1]
    chunk = bias.shape[0]
    rank = lift.shape[0]
    begin, count = span[0] // tile, (span[1] - span[0]) // tile
    first, last = before is None, final is not None

    def row_block(width):
        return pl.BlockSpec((tile, width), lambda i: (begin + i, 0))

    def out_block(width):
        return pl.BlockSpec((tile, width), lambda i: (i, 0))

    def fixed(shape, column=0):
        return pl.BlockSpec(shape, lambda i: (0, column), pipeline_mode=pl.Buffered(1))

    args = [rows, cots, rank_in, rank_grad, lift, bias[None], down]
    specs = [
        row_block(feats),
        row_block(feats),
        row_block(rank),
        row_block(rank),
        fixed((rank, chunk), at),
        fixed((1, chunk), 0),
        fixed((rank, chunk), at),
    ]
    for piece, column in weight:
        args.append(piece)
        specs.append(fixed((piece.shape[0], 2 * chunk), column))
    if not first:
        args += [before[0][0], before[1][0], before[2], before[3]]
        specs += [row_block(feats), row_block(feats), row_block(rank), row_block(rank)]
    if last:
        args += list(final)
        specs += [fixed((rank, feats)), fixed((rank, feats))]
    size = span[1] - span[0]
    flops = size * feats * chunk
    if last:
        wide_specs = [fixed((tile, feats))] * (2 * count)
        wide_shapes = [jax.ShapeDtypeStruct((tile, feats), BF)] * (2 * count)
    else:
        wide_specs = [out_block(feats)] * 2
        wide_shapes = [jax.ShapeDtypeStruct((size, feats), BF)] * 2
    results = pl.pallas_call(
        functools.partial(feed_kernel, first, last, len(weight)),
        grid=(count,),
        in_specs=specs,
        out_specs=wide_specs
        + [
            out_block(rank),
            out_block(rank),
            pl.BlockSpec((rank, chunk), lambda i: (0, 0)),
            pl.BlockSpec((rank, chunk), lambda i: (0, 0)),
        ],
        out_shape=wide_shapes
        + [
            jax.ShapeDtypeStruct((size, rank), F32),
            jax.ShapeDtypeStruct((size, rank), F32),
            jax.ShapeDtypeStruct((rank, chunk), F32),
            jax.ShapeDtypeStruct((rank, chunk), F32),
        ],
        cost_estimate=pl.CostEstimate(
            flops=flops, bytes_accessed=size * feats * 20, transcendentals=size * chunk * 2
        ),
        name="feed_forward",
    )(*args)
    wide = len(wide_specs) // 2
    return results[:wide], results[wide : 2 * wide], *results[2 * wide :]


def attend_kernel(scale, turn, *refs):
    count = (len(refs) - 3) // 3
    query, key, value = refs[:count], refs[count : 2 * count], refs[2 * count : 3 * count]
    bias, attended, level = refs[3 * count :]
    rows = query[0].shape[0]
    for i in range(count):
        here = slice(i * rows, (i + 1) * rows)
        scores = [
            product_cols(query[i][...], key[j][...]) * scale
            + bias[here, j * rows : (j + 1) * rows]
            for j in range(i + 1)
        ]
        top = functools.reduce(
            jnp.maximum, [jnp.max(v, axis=-1, keepdims=True) for v in scores]
        )
        raised = [jnp.exp(v - top) for v in scores]
        total = sum(jnp.sum(v, axis=-1, keepdims=True) for v in raised)
        share = 1.0 / total
        mixed = sum(
            product((v * share).astype(BF), value[j][...]) for j, v in enumerate(raised)
        )
        to = pl.multiple_of((i ^ turn[0]) * rows, rows)
        attended[pl.ds(to, rows), :] = mixed.astype(BF)
        level[here, :] = jnp.broadcast_to(top + jnp.log(total), (rows, level.shape[1]))


def attend_back_kernel(scale, turn, *refs):
    count = (len(refs) - 7) // 4
    query, key, value, grad = (refs[n * count : (n + 1) * count] for n in range(4))
    bias, level = refs[4 * count : 4 * count + 2]
    grad_query, grad_key, grad_value, key_sum, value_sum = refs[-5:]
    rows = query[0].shape[0]
    for i in range(count):
        here = slice(i * rows, (i + 1) * rows)
        row_level = level[here, :1]
        probs = [
            jnp.exp(
                product_cols(query[i][...], key[j][...]) * scale
                + bias[here, j * rows : (j + 1) * rows]
                - row_level
            )
            for j in range(i + 1)
        ]
        grad_probs = [product_cols(grad[i][...], value[j][...]) for j in range(i + 1)]
        mean = sum(
            jnp.sum(p * g, axis=-1, keepdims=True) for p, g in zip(probs, grad_probs)
        )
        query_sum = 0.0
        for j in range(i + 1):
            there = slice(j * rows, (j + 1) * rows)
            grad_score = (probs[j] * (grad_probs[j] - mean)).astype(BF)
            query_sum = query_sum + product(grad_score, key[j][...])
            key_part = product_rows(grad_score, query[i][...])
            value_part = product_rows(probs[j].astype(BF), grad[i][...])
            if i > j:
                key_part = key_part + key_sum[there, :]
                value_part = value_part + value_sum[there, :]
            key_sum[there, :] = key_part
            value_sum[there, :] = value_part
        to = pl.multiple_of((i ^ turn[0]) * rows, rows)
        grad_query[pl.ds(to, rows), :] = (query_sum * scale).astype(BF)
    for j in range(count):
        there = slice(j * rows, (j + 1) * rows)
        to = pl.multiple_of((j ^ turn[0]) * rows, rows)
        grad_key[pl.ds(to, rows), :] = (key_sum[there, :] * scale).astype(BF)
        grad_value[pl.ds(to, rows), :] = value_sum[there, :].astype(BF)


def by_head(kernel, turn, blocked, whole, outs, scratch, heads, name, before=()):
    first, count = heads
    seq_len, width = blocked[0].shape
    blocks = 4
    rows = seq_len // blocks
    specs, args = [], []
    for v in blocked:
        for k in range(blocks):
            specs.append(
                pl.BlockSpec((rows, HEAD_DIM), lambda h, turn, k=k: (k ^ turn[0], first + h))
            )
            args.append(v)
    for v in whole:
        if v.shape[1] == seq_len:
            specs.append(
                pl.BlockSpec(v.shape, lambda h, turn: (0, 0), pipeline_mode=pl.Buffered(1))
            )
        else:
            specs.append(pl.BlockSpec((seq_len, HEAD_DIM), lambda h, turn: (0, first + h)))
        args.append(v)
    aliases = {1 + len(args) + n: n for n in range(len(before))}
    specs += [pl.BlockSpec(memory_space=pl.ANY)] * len(before)
    args += before
    return pl.pallas_call(
        functools.partial(kernel, HEAD_DIM ** (-0.5)),
        grid_spec=pltpu.PrefetchScalarGridSpec(
            num_scalar_prefetch=1,
            grid=(count,),
            in_specs=specs,
            out_specs=[pl.BlockSpec((seq_len, HEAD_DIM), lambda h, turn: (0, first + h))] * len(outs),
            scratch_shapes=scratch,
        ),
        out_shape=[jax.ShapeDtypeStruct((seq_len, width), t) for t in outs],
        input_output_aliases=aliases,
        cost_estimate=pl.CostEstimate(flops=10**8, bytes_accessed=10**6, transcendentals=0),
        name=name,
    )(turn, *args)


def branch_kernel(zero, one, far, base, unit, scale, gain, wide, low):
    unit_rows = unit[...]
    scaled = (
        zero[...].astype(F32) + one[...].astype(F32) + far[...].astype(F32)
    ) * gain[...]
    total = base[...].astype(F32) + scale[...] * (
        scaled
        - jnp.mean(scaled, axis=-1, keepdims=True)
        - unit_rows * jnp.mean(scaled * unit_rows, axis=-1, keepdims=True)
    )
    wide[...] = total
    low[...] = total.astype(BF)


def branch_rows(zero, one, far, base, unit, scale, gain):
    rows, feats = unit.shape
    tile = rows // 4
    wide = pl.BlockSpec((tile, feats), lambda i: (i, 0))
    return pl.pallas_call(
        branch_kernel,
        grid=(rows // tile,),
        in_specs=[wide] * 5
        + [pl.BlockSpec((tile, 1), lambda i: (i, 0)), pl.BlockSpec((1, feats), lambda i: (0, 0))],
        out_specs=[wide, wide],
        out_shape=[
            jax.ShapeDtypeStruct((rows, feats), F32),
            jax.ShapeDtypeStruct((rows, feats), BF),
        ],
        cost_estimate=pl.CostEstimate(flops=10**7, bytes_accessed=10**6, transcendentals=0),
        name="branch_rows",
    )(zero, one, far, base, unit, scale, gain[None])


def back_kernel(query, key, value, rank, qk_own, qk_other, vo_own, vo_other, down, *outs):
    width = query.shape[1]
    half = qk_own.shape[0]
    for at, qk, vo in ((0, qk_own, vo_own), (half, qk_other, vo_other)):
        rows = (
            product_cols(query[...], qk[:, :width])
            + product_cols(key[...], qk[:, width:])
            + product_cols(value[...], vo[...])
            + product(rank[...], down[:, at : at + half])
        ).astype(BF)
        for k, out in enumerate(outs):

            @pl.when(pl.program_id(0) == k)
            def _(out=out, rows=rows, at=at):
                out[:, at : at + half] = rows


def out_kernel(rows, down, lift, own, other, *outs):
    half = own.shape[0]
    rank = product_cols(rows[...], down[...]).astype(BF)
    for at, weight in ((0, own), (half, other)):
        here = slice(at, at + half)
        mixed = product_cols(rows[...], weight[...]) + product(rank, lift[:, here])
        for k, out in enumerate(outs):

            @pl.when(pl.program_id(0) == k)
            def _(out=out, mixed=mixed, here=here):
                out[:, here] = mixed.astype(BF)


def out_rows(rows, down, lift, weight, tile, first, count):
    half, width = weight[0].shape[0], rows.shape[1]

    def fixed(shape, column=0):
        return pl.BlockSpec(shape, lambda i: (0, column), pipeline_mode=pl.Buffered(1))

    return pl.pallas_call(
        out_kernel,
        grid=(count,),
        in_specs=[pl.BlockSpec((tile, width), lambda i: (first - i, 0))]
        + [fixed(down.shape), fixed(lift.shape)]
        + [fixed((half, width), 1)] * 2,
        out_specs=[fixed((tile, lift.shape[1]))] * count,
        out_shape=[jax.ShapeDtypeStruct((tile, lift.shape[1]), BF)] * count,
        cost_estimate=pl.CostEstimate(flops=10**7, bytes_accessed=10**5, transcendentals=0),
        name="out_rows",
    )(rows, down, lift, *weight[:2])


def back_rows(grads, weight_qk, weight_vo, down, tile, first, count):
    half, width = weight_vo[0].shape[0], grads[0].shape[1]

    def fixed(shape):
        return pl.BlockSpec(shape, lambda i: (0, 0), pipeline_mode=pl.Buffered(1))

    return pl.pallas_call(
        back_kernel,
        grid=(count,),
        in_specs=[pl.BlockSpec((tile, v.shape[1]), lambda i: (first - i, 0)) for v in grads]
        + [fixed((half, 2 * width))] * 2
        + [fixed((half, width))] * 2
        + [fixed(down.shape)],
        out_specs=[fixed((tile, down.shape[1]))] * count,
        out_shape=[jax.ShapeDtypeStruct((tile, down.shape[1]), BF)] * count,
        cost_estimate=pl.CostEstimate(flops=10**8, bytes_accessed=10**6, transcendentals=0),
        name="back_rows",
    )(*grads, *weight_qk[:2], *weight_vo[:2], down)


def by_place(place, parts):
    core_odd, chip_odd = place[1] % 2 == 1, place[1] // 2 == 1
    low = [jnp.where(core_odd, parts[1], parts[0]), jnp.where(core_odd, parts[0], parts[1])]
    high = [jnp.where(core_odd, parts[3], parts[2]), jnp.where(core_odd, parts[2], parts[3])]
    return [jnp.where(chip_odd, b, a) for a, b in zip(low + high, high + low)]


def in_order(place, blocks, values):
    size = values.shape[1] // blocks
    parts = [values[:, k * size : (k + 1) * size] for k in range(blocks)]
    ordered = []
    for own, other in zip(parts[: blocks // 2], parts[blocks // 2 :]):
        ordered.append(jnp.where(place[0] == 1, other, own))
        ordered.append(jnp.where(place[0] == 1, own, other))
    return jnp.concatenate(ordered, axis=1)


def pack(place, blocks, wide, base, send, far):
    total = base.shape[0]
    for k, values in enumerate(wide):
        ordered = in_order(place, blocks, values)
        size = ordered.shape[1] // 4
        parts = by_place(place, [ordered[:, t * size : (t + 1) * size] for t in range(4)])
        at, rows = k * values.shape[0], values.shape[0]
        base[at : at + rows] = parts[0].astype(BF)
        send[at : at + rows] = parts[1].astype(BF)
        send[total + at : total + at + rows] = parts[3].astype(BF)
        far[at : at + rows] = parts[2].astype(BF)


def pack_kernel(blocks, place, *refs):
    *wide, rank, first, second, base, send, far = refs
    tile = first.shape[0]
    wide = [ref[...] for ref in wide]
    wide[-1] = (
        wide[-1] + product_rows(rank[:tile], first[...]) + product_rows(rank[tile:], second[...])
    )
    pack(place, blocks, wide, base, send, far)


def in_kernel(first, second, lift, down, own, other, grad, rank):
    half, tile = own.shape[0], first.shape[0]
    for k, rows in enumerate((first, second)):
        here = slice(k * tile, (k + 1) * tile)
        ranks = product_cols(rows[...], lift[...]).astype(BF)
        rank[here, :] = ranks
        grad[here, :] = (
            product(rows[:, :half], own[...])
            + product(rows[:, half:], other[...])
            + product(ranks, down[...])
        ).astype(BF)


def in_rows(first, second, lift, down, weight):
    half, width = weight[0].shape[0], down.shape[1]
    rows = 2 * first.shape[0]
    whole = [pl.BlockSpec(v.shape, lambda i: (0, 0)) for v in (first, second, lift, down)]
    return pl.pallas_call(
        in_kernel,
        grid=(1,),
        in_specs=whole + [pl.BlockSpec((half, width), lambda i: (0, 1))] * 2,
        out_specs=[
            pl.BlockSpec((rows, width), lambda i: (0, 0)),
            pl.BlockSpec((rows, lift.shape[0]), lambda i: (0, 0)),
        ],
        out_shape=[
            jax.ShapeDtypeStruct((rows, width), BF),
            jax.ShapeDtypeStruct((rows, lift.shape[0]), BF),
        ],
        cost_estimate=pl.CostEstimate(flops=10**7, bytes_accessed=10**5, transcendentals=0),
        name="in_rows",
    )(first, second, lift, down, *weight[:2])


def late_kernel(blocks, place, *refs):
    grads, lifts, rows, ranks = refs[:3], refs[3:6], refs[6], refs[7]
    rank_grad, base, send, far, *ups = refs[8:]
    width = lifts[0].shape[0]
    wide = []
    for k, (grad, lift, up) in enumerate(zip(grads, lifts, ups)):
        here = slice(k * width, (k + 1) * width)
        rank = product_cols(grad[...], lift[...]).astype(BF)
        rank_grad[:, here] = rank
        wide.append(product_rows(rank, rows[...]))
        up[...] = product_rows(ranks[:, here], grad[...])
    pack(place, blocks, wide, base, send, far)


def across_kernel(place, *refs):
    parts, outs = refs[:4], refs[4:]
    size = parts[0].shape[1] // len(outs)
    for k, out in enumerate(outs):
        here = slice(k * size, (k + 1) * size)
        for t, part in enumerate(by_place(place, [v[:, here].astype(F32) for v in parts])):
            out[:, t * size : (t + 1) * size] = part


def output_kernel(blocks, place, zero, one, far, base, bias, out):
    total = base[...] + bias[...] + zero[...].astype(F32)
    total = total + one[...].astype(F32) + far[...].astype(F32)
    out[...] = in_order(place, blocks, total).astype(BF)


def local_call(kernel, name, place, args, shapes, tile=None):
    specs = [pl.BlockSpec(memory_space=pltpu.SMEM)]
    options = {}
    if tile is None:
        specs += [pl.BlockSpec(memory_space=pltpu.VMEM) for _ in args]
        out_specs = [pl.BlockSpec(memory_space=pltpu.VMEM) for _ in shapes]
    else:
        rows = shapes[0][0][0]

        def spec(shape):
            if shape[0] == rows:
                return pl.BlockSpec((tile, shape[1]), lambda i: (i, 0))
            return pl.BlockSpec(shape, lambda i: (0, 0))

        options = {"grid": (rows // tile,)}
        specs += [spec(v.shape) for v in args]
        out_specs = [spec(shape) for shape, _ in shapes]
    return pl.pallas_call(
        kernel,
        in_specs=specs,
        out_specs=out_specs,
        out_shape=[jax.ShapeDtypeStruct(shape, kind) for shape, kind in shapes],
        cost_estimate=pl.CostEstimate(flops=10**6, bytes_accessed=10**5, transcendentals=0),
        name=name,
        **options,
    )(place, *args)


def flat_kernel(rank, *refs):
    base, near, far, *slim, marks, out = refs
    mine = (
        base[...].astype(F32) + near[...].astype(F32) + far[...].astype(F32)
    ).astype(BF)
    width = mine.shape[1]
    at = 0
    for k in range(mine.shape[0] // rank):
        out[:, at : at + width] = mine[k * rank : (k + 1) * rank]
        at += width
    for part in slim:
        out[:, at : at + part.shape[1]] = part[...].astype(BF)
        at += part.shape[1]
    out[:, at:] = marks[...]


def slots_kernel(slot_count, rank, *refs):
    tree_count = len(refs) - 4
    trees = jnp.concatenate([ref[...] for ref in refs[:tree_count]], axis=0)
    lanes = slot_count * rank
    width = trees.shape[1] - lanes
    source = lax.broadcasted_iota(jnp.int32, (lanes, lanes), 0)
    target = lax.broadcasted_iota(jnp.int32, (lanes, lanes), 1)
    spread = jnp.where(source == target // rank, 1.0, 0.0).astype(BF)
    marks = product(trees[:, width:], spread)
    row = lax.broadcasted_iota(jnp.int32, marks.shape, 0)
    lane = lax.broadcasted_iota(jnp.int32, marks.shape, 1)
    marks = jnp.where(row % rank == lane % rank, marks, 0.0).astype(BF)
    at = 0
    for out in refs[tree_count:]:
        size = out.shape[1]
        out[...] = product_rows(marks, trees[:, at : at + size]).astype(out.dtype)
        at += size


def sum_slots(trees, slot_count, rank, wide, slim):
    rows = slot_count * rank
    wide_sum, *slim_sums = pl.pallas_call(
        functools.partial(slots_kernel, slot_count, rank),
        out_shape=[jax.ShapeDtypeStruct((rows, wide), BF)]
        + [jax.ShapeDtypeStruct((rows, n), F32) for n in slim],
        cost_estimate=pl.CostEstimate(flops=10**6, bytes_accessed=10**5, transcendentals=0),
        name="sum_slots",
    )(*trees)
    return [v.reshape(slot_count, rank, -1) for v in (wide_sum, *slim_sums)]


def shards(
    dp_size,
    inputs,
    cotangent,
    segment_ids,
    parent_links,
    adapter_choice,
    gain_one,
    shift_one,
    gain_two,
    shift_two,
    query_weight,
    key_weight,
    value_weight,
    output_weight,
    expand_weight,
    shrink_weight,
    query_bias,
    value_bias,
    output_bias,
    expand_bias,
    shrink_bias,
    query_down,
    query_up,
    key_down,
    key_up,
    value_down,
    value_up,
    output_down,
    output_up,
    expand_down,
    expand_up,
    shrink_down,
    shrink_up,
):
    slot_count = query_down.shape[0]
    rank_width = query_down.shape[1]
    feats = inputs.shape[1]
    row_count = inputs.shape[0]
    width_local = query_weight.shape[1]
    hidden_local = expand_weight.shape[1]
    pair_count = dp_size // 2
    block = feats // dp_size
    half = feats // 2

    tensor_index = lax.axis_index("tensor")
    core_odd = (tensor_index % 2) == 1
    chip_odd = (tensor_index // 2) == 1
    dp_odd = (lax.axis_index("dp") % 2) == 1

    core_pairs = [(0, 1), (1, 0), (2, 3), (3, 2)]
    chip_pairs = [(0, 2), (2, 0), (1, 3), (3, 1)]
    dp_pairs = [(i, i ^ 1) for i in range(dp_size)]
    line_groups = [list(range(0, dp_size, 2)), list(range(1, dp_size, 2))]

    def to_core(v):
        return lax.ppermute(v, "tensor", core_pairs)

    def to_chip(v):
        return lax.ppermute(v, "tensor", chip_pairs)

    def own_first(v):
        parts = [v[..., b * block : (b + 1) * block] for b in range(dp_size)]
        pairs = [(parts[2 * p], parts[2 * p + 1]) for p in range(pair_count)]
        return jnp.concatenate(
            [jnp.where(dp_odd, odd, even) for even, odd in pairs]
            + [jnp.where(dp_odd, even, odd) for even, odd in pairs],
            axis=-1,
        )

    def natural(v):
        parts = [v[..., b * block : (b + 1) * block] for b in range(dp_size)]
        pairs = [(parts[p], parts[pair_count + p]) for p in range(pair_count)]
        return jnp.concatenate(
            [
                jnp.where(dp_odd, a, b)
                for own, other in pairs
                for a, b in ((other, own), (own, other))
            ],
            axis=-1,
        )

    def after(value, *others):
        return lax.optimization_barrier((value,) + others)[0]

    def gather_rows(rows, *held):
        near = to_core(rows)
        far = to_chip(rows)
        if held:
            far = after(far, *held)
        far_near = to_core(far)
        return jnp.concatenate([rows, near, far, far_near], axis=0)

    def line_gather(shard, held):
        if held:
            shard = after(shard, *held)
        return lax.all_gather(shard, "dp", axis=0, tiled=True, axis_index_groups=line_groups)

    def fetch(shard, *held):
        own = line_gather(shard, held)
        return own, lax.ppermute(own, "dp", dp_pairs), 0

    def fetch_pieces(shard, parts, *held):
        own = line_gather(shard, held)
        size = own.shape[0] // parts
        swapped = [
            lax.ppermute(own[k * size : (k + 1) * size], "dp", dp_pairs) for k in range(parts)
        ]
        return [(v, 0) for v in (own, *swapped)]

    def swap_after(pieces, *held):
        own = pieces[0][0]
        return [(own, 0), (lax.ppermute(after(own, *held), "dp", dp_pairs), 0)]

    def fetch_paired(pair, *held):
        both = line_gather(pair, held)
        return [(both, 0), (both, 1)]

    def into(left, weight, first, last):
        own, other, skip = weight
        return product(left[:, :half], own[:, first:last]) + product(
            left[:, half:], other[:, skip + first : skip + last]
        )

    def out_of(left, weight, first, last, base=None):
        own, other, skip = weight
        near = product_cols(left, own[:, first:last])
        far = product_cols(left, other[:, skip + first : skip + last])
        if base is not None:
            near, far = base[0] + near, base[1] + far
        return near, far

    def beside(pair):
        return jnp.concatenate(pair, axis=1)

    chunk_count = 4
    chunk = hidden_local // chunk_count
    output_turned = output_weight.T
    shrink_turned = shrink_weight.T
    def feed_shard(h):
        return jnp.concatenate(
            [
                expand_weight[:, h * chunk : (h + 1) * chunk],
                shrink_turned[:, h * chunk : (h + 1) * chunk],
            ],
            axis=1,
        )

    last_shard = feed_shard(chunk_count - 1)
    last_pair = jnp.concatenate([last_shard, lax.ppermute(last_shard, "dp", dp_pairs)], axis=1)
    weight_qk = fetch(jnp.concatenate([query_weight, key_weight], axis=1))
    weight_vo = fetch(jnp.concatenate([value_weight, output_turned], axis=1))
    select = (jnp.arange(slot_count, dtype=jnp.int32) == adapter_choice[0]).astype(BF)

    def adapter_of(adapter_table):
        return jnp.einsum(
            "a,ard->rd", select, adapter_table, preferred_element_type=F32
        ).astype(BF)

    down_qkv = own_first(
        jnp.concatenate(
            [adapter_of(query_down), adapter_of(key_down), adapter_of(value_down)], axis=0
        )
    )
    lift_query = adapter_of(query_up)
    lift_key = adapter_of(key_up)
    lift_value = adapter_of(value_up)
    down_output = adapter_of(output_down)
    lift_output = own_first(adapter_of(output_up))
    down_expand = own_first(adapter_of(expand_down))
    lift_expand = adapter_of(expand_up)
    down_shrink = adapter_of(shrink_down)
    lift_shrink = own_first(adapter_of(shrink_up))

    gain_a, shift_a = own_first(gain_one), own_first(shift_one)
    gain_b, shift_b = own_first(gain_two), own_first(shift_two)
    out_bias = own_first(output_bias)
    last_bias = own_first(shrink_bias)

    def normalize(values):
        row_mean = jnp.mean(values, axis=-1, keepdims=True)
        centred = values - row_mean
        row_var = jnp.mean(centred * centred, axis=-1, keepdims=True)
        scale = lax.rsqrt(row_var + 1e-05)
        return centred * scale, scale

    def norm_back(grad, gain, unit, scale):
        scaled = grad * gain
        return (
            scaled
            - jnp.mean(scaled, axis=-1, keepdims=True)
            - unit * jnp.mean(scaled * unit, axis=-1, keepdims=True)
        ) * scale

    inputs_wide = own_first(inputs).astype(F32)
    cot = own_first(cotangent)
    unit_one, scale_one = normalize(inputs_wide)
    rows_one = (unit_one * gain_a + shift_a).astype(BF)
    full_one = gather_rows(rows_one, gain_b, shift_b, out_bias, last_bias)
    full_cot = gather_rows(cot)
    seq_len = full_one.shape[0]
    head_count = width_local // HEAD_DIM

    rank_one = product_cols(full_one, down_qkv).astype(BF)
    weight_ffn, held = [], [weight_qk[0], weight_vo[0]]
    for h in range(chunk_count - 1):
        more = (last_pair, rank_one) if h == 0 else ()
        weight_ffn.append(fetch_pieces(feed_shard(h), 2 if h == 1 else 1, held[h], *more))
        held.append(weight_ffn[-1][0][0])
    weight_ffn.append(fetch_paired(last_pair, held[-2]))

    rank_query = rank_one[:, :rank_width]
    rank_key = rank_one[:, rank_width : 2 * rank_width]
    rank_value = rank_one[:, 2 * rank_width :]
    query_key = into(after(full_one, weight_vo[0]), weight_qk, 0, 2 * width_local)
    queries = (query_key[:, :width_local] + product(rank_query, lift_query) + query_bias).astype(BF)
    keys_low = (query_key[:, width_local:] + product(rank_key, lift_key)).astype(BF)
    values_low = (
        into(after(full_one, held[2]), weight_vo, 0, width_local)
        + product(rank_value, lift_value)
        + value_bias
    ).astype(BF)
    seg_range = jnp.arange(SEGS, dtype=jnp.int32)
    seg_hot = (segment_ids[0][:, None] == seg_range[None, :]).astype(BF)
    path_hot = product(seg_hot, ancestry(parent_links[0]).astype(BF)).astype(BF)
    positions = jnp.arange(seq_len, dtype=jnp.int32)
    allowed = jnp.logical_and(
        product_cols(path_hot, seg_hot) > 0.5, positions[:, None] >= positions[None, :]
    )
    bias = jnp.where(allowed, 0.0, -1e30)
    turn = tensor_index.astype(jnp.int32).reshape(1)
    attended, level = by_head(
        attend_kernel,
        turn,
        [queries, keys_low, values_low],
        [bias],
        [BF, F32],
        [],
        (0, head_count),
        "attend",
    )
    rank_out = product_cols(attended, down_output).astype(BF)

    def far_part(two, three):
        return (two.astype(F32) + to_core(three).astype(F32)).astype(BF)

    def near_part(zero, one):
        return zero.astype(F32) + to_core(one).astype(F32)

    def out_blocks(rows, first):
        return out_rows(rows, down_output, lift_output, weight_vo, row_count, first, 2)

    out_third, out_second = out_blocks(attended, 3)
    out_far = far_part(out_second, out_third)
    out_first, out_zero = out_blocks(after(attended, out_far, weight_ffn[0][1][0]), 1)
    main_rows = near_part(out_zero, out_first) + to_chip(out_far).astype(F32)
    main_rows = after(main_rows, held[3])
    rank_grad = product_cols(full_cot, lift_shrink).astype(BF)
    residual = inputs_wide + main_rows + out_bias
    unit_two, scale_two = normalize(residual)
    rows_two = (unit_two * gain_b + shift_b).astype(BF)
    near_two = to_core(rows_two)
    far_two = after(to_chip(rows_two), weight_ffn[1][1][0], weight_ffn[1][2][0], rank_grad)
    weight_ffn[2] = swap_after(weight_ffn[2], far_two)
    last_two = to_core(far_two)
    full_two, rank_two = join_rows([rows_two, near_two, far_two, last_two], down_expand)

    state = None
    down_parts, up_parts = [], []

    def feed(h, rows, span):
        last = h == chunk_count - 1
        results = feed_forward(
            rows,
            full_cot,
            rank_two,
            rank_grad,
            weight_ffn[h],
            lift_expand,
            expand_bias[h * chunk : (h + 1) * chunk],
            down_shrink,
            h,
            state,
            (lift_shrink, down_expand) if last else None,
            span,
        )
        return results[:4], results[4], results[5]

    for h in range(chunk_count - 1):
        state, down_part, up_part = feed(h, full_two, (0, seq_len))
        down_parts.append(down_part)
        up_parts.append(up_part)

    last = chunk_count - 1
    third, *third_deltas = feed(last, full_two, (3 * row_count, seq_len))
    second, *second_deltas = feed(
        last, after(full_two, third[1][0]), (2 * row_count, 3 * row_count)
    )
    grad_far = far_part(second[1][0], third[1][0])
    near, *near_deltas = feed(last, after(full_two, grad_far), (0, 2 * row_count))
    down_parts.append(third_deltas[0] + second_deltas[0] + near_deltas[0])
    up_parts.append(third_deltas[1] + second_deltas[1] + near_deltas[1])
    grad_rank_two = jnp.concatenate([near[3], second[3], third[3]], axis=0).astype(BF)
    rank_shrink = jnp.concatenate([near[2], second[2], third[2]], axis=0).astype(BF)
    far_arrived = to_chip(grad_far)
    grad_residual, grad_branch = branch_rows(
        near[1][0],
        to_core(after(near[1][1], far_arrived)),
        far_arrived,
        cot,
        unit_two,
        scale_two,
        gain_b,
    )

    branch_near = to_core(grad_branch)
    branch_far = to_chip(grad_branch)
    delta_shrink_up = product_rows(after(rank_shrink, grad_branch), full_cot)
    delta_expand_down = product_rows(after(grad_rank_two, grad_branch), full_two)
    main_far = far_part(after(second[0][0], grad_branch), after(third[0][0], grad_branch))
    main_one = to_core(near[0][1])
    near_grad, near_rank = in_rows(
        grad_branch, branch_near, lift_output, down_output, weight_vo
    )
    middle = 2 * row_count
    delta_near = product_rows(rank_out[:row_count], grad_branch) + product_rows(
        rank_out[row_count:middle], branch_near
    )
    branch_held = after(
        branch_far, delta_shrink_up, delta_expand_down, main_far, near_grad, delta_near
    )
    branch_last = to_core(branch_held)

    hot_lanes = (
        jnp.arange(128, dtype=jnp.int32)[None, :] == adapter_choice[0]
    ).astype(BF) * jnp.ones((rank_width, 1), BF)

    quarter = feats // 4

    place = jnp.stack([dp_odd.astype(jnp.int32), tensor_index.astype(jnp.int32)])

    def packed(count):
        rows = count * rank_width
        return [((rows, quarter), BF), ((2 * rows, quarter), BF), ((rows, quarter), BF)]

    def settle_near(base, send, far):
        near = to_core(send)
        far = (far.astype(F32) + near[base.shape[0] :].astype(F32)).astype(BF)
        return base, near, far

    def settle_flat(base, near, far, slim):
        parts = [base, near, far, *slim, hot_lanes]
        rows = base.shape[0] // rank_width
        width = rows * quarter + sum(v.shape[1] for v in slim) + hot_lanes.shape[1]
        shapes = [v.shape for v in parts]
        shapes[1] = base.shape
        return pl.pallas_call(
            functools.partial(flat_kernel, rank_width),
            grid=(1,),
            in_specs=[pl.BlockSpec(shape, lambda i: (0, 0)) for shape in shapes],
            out_specs=pl.BlockSpec((rank_width, width), lambda i: (0, 0)),
            out_shape=jax.ShapeDtypeStruct((rank_width, width), BF),
            cost_estimate=pl.CostEstimate(flops=10**6, bytes_accessed=10**5, transcendentals=0),
            name="flatten",
        )(*parts)

    def settle_outs(own, near, away, away_near):
        flat = [v.reshape(slot_count * rank_width, -1) for v in (own, near, away, away_near)]
        shapes = [((slot_count * rank_width, feats), F32)] * 3
        outs = local_call(across_kernel, "across", place, flat, shapes)
        return [v.reshape(slot_count, rank_width, feats) for v in outs]

    def settle_pair(flat):
        return jnp.concatenate([flat, lax.ppermute(flat, "dp", dp_pairs)], axis=0)

    def settle_line(pair):
        return [pair] + [
            lax.ppermute(pair, "dp", [(i, (i + 2 * s) % dp_size) for i in range(dp_size)])
            for s in range(1, pair_count)
        ]

    early_parts = settle_near(
        *local_call(
            functools.partial(pack_kernel, dp_size),
            "pack",
            place,
            [
                delta_shrink_up,
                delta_expand_down,
                delta_near,
                rank_out[middle:],
                branch_held,
                branch_last,
            ],
            packed(3),
        )
    )
    far_grad, far_rank = in_rows(
        after(branch_held, early_parts[2]), branch_last, lift_output, down_output, weight_vo
    )
    rank_grad_out = jnp.concatenate([near_rank, far_rank], axis=0)
    grad_attended = jnp.concatenate([near_grad, far_grad], axis=0)
    delta_output_down = product_rows(rank_grad_out, attended)
    main_arrived = to_chip(after(main_far, early_parts[2], branch_far))

    def attend_back(grad, heads, before=()):
        return by_head(
            attend_back_kernel,
            turn,
            [queries, keys_low, values_low, grad],
            [bias, level],
            [BF, BF, BF],
            [pltpu.VMEM((seq_len, HEAD_DIM), F32)] * 2,
            heads,
            "attend_back",
            before,
        )

    grads = attend_back(after(grad_attended, early_parts[2]), (0, 1))
    early_flat = settle_flat(
        after(early_parts[0], grads[0]),
        early_parts[1],
        to_chip(early_parts[2]),
        [*down_parts, *up_parts, delta_output_down],
    )
    early_pair = settle_pair(early_flat)
    grads = attend_back(after(grad_attended, early_flat), (1, 1), grads)
    early_trees = lax.all_gather(
        after(early_pair, grads[0]), "dp", axis=0, tiled=True, axis_index_groups=line_groups
    )
    grads = attend_back(after(grad_attended, early_pair), (2, head_count - 2), grads)
    grad_query_low, grad_key_low, grad_value_low = grads
    grad_rank_one, *late_parts, delta_query_up, delta_key_up, delta_value_up = local_call(
        functools.partial(late_kernel, dp_size),
        "late_deltas",
        place,
        [*grads, lift_query, lift_key, lift_value, full_one, rank_one],
        [((seq_len, 3 * rank_width), BF)]
        + packed(3)
        + [((rank_width, width_local), F32)] * 3,
    )
    def rows_back(first, count, *held):
        rank = after(grad_rank_one, *held) if held else grad_rank_one
        return back_rows(
            [grad_query_low, grad_key_low, grad_value_low, rank],
            weight_qk,
            weight_vo,
            down_qkv,
            row_count,
            first,
            count,
        )

    (back_third,) = rows_back(3, 1)
    late_parts[1] = after(late_parts[1], main_arrived, back_third)
    late_base, late_near, late_far = settle_near(*late_parts)
    late_chip = to_chip(late_far)

    late_flat = settle_flat(
        late_base, late_near, late_chip, [delta_query_up, delta_key_up, delta_value_up]
    )
    late_other = lax.ppermute(late_flat, "dp", dp_pairs)
    early_own, shrink_down_out, expand_up_out, output_down_out = sum_slots(
        [after(early_trees, late_flat)],
        slot_count,
        rank_width,
        3 * quarter,
        [hidden_local, hidden_local, width_local],
    )
    late_pair = jnp.concatenate([late_flat, after(late_other, early_own)], axis=0)
    late_trees = settle_line(late_pair)
    back_core = to_core(back_third)
    (back_second,) = rows_back(2, 1, late_pair)
    early_away = to_chip(early_own)
    back_far = (back_second.astype(F32) + back_core.astype(F32)).astype(BF)
    back_far = after(back_far, early_away)
    back_arrived = to_chip(back_far)
    (output,) = local_call(
        functools.partial(output_kernel, dp_size),
        "output",
        place,
        [near[0][0], main_one, after(main_arrived, back_far), residual, last_bias[None]],
        [((row_count, feats), BF)],
        row_count // 4,
    )
    (back_first,) = rows_back(1, 1, output, late_trees[1])
    (back_zero,) = rows_back(0, 1, back_first, *late_trees[1:])
    late_own, query_up_out, key_up_out, value_up_out = sum_slots(
        [after(late_trees[0], back_zero), *late_trees[1:]],
        slot_count,
        rank_width,
        3 * quarter,
        [width_local] * 3,
    )
    late_away = to_chip(after(late_own, back_far))
    early_outs = settle_outs(
        early_own, to_core(early_own), early_away, to_core(after(early_away, late_own))
    )
    shrink_up_out, expand_down_out, output_up_out = early_outs
    back_one = to_core(after(back_first, back_arrived, late_own))
    grad_norm_one = (
        back_zero.astype(F32) + back_one.astype(F32) + back_arrived.astype(F32)
    )
    input_delta = natural(
        (grad_residual + norm_back(grad_norm_one, gain_a, unit_one, scale_one)).astype(BF)
    )
    query_down_out, key_down_out, value_down_out = settle_outs(
        late_own, to_core(late_own), late_away, to_core(after(late_away, input_delta, early_outs[0]))
    )
    return (
        output,
        input_delta,
        query_down_out,
        query_up_out,
        key_down_out,
        key_up_out,
        value_down_out,
        value_up_out,
        output_down_out,
        output_up_out,
        expand_down_out,
        expand_up_out,
        shrink_down_out,
        shrink_up_out,
    )


def solution(mesh):
    rows = P(("dp", "tensor"), None)
    tree = P("dp", None)
    whole = P()
    slim = P(None, None, "tensor")
    inward = P("dp", "tensor")
    outward = P("tensor", "dp")
    return jax.shard_map(
        functools.partial(shards, mesh.shape["dp"]),
        mesh=mesh,
        in_specs=(
            rows,
            rows,
            tree,
            tree,
            P("dp"),
            whole,
            whole,
            whole,
            whole,
            inward,
            inward,
            inward,
            outward,
            inward,
            outward,
            P("tensor"),
            P("tensor"),
            whole,
            P("tensor"),
            whole,
            whole,
            slim,
            whole,
            slim,
            whole,
            slim,
            slim,
            whole,
            whole,
            slim,
            slim,
            whole,
        ),
        out_specs=(
            rows,
            rows,
            whole,
            slim,
            whole,
            slim,
            whole,
            slim,
            slim,
            whole,
            whole,
            slim,
            slim,
            whole,
        ),
        check_vma=False,
    )
```
